32 devices in a mesh: section: 2 (over x), dp: 8 (over z, y), tensor: 2 (over core).
Axes of the slice: x: 2, y: 2, z: 4, core: 2. Of those that a mesh axis runs over, the one named last changes fastest.
Arguments:
- images_in: bfloat16 [256, 32, 1152], P('tensor', 'dp'), may hold values from -6 to 6
- timesteps: int32 [32], P('dp'), may hold values from 0 to 999
- labels: int32 [32], P('dp'), may hold values from 0 to 1000
- counts: int32 [8], P('dp'), may hold values from 1 to 4, 21 in all
- label_table: bfloat16 [1001, 1152], replicated, may hold values from -6 to 6
- ada_weight: bfloat16 [2, 1152, 6912], P('section', None, 'tensor'), may hold values from -0.1875 to 0.1875
- ada_bias: bfloat16 [2, 6912], P('section', 'tensor'), may hold values from -3 to 3
- qkv_weight: bfloat16 [2, 1152, 3, 1152], P('section', None, None, 'tensor'), may hold values from -0.1875 to 0.1875
- qkv_bias: bfloat16 [2, 2, 1152], P('section', None, 'tensor'), may hold values from -3 to 3
- out_weight: bfloat16 [2, 1152, 1152], P('section', 'tensor'), may hold values from -1.5 to 1.5
- out_bias: bfloat16 [2, 1152], P('section'), may hold values from -6 to 6
- up_weight: bfloat16 [2, 1152, 4608], P('section', None, 'tensor'), may hold values from -0.1875 to 0.1875
- up_bias: bfloat16 [2, 4608], P('section', 'tensor'), may hold values from -3 to 3
- down_weight: bfloat16 [2, 4608, 1152], P('section', 'tensor'), may hold values from -0.09375 to 0.09375
- down_bias: bfloat16 [2, 1152], P('section'), may hold values from -6 to 6
- out_cotangent: bfloat16 [256, 32, 1152], P('tensor', 'dp'), may hold values from -6 to 6
Outputs:
- layer_out: bfloat16 [2, 256, 32, 1152], P('section', 'tensor', 'dp')
- in_grad: bfloat16 [2, 256, 32, 1152], P('section', 'tensor', 'dp')
- cond_grad: float32 [32, 1152], P('dp')
- table_grad: float32 [1001, 1152], replicated
- grad_ada_weight: float32 [2, 1152, 6912], P('section', None, 'tensor')
- grad_ada_bias: float32 [2, 6912], P('section', 'tensor')
- grad_qkv_weight: float32 [2, 1152, 3, 1152], P('section', None, None, 'tensor')
- grad_qkv_bias: float32 [2, 2, 1152], P('section', None, 'tensor')
- grad_out_weight: float32 [2, 1152, 1152], P('section', 'tensor')
- grad_out_bias: float32 [2, 1152], P('section')
- grad_up_weight: float32 [2, 1152, 4608], P('section', None, 'tensor')
- grad_up_bias: float32 [2, 4608], P('section', 'tensor')
- grad_down_weight: float32 [2, 4608, 1152], P('section', 'tensor')
- grad_down_bias: float32 [2, 1152], P('section')
The draws below stay inside these ranges and needn't reach their ends.
Inputs may be any that keep to these rules, and one draw needn't show every extreme that they name: `counts`: the groups hold 21 images in all, and some group holds 4; a group's images fill its first slots.
All inputs are finite; a program needn't handle non-finite values.
Results may differ from the reference program's by a relative error of at most 0.035.
Values may be sent and summed in bfloat16 or wider, within the bound.
No kernel may reach another device: no remote copies, remote signals or barrier semaphores. Data moves between devices by JAX's collectives and lax.ppermute only.
A program may use at most 320 MiB of HBM per device.

```python
import math
import jax
import jax.numpy as jnp
import numpy as np
from jax import lax

D = 1152
HEADS = 16
FF = 4608
CLASSES = 1001
SEQ = 256
SLOTS = 4
IMG_SLOTS = 32
IMAGES = 21
N_DP = 8


def set_ends(array, rng, low, top_value):
    extent = array.shape
    spot = [jax.random.randint(jax.random.fold_in(rng, axis), (), 0, extent[axis]) for axis in range(len(extent))]
    array = array.at[tuple(spot)].set(low)
    longest = extent.index(max(extent))
    spot[longest] = (spot[longest] + 1) % extent[longest]
    return array.at[tuple(spot)].set(top_value)


def shard_levels(rng, extent, pieces, low, largest):
    loudness, own = 1.0, jax.random.fold_in(rng, 6)
    for axis_at, shards_of in pieces:
        heights = jnp.exp(jax.random.uniform(jax.random.fold_in(own, axis_at), (shards_of,), jnp.float32, low / len(pieces), largest / len(pieces)))
        loudness = loudness * jnp.repeat(heights, extent[axis_at] // shards_of).reshape([-1 if axis == axis_at else 1 for axis in range(len(extent))])
    return loudness


def length_profile(count, total, limit, slope):
    loads = [(1 << 20) // math.isqrt(standing ** slope) + 1 for standing in range(2, count + 1)]
    spare, given = total - limit - (count - 1), [1] * (count - 1)
    while spare > 0:
        free = [i for i in range(count - 1) if given[i] < limit]
        pool, left = sum([loads[i] for i in free]), spare
        for i in free:
            addition = min(limit - given[i], max(1, left * loads[i] // pool), spare)
            given[i] = given[i] + addition
            spare = spare - addition
    return np.array([limit] + given)


def ragged(key, count, total, most, slope):
    if count == 2:
        one = jax.random.randint(key, (), max(1, total - most), min(most, total - 1) + 1)
        return jnp.stack([one, total - one])
    lengths = jnp.asarray(length_profile(count, total, most, slope), jnp.int32)
    pairs = (count - 1) // 2
    giver, taker = lengths[1:1 + 2 * pairs:2], lengths[2:2 + 2 * pairs:2]
    room = jnp.minimum(giver - 1, most - taker)
    moved = jax.random.randint(jax.random.fold_in(key, 1), (pairs,), 0, 1 << 20) % (room + 1)
    lengths = lengths.at[1:1 + 2 * pairs:2].set(giver - moved).at[2:2 + 2 * pairs:2].set(taker + moved)
    return lengths[jax.random.permutation(jax.random.fold_in(key, 2), count)]


def centred(key, shape, scale, most, cuts=(), kind=jnp.bfloat16):
    gain = shard_levels(key, shape, cuts, -0.22, 0.18) if cuts else 1.0
    entries = jax.random.normal(key, shape, jnp.float32) * scale * gain
    return jnp.minimum(jnp.maximum(entries, -most), most).astype(kind)


def setup_inputs(seed: int = 0) -> dict:
    streams_of = jax.random.split(jax.random.key(seed), 17)
    images_in = centred(streams_of[0], (SEQ, IMG_SLOTS, D), 1.0, 6.0, ((0, 2), (1, 8)))
    timesteps = set_ends(jax.random.randint(streams_of[1], (IMG_SLOTS,), 0, 1000), jax.random.fold_in(streams_of[1], 1), 0, 999).astype(jnp.int32)
    labels = set_ends(jax.random.randint(streams_of[2], (IMG_SLOTS,), 0, CLASSES), jax.random.fold_in(streams_of[2], 1), 0, CLASSES - 1).astype(jnp.int32)
    counts = ragged(streams_of[3], N_DP, IMAGES, SLOTS, 2).astype(jnp.int32)
    label_table = centred(streams_of[4], (CLASSES, D), 1.0, 6.0)
    ada_weight = centred(streams_of[5], (2, D, 6 * D), D ** -0.5, 0.1875, ((0, 2), (2, 2)))
    ada_bias = centred(streams_of[6], (2, 6 * D), 0.5, 3.0, ((0, 2), (1, 2)))
    qkv_weight = centred(streams_of[7], (2, D, 3, D), D ** -0.5, 0.1875, ((0, 2), (3, 2)))
    qkv_bias = centred(streams_of[8], (2, 2, D), 0.5, 3.0, ((0, 2), (2, 2)))
    out_weight = centred(streams_of[9], (2, D, D), (D // 64) ** -0.5, 1.5, ((0, 2), (1, 2)))
    out_bias = centred(streams_of[10], (2, D), 1.5, 6.0, ((0, 2),))
    up_weight = centred(streams_of[11], (2, D, FF), D ** -0.5, 0.1875, ((0, 2), (2, 2)))
    up_bias = centred(streams_of[12], (2, FF), 0.5, 3.0, ((0, 2), (1, 2)))
    down_weight = centred(streams_of[13], (2, FF, D), FF ** -0.5, 0.09375, ((0, 2), (1, 2)))
    down_bias = centred(streams_of[14], (2, D), 1.5, 6.0, ((0, 2),))
    out_cotangent = centred(streams_of[15], (SEQ, IMG_SLOTS, D), 1.0, 6.0, ((0, 2), (1, 8)))
    return dict(images_in=images_in, timesteps=timesteps, labels=labels, counts=counts, label_table=label_table, ada_weight=ada_weight, ada_bias=ada_bias, qkv_weight=qkv_weight, qkv_bias=qkv_bias, out_weight=out_weight, out_bias=out_bias, up_weight=up_weight, up_bias=up_bias, down_weight=down_weight, down_bias=down_bias, out_cotangent=out_cotangent)


@jax.custom_vjp
def low(v):
    return lax.optimization_barrier(v.astype(jnp.bfloat16)).astype(jnp.float32)

@jax.custom_vjp
def low_back(v):
    return v

def low_keep(v):
    return (low(v), None)

def low_pass(kept, grad):
    return (grad,)

def back_keep(v):
    return (v, None)

def back_low(kept, grad):
    return (low(grad),)
low.defvjp(low_keep, low_pass)
low_back.defvjp(back_keep, back_low)
eps_norm = 1e-06
highest = lax.Precision.HIGHEST

def time_embed(timesteps, width_all):
    half_width = width_all // 2
    frequencies = jnp.exp(-math.log(10000.0) * jnp.arange(half_width, dtype=jnp.float32) / half_width)
    angles = timesteps.astype(jnp.float32)[:, None] * frequencies[None, :]
    return jnp.concatenate([jnp.cos(angles), jnp.sin(angles)], axis=1)

def modulate(row_block, shift_rows, scale_rows):
    centered = row_block - lax.optimization_barrier(jnp.mean(row_block, axis=-1, keepdims=True))
    variance = lax.optimization_barrier(jnp.mean(centered * centered, axis=-1, keepdims=True))
    return centered * lax.rsqrt(variance + eps_norm) * (1.0 + scale_rows[None]) + shift_rows[None]

def layer_apply(rows_in, condition, valid_rows, params):
    ada_w, ada_b, qkv_w, qkv_b, out_w, out_b, up_w, up_b, down_w, down_b = params
    seq_len, batch_len = (rows_in.shape[0], rows_in.shape[1])
    head_size = D // HEADS
    modulation = low_back(jnp.dot(low(jax.nn.silu(condition)), ada_w, precision=highest) + ada_b)
    shift_one, scale_one, gate_one, shift_two, scale_two, gate_two = jnp.split(modulation, 6, axis=1)
    normed_one = low(modulate(rows_in, shift_one, scale_one))
    mixed_qkv = jnp.einsum('nbd,dsk->nbsk', normed_one, qkv_w, precision=highest)
    bias_full = jnp.stack([qkv_b[0], jnp.zeros_like(qkv_b[0]), qkv_b[1]])
    mixed_qkv = low_back(mixed_qkv + bias_full[None, None])
    queries = low(mixed_qkv[:, :, 0]).reshape(seq_len, batch_len, HEADS, head_size)
    keys_f = low(mixed_qkv[:, :, 1]).reshape(seq_len, batch_len, HEADS, head_size)
    values_f = low(mixed_qkv[:, :, 2]).reshape(seq_len, batch_len, HEADS, head_size)
    scores = low_back(jnp.einsum('nbhe,mbhe->bhnm', queries, keys_f, precision=highest) * head_size ** (-0.5))
    attn_probs = jax.nn.softmax(scores, axis=-1)
    attended = jnp.einsum('bhnm,mbhe->nbhe', low(attn_probs), values_f, precision=highest)
    attended = low_back(low(attended)).reshape(seq_len, batch_len, D)
    attn_out = low_back(jnp.einsum('nbk,kd->nbd', attended, out_w, precision=highest) + out_b)
    middle = rows_in + gate_one[None] * attn_out
    normed_two = low(modulate(middle, shift_two, scale_two))
    pre_act = jnp.einsum('nbd,df->nbf', normed_two, up_w, precision=highest)
    pre_act = low_back(pre_act + up_b)
    act_rows = low(jax.nn.gelu(pre_act, approximate=True))
    mlp_out = low_back(jnp.einsum('nbf,fd->nbd', act_rows, down_w, precision=highest) + down_b)
    return (middle + gate_two[None] * mlp_out) * valid_rows[None, :, None]

def reference(images_in, timesteps, labels, counts, label_table, ada_weight, ada_bias, qkv_weight, qkv_bias, out_weight, out_bias, up_weight, up_bias, down_weight, down_bias, out_cotangent):
    weights_all = (ada_weight, ada_bias, qkv_weight, qkv_bias, out_weight, out_bias, up_weight, up_bias, down_weight, down_bias)
    params_zero = tuple((w[0].astype(jnp.float32) for w in weights_all))
    params_one = tuple((w[1].astype(jnp.float32) for w in weights_all))

    def embed_labels(table_f):
        return table_f[labels] + time_embed(timesteps, D)
    condition_all, embed_back = jax.vjp(embed_labels, label_table.astype(jnp.float32))
    slot_total = images_in.shape[1]
    groups_dp = slot_total // SLOTS
    slot_index = jnp.arange(slot_total, dtype=jnp.int32) % SLOTS
    owner_group = jnp.arange(slot_total, dtype=jnp.int32) // SLOTS
    valid_all = (slot_index < counts[owner_group]).astype(jnp.float32)

    def by_group(array_in):
        shaped = array_in.reshape(SEQ, groups_dp, SLOTS, D)
        return jnp.moveaxis(shaped, 1, 0)
    inputs_g = by_group(images_in)
    cot_g = by_group(out_cotangent)
    cond_g = condition_all.reshape(groups_dp, SLOTS, D)
    valid_g = valid_all.reshape(groups_dp, SLOTS)

    def group_step(carried, group_item):
        rows_g, cond_rows, valid_rows, cot_rows = group_item

        def apply_here(rows_in, condition, params):
            return layer_apply(rows_in, condition, valid_rows, params)
        first_out, first_back = jax.vjp(apply_here, rows_g.astype(jnp.float32), cond_rows, params_zero)
        first_b = first_out.astype(jnp.bfloat16)
        second_out, second_back = jax.vjp(apply_here, first_b.astype(jnp.float32), cond_rows, params_one)
        middle_grad, cond_two, grads_one = second_back(cot_rows.astype(jnp.float32))
        input_grad, cond_one, grads_zero = first_back(middle_grad)
        carried = (jax.tree.map(lambda first_val, later_val: first_val + later_val, carried[0], grads_zero), jax.tree.map(lambda first_val, later_val: first_val + later_val, carried[1], grads_one))
        emitted = (first_b, second_out.astype(jnp.bfloat16), input_grad.astype(jnp.bfloat16), middle_grad.astype(jnp.bfloat16), cond_one + cond_two)
        return (carried, emitted)
    initial = (jax.tree.map(jnp.zeros_like, params_zero), jax.tree.map(jnp.zeros_like, params_one))
    grads_sum, emitted = lax.scan(group_step, initial, (inputs_g, cond_g, valid_g, cot_g))
    first_b, second_b, input_grad, middle_grad, cond_rows = emitted

    def back_layout(stacked):
        return jnp.moveaxis(stacked, 0, 1).reshape(SEQ, slot_total, D)
    layer_out = jnp.stack([back_layout(first_b), back_layout(second_b)])
    in_grad = jnp.stack([back_layout(input_grad), back_layout(middle_grad)])
    cond_grad = cond_rows.reshape(slot_total, D)
    table_grad = embed_back(cond_grad)[0]
    stacked = [jnp.stack([grads_sum[0][i], grads_sum[1][i]]) for i in range(10)]
    return (layer_out, in_grad, cond_grad, table_grad, stacked[0], stacked[1], stacked[2], stacked[3], stacked[4], stacked[5], stacked[6], stacked[7], stacked[8], stacked[9])
```

```python
import functools
import math
import jax
import jax.numpy as jnp
from jax import lax
from jax.experimental import pallas as pl
from jax.experimental.pallas import tpu as pltpu
from jax.sharding import PartitionSpec as P

HEADS = 16
eps_norm = 1e-06
BF, F32 = jnp.bfloat16, jnp.float32
ANY = pl.BlockSpec(memory_space=pl.ANY)
VM = pl.BlockSpec(memory_space=pltpu.VMEM)
LIMIT = 60 * 1024 * 1024
ROOT = math.sqrt(2.0 / math.pi)
CUBE = 0.044715


def nt(left, right):
    return lax.dot_general(left, right, (((1,), (1,)), ((), ())), preferred_element_type=F32)


def tn(left, right):
    return lax.dot_general(left, right, (((0,), (0,)), ((), ())), preferred_element_type=F32)


def nn(left, right):
    return jnp.dot(left, right, preferred_element_type=F32)


def norm_parts(rows):
    centered = rows - jnp.mean(rows, axis=-1, keepdims=True)
    inverse = lax.rsqrt(jnp.mean(centered * centered, axis=-1, keepdims=True) + eps_norm)
    return centered * inverse, inverse


def windows(width, size):
    spans = []
    for head in range(width // size):
        low, high = head * size, (head + 1) * size
        spans.append((low, high, low // 128 * 128, min(width, (high + 127) // 128 * 128)))
    return spans


def head_mask(span):
    low, high, start, stop = span
    lanes = lax.broadcasted_iota(jnp.int32, (1, stop - start), 1) + start
    return (lanes >= low) & (lanes < high)


class Copies:
    def __init__(self, sems):
        self.sems, self.used = sems, 0

    def start(self, source, target):
        copy = pltpu.make_async_copy(source, target, self.sems.at[self.used])
        self.used += 1
        copy.start()
        return copy


def soft(scores, scale):
    top = jnp.max(scores, axis=-1, keepdims=True)
    powers = jnp.exp2((scores - top) * (scale * math.log2(math.e)))
    return powers * (1.0 / jnp.sum(powers, axis=-1, keepdims=True))


def layer_kernel(chunks, index_ref, x_ref, mod_ref, bqv_ref, bup_ref, bod_ref,
                 wqo, wqt, woo, wot, wuo, wut, wdo, wdt, *rest):
    extra = len(rest) - 28
    rest = rest[extra:]
    (y_ref, xs, h1s, qkvo, qkvt, atts, aos, h2s, preo, pret, acto, actt, mos,
     wq, wo, wu, wd, h1, qkv, att, attf, ao, h2, pre, act, mo, mid, sems) = rest
    copies = Copies(sems)
    img = index_ref[0]
    qkv_in = [copies.start(wqo, wq.at[0]), copies.start(wqt, wq.at[1])]
    out_in = [copies.start(woo, wo.at[0]), copies.start(wot, wo.at[1])]
    up_in = [copies.start(wuo, wu.at[0]), copies.start(wut, wu.at[1])]
    down_in = [copies.start(wdo, wd.at[0]), copies.start(wdt, wd.at[1])]
    pending = [copies.start(x_ref, xs.at[img])]
    half = att.shape[2]
    size = 2 * half // HEADS
    scale = size ** (-0.5)
    mods = mod_ref[img]
    rows = x_ref[...].astype(F32)
    normed, _ = norm_parts(rows)
    h1[...] = (normed * (1.0 + mods[1:2]) + mods[0:1]).astype(BF)
    pending.append(copies.start(h1, h1s.at[img]))
    for copy in qkv_in:
        copy.wait()

    def project(part, carry):
        side, kind = part // 3, part % 3
        mixed = nn(h1[...], wq[side, kind])
        qkv[side, kind] = (mixed + bqv_ref[pl.ds(part, 1)]).astype(BF)
        return carry

    lax.fori_loop(0, 6, project, 0)
    pending += [copies.start(qkv.at[0], qkvo.at[img]), copies.start(qkv.at[1], qkvt.at[img])]

    def attend(side, carry):
        attf[...] = jnp.zeros_like(attf)
        for span in windows(half, size):
            part = slice(span[2], span[3])
            mask = head_mask(span)
            zero = jnp.zeros((), BF)
            queries = jnp.where(mask, qkv[side, 0, :, part], zero)
            scores = nt(queries, qkv[side, 1, :, part])
            probs = soft(scores, scale).astype(BF)
            attf[:, part] += nn(probs, jnp.where(mask, qkv[side, 2, :, part], zero))
        att[side] = attf[...].astype(BF)
        return carry

    lax.fori_loop(0, 2, attend, 0)
    pending.append(copies.start(att, atts.at[img]))
    for copy in out_in:
        copy.wait()
    ao[...] = nn(att[0], wo[0]) + nn(att[1], wo[1]) + bod_ref[0:1]
    pending.append(copies.start(ao, aos.at[img]))
    mid[...] = rows + mods[2:3] * ao[...]
    normed, _ = norm_parts(mid[...])
    h2[...] = (normed * (1.0 + mods[4:5]) + mods[3:4]).astype(BF)
    pending.append(copies.start(h2, h2s.at[img]))
    mo[...] = jnp.broadcast_to(bod_ref[1:2], mo.shape)
    for copy in up_in:
        copy.wait()
    for copy in down_in:
        copy.wait()
    step = bup_ref.shape[1] // chunks

    def mlp(part, carry):
        side, place = part // chunks, part % chunks
        spot = pl.ds(pl.multiple_of(place * step, 128), step)
        values = nn(h2[...], wu[side, :, spot]) + bup_ref[pl.ds(side, 1), spot]
        pre[side, :, spot] = values.astype(BF)
        inner = jnp.tanh(values * (ROOT + ROOT * CUBE * values * values))
        acted = (0.5 * values * (1.0 + inner)).astype(BF)
        act[side, :, spot] = acted
        mo[...] += nn(acted, wd[side, spot, :])
        return carry

    lax.fori_loop(0, 2 * chunks, mlp, 0)
    pending += [copies.start(pre.at[0], preo.at[img]), copies.start(pre.at[1], pret.at[img]),
                copies.start(act.at[0], acto.at[img]), copies.start(act.at[1], actt.at[img]),
                copies.start(mo, mos.at[img])]
    y_ref[...] = (mods[6:7] * (mid[...] + mods[5:6] * mo[...])).astype(BF)
    for copy in pending:
        copy.wait()


def layer_call(index, x, mods, bqv, bup, bod, weights, saved, images):
    tokens, width = x.shape
    half, hidden = width // 2, bup.shape[1]
    chunks = 3 if hidden % 384 == 0 else 1
    sd = jax.ShapeDtypeStruct
    outs = (
        sd((tokens, width), BF),
        sd((images, tokens, width), BF),
        sd((images, tokens, width), BF),
        sd((images, 3, tokens, half), BF),
        sd((images, 3, tokens, half), BF),
        sd((images, 2, tokens, half), BF),
        sd((images, tokens, width), F32),
        sd((images, tokens, width), BF),
        sd((images, tokens, hidden), BF),
        sd((images, tokens, hidden), BF),
        sd((images, tokens, hidden), BF),
        sd((images, tokens, hidden), BF),
        sd((images, tokens, width), F32),
    )
    saved = tuple(saved) if saved is not None else ()
    aliases = {14 + i: 1 + i for i in range(len(saved))}
    scratch = [
        pltpu.VMEM((2, 3, width, half), BF),
        pltpu.VMEM((2, half, width), BF),
        pltpu.VMEM((2, width, hidden), BF),
        pltpu.VMEM((2, hidden, width), BF),
        pltpu.VMEM((tokens, width), BF),
        pltpu.VMEM((2, 3, tokens, half), BF),
        pltpu.VMEM((2, tokens, half), BF),
        pltpu.VMEM((tokens, half), F32),
        pltpu.VMEM((tokens, width), F32),
        pltpu.VMEM((tokens, width), BF),
        pltpu.VMEM((2, tokens, hidden), BF),
        pltpu.VMEM((2, tokens, hidden), BF),
        pltpu.VMEM((tokens, width), F32),
        pltpu.VMEM((tokens, width), F32),
        pltpu.SemaphoreType.DMA((32,)),
    ]
    return pl.pallas_call(
        functools.partial(layer_kernel, chunks),
        out_shape=outs,
        in_specs=[pl.BlockSpec(memory_space=pltpu.SMEM)] + [VM] * 5 + [ANY] * (8 + len(saved)),
        out_specs=[VM] + [ANY] * 12,
        scratch_shapes=scratch,
        input_output_aliases=aliases,
        compiler_params=pltpu.CompilerParams(vmem_limit_bytes=LIMIT),
        cost_estimate=pl.CostEstimate(flops=2 * tokens * width * (6 * half * 2 + 4 * hidden), bytes_accessed=4 * width * (4 * half + 2 * hidden), transcendentals=0),
        name="layer",
    )(index, x, mods, bqv, bup, bod, *weights, *saved)


def mlp_back_kernel(chunks, index_ref, g_ref, mod_ref, xs, aos, mos, preo, pret, wuo, wut, wdo, wdt, *rest):
    rest = rest[len(rest) - 18:]
    (mg_ref, sum_ref, bu_ref, dis, pgo, pgt, wu, wd, x, ao, mo, pre, di, pg, ng, og, sems, _) = rest
    copies = Copies(sems)
    img = index_ref[0]
    first = [copies.start(mos.at[img], mo)]
    second = [copies.start(preo.at[img], pre.at[0]), copies.start(pret.at[img], pre.at[1]),
              copies.start(wdo, wd.at[0]), copies.start(wdt, wd.at[1]),
              copies.start(wuo, wu.at[0]), copies.start(wut, wu.at[1])]
    third = [copies.start(xs.at[img], x), copies.start(aos.at[img], ao)]
    mods = mod_ref[img]
    og[...] = g_ref[...].astype(F32) * mods[6:7]
    di[...] = (og[...] * mods[5:6]).astype(BF)
    pending = [copies.start(di, dis.at[img])]
    for copy in first:
        copy.wait()
    sum_ref[2:3] = jnp.sum(og[...] * mo[...], axis=0, keepdims=True)
    sum_ref[3:4] = jnp.sum(di[...].astype(F32), axis=0, keepdims=True)
    ng[...] = jnp.zeros_like(ng)
    for copy in second:
        copy.wait()
    step = pre.shape[2] // chunks

    def mlp(part, carry):
        side, place = part // chunks, part % chunks
        spot = pl.ds(pl.multiple_of(place * step, 128), step)
        values = pre[side, :, spot].astype(F32)
        grad = nt(di[...], wd[side, spot, :])
        square = values * values
        inner = jnp.tanh(values * (ROOT + ROOT * CUBE * square))
        slope = 0.5 * (1.0 + inner) + 0.5 * values * (1.0 - inner * inner) * (ROOT + 3.0 * ROOT * CUBE * square)
        graded = (grad * slope).astype(BF)
        pg[side, :, spot] = graded
        bu_ref[pl.ds(side, 1), spot] = jnp.sum(graded.astype(F32), axis=0, keepdims=True)
        ng[...] += nt(graded, wu[side, :, spot])
        return carry

    lax.fori_loop(0, 2 * chunks, mlp, 0)
    pending += [copies.start(pg.at[0], pgo.at[img]), copies.start(pg.at[1], pgt.at[img])]
    for copy in third:
        copy.wait()
    normed, inverse = norm_parts(x[...].astype(F32) + mods[2:3] * ao[...])
    sum_ref[0:1] = jnp.sum(ng[...], axis=0, keepdims=True)
    sum_ref[1:2] = jnp.sum(ng[...] * normed, axis=0, keepdims=True)
    dn = ng[...] * (1.0 + mods[4:5])
    mg_ref[...] = og[...] + inverse * (
        dn - jnp.mean(dn, axis=-1, keepdims=True) - normed * jnp.mean(dn * normed, axis=-1, keepdims=True))
    for copy in pending:
        copy.wait()


def mlp_back_call(index, grad, mods, saved, weights, kept, images):
    xs, aos, mos, preo, pret = saved
    tokens, width = grad.shape
    hidden = preo.shape[2]
    chunks = 3 if hidden % 384 == 0 else 1
    sd = jax.ShapeDtypeStruct
    kept = tuple(kept) if kept is not None else ()
    aliases = {12 + i: 3 + i for i in range(len(kept))}
    scratch = [
        pltpu.VMEM((2, width, hidden), BF),
        pltpu.VMEM((2, hidden, width), BF),
        pltpu.VMEM((tokens, width), BF),
        pltpu.VMEM((tokens, width), F32),
        pltpu.VMEM((tokens, width), F32),
        pltpu.VMEM((2, tokens, hidden), BF),
        pltpu.VMEM((tokens, width), BF),
        pltpu.VMEM((2, tokens, hidden), BF),
        pltpu.VMEM((tokens, width), F32),
        pltpu.VMEM((tokens, width), F32),
        pltpu.SemaphoreType.DMA((16,)),
        pltpu.VMEM((8, 128), F32),
    ]
    return pl.pallas_call(
        functools.partial(mlp_back_kernel, chunks),
        out_shape=(
            sd((tokens, width), F32), sd((8, width), F32), sd((2, hidden), F32),
            sd((images, tokens, width), BF), sd((images, tokens, hidden), BF), sd((images, tokens, hidden), BF)),
        in_specs=[pl.BlockSpec(memory_space=pltpu.SMEM)] + [VM] * 2 + [ANY] * (9 + len(kept)),
        out_specs=[VM] * 3 + [ANY] * 3,
        scratch_shapes=scratch,
        input_output_aliases=aliases,
        compiler_params=pltpu.CompilerParams(vmem_limit_bytes=LIMIT),
        cost_estimate=pl.CostEstimate(flops=2 * tokens * width * 4 * hidden, bytes_accessed=4 * width * 2 * hidden, transcendentals=0),
        name="mlp_back",
    )(index, grad, mods, xs, aos, mos, preo, pret, *weights, *kept)


def attn_back_kernel(index_ref, mg_ref, mod_ref, xs, aos, qkvo, qkvt, wqo, wqt, woo, wot, *rest):
    rest = rest[len(rest) - 17:]
    (rg_ref, sum_ref, bqv_ref, ois, qgo, qgt, wq, wo, x, ao, qkv, oi, qg, da, acc, ng, sems) = rest
    copies = Copies(sems)
    img = index_ref[0]
    first = [copies.start(aos.at[img], ao)]
    second = [copies.start(woo, wo.at[0]), copies.start(wot, wo.at[1])]
    third = [copies.start(qkvo.at[img], qkv.at[0]), copies.start(qkvt.at[img], qkv.at[1])]
    fourth = [copies.start(wqo, wq.at[0]), copies.start(wqt, wq.at[1])]
    fifth = [copies.start(xs.at[img], x)]
    half = wo.shape[1]
    size = 2 * half // HEADS
    scale = size ** (-0.5)
    mods = mod_ref[img]
    oi[...] = (mg_ref[...] * mods[2:3]).astype(BF)
    pending = [copies.start(oi, ois.at[img])]
    sum_ref[3:4] = jnp.sum(oi[...].astype(F32), axis=0, keepdims=True)
    for copy in first + second + third:
        copy.wait()
    sum_ref[2:3] = jnp.sum(mg_ref[...] * ao[...], axis=0, keepdims=True)

    def attend(side, carry):
        da[...] = nt(oi[...], wo[side]).astype(BF)
        for kind in range(3):
            acc[kind] = jnp.zeros_like(acc[kind])
        for span in windows(half, size):
            part = slice(span[2], span[3])
            mask = head_mask(span)
            zero = jnp.zeros((), BF)
            queries = jnp.where(mask, qkv[side, 0, :, part], zero)
            keys = jnp.where(mask, qkv[side, 1, :, part], zero)
            outer = jnp.where(mask, da[:, part], zero)
            probs = soft(nt(queries, keys), scale)
            grads = nt(outer, qkv[side, 2, :, part])
            inner = jnp.sum(grads * probs, axis=-1, keepdims=True)
            spread = (probs * (grads - inner)).astype(BF)
            acc[2, :, part] += tn(probs.astype(BF), outer)
            acc[0, :, part] += nn(spread, keys)
            acc[1, :, part] += tn(spread, queries)
        for kind in range(3):
            factor = 1.0 if kind == 2 else scale
            qg[side, kind] = (acc[kind] * factor).astype(BF)
        return carry

    lax.fori_loop(0, 2, attend, 0)
    pending += [copies.start(qg.at[0, 0], qgo.at[0, img]), copies.start(qg.at[0, 1], qgo.at[1, img]),
                copies.start(qg.at[0, 2], qgo.at[2, img]), copies.start(qg.at[1, 0], qgt.at[0, img]),
                copies.start(qg.at[1, 1], qgt.at[1, img]), copies.start(qg.at[1, 2], qgt.at[2, img])]
    ng[...] = jnp.zeros_like(ng)
    for copy in fourth:
        copy.wait()

    def project(part, carry):
        side, kind = part // 3, part % 3
        graded = qg[side, kind]
        bqv_ref[pl.ds(part, 1)] = jnp.sum(graded.astype(F32), axis=0, keepdims=True)
        ng[...] += nt(graded, wq[side, kind])
        return carry

    lax.fori_loop(0, 6, project, 0)
    for copy in fifth:
        copy.wait()
    normed, inverse = norm_parts(x[...].astype(F32))
    sum_ref[0:1] = jnp.sum(ng[...], axis=0, keepdims=True)
    sum_ref[1:2] = jnp.sum(ng[...] * normed, axis=0, keepdims=True)
    dn = ng[...] * (1.0 + mods[1:2])
    rg_ref[...] = (mg_ref[...] + inverse * (
        dn - jnp.mean(dn, axis=-1, keepdims=True) - normed * jnp.mean(dn * normed, axis=-1, keepdims=True))).astype(BF)
    for copy in pending:
        copy.wait()


def attn_back_call(index, grad, mods, saved, weights, kept, images):
    xs, aos, qkvo, qkvt = saved
    tokens, width = grad.shape
    half = width // 2
    sd = jax.ShapeDtypeStruct
    kept = tuple(kept) if kept is not None else ()
    aliases = {11 + i: 3 + i for i in range(len(kept))}
    scratch = [
        pltpu.VMEM((2, 3, width, half), BF),
        pltpu.VMEM((2, half, width), BF),
        pltpu.VMEM((tokens, width), BF),
        pltpu.VMEM((tokens, width), F32),
        pltpu.VMEM((2, 3, tokens, half), BF),
        pltpu.VMEM((tokens, width), BF),
        pltpu.VMEM((2, 3, tokens, half), BF),
        pltpu.VMEM((tokens, half), BF),
        pltpu.VMEM((3, tokens, half), F32),
        pltpu.VMEM((tokens, width), F32),
        pltpu.SemaphoreType.DMA((16,)),
    ]
    return pl.pallas_call(
        attn_back_kernel,
        out_shape=(
            sd((tokens, width), BF), sd((8, width), F32), sd((8, half), F32),
            sd((images, tokens, width), BF), sd((3, images, tokens, half), BF), sd((3, images, tokens, half), BF)),
        in_specs=[pl.BlockSpec(memory_space=pltpu.SMEM)] + [VM] * 2 + [ANY] * (8 + len(kept)),
        out_specs=[VM] * 3 + [ANY] * 3,
        scratch_shapes=scratch,
        input_output_aliases=aliases,
        compiler_params=pltpu.CompilerParams(vmem_limit_bytes=LIMIT),
        cost_estimate=pl.CostEstimate(flops=2 * tokens * width * 12 * half, bytes_accessed=4 * width * 4 * half, transcendentals=0),
        name="attn_back",
    )(index, grad, mods, xs, aos, qkvo, qkvt, *weights, *kept)


def time_embed(timesteps, width_all):
    half_width = width_all // 2
    frequencies = jnp.exp(-math.log(10000.0) * jnp.arange(half_width, dtype=F32) / half_width)
    angles = timesteps.astype(F32)[:, None] * frequencies[None, :]
    return jnp.concatenate([jnp.cos(angles), jnp.sin(angles)], axis=1)


def swap(array):
    return lax.ppermute(array, "tensor", [(0, 1), (1, 0)])


def ring_order(peers):
    order = list(range(0, peers, 2)) + list(range(1, peers, 2))[::-1]
    place = [order.index(peer) for peer in range(peers)]
    ahead = [(order[i], order[(i + 1) % peers]) for i in range(peers)]
    return place, ahead, [(b, a) for a, b in ahead]


def ring_sum(terms):
    peers = lax.axis_size("dp")
    place, ahead, behind = ring_order(peers)
    here = jnp.asarray(place, jnp.int32)[lax.axis_index("dp")]
    count, width = terms.shape
    part = count // (2 * peers)
    blocks = terms.reshape(2, peers, part, width)
    total = jnp.zeros((2, peers, part, width), F32)
    lanes = ((ahead, 1), (behind, -1))

    def block(side, number):
        return lax.dynamic_slice(blocks, (side, number % peers, 0, 0), (1, 1, part, width))

    moving = [block(side, here) for side in range(2)]
    for step in range(1, peers):
        for side, (pairs, sign) in enumerate(lanes):
            came = lax.ppermute(moving[side], "dp", pairs)
            mine = block(side, here - sign * step)
            moving[side] = (came.astype(F32) + mine.astype(F32)).astype(BF)
    for step in range(peers):
        for side, (pairs, sign) in enumerate(lanes):
            owner = (here - sign * (peers - 1 + step)) % peers
            total = lax.dynamic_update_slice(total, moving[side].astype(F32), (side, owner, 0, 0))
            if step < peers - 1:
                moving[side] = lax.ppermute(moving[side], "dp", pairs)
    return total.reshape(count, width)


def folded(other, own):
    came = swap(other.astype(BF))
    return (own + came.astype(F32)).astype(BF)


def outer(left, right):
    return jnp.einsum("btk,btd->kd", left, right, preferred_element_type=F32)


def outers(left, right):
    return jnp.einsum("jbtk,btd->jkd", left, right, preferred_element_type=F32)


def shards(images_in, timesteps, labels, counts, label_table, ada_weight, ada_bias, qkv_weight,
           qkv_bias, out_weight, out_bias, up_weight, up_bias, down_weight, down_bias, out_cotangent):
    is_first = lax.axis_index("section") == 0
    core = lax.axis_index("tensor")
    slots = images_in.shape[1]
    images = slots // 2
    width = images_in.shape[2]
    hidden = up_weight.shape[2]
    half = out_weight.shape[1]

    def by_section(first_val, later_val):
        return jnp.where(is_first, first_val, later_val)

    def by_core(first_val, later_val):
        return jnp.where(core == 0, first_val, later_val)

    def mine(array, axis):
        return lax.dynamic_slice_in_dim(array, core * images, images, axis)

    def others(array, axis):
        return lax.dynamic_slice_in_dim(array, (1 - core) * images, images, axis)

    def in_order(own, came, axis):
        return by_core(jnp.concatenate([own, came], axis), jnp.concatenate([came, own], axis))

    def whole_images(rows):
        came = swap(others(rows, 1))
        return jnp.moveaxis(jnp.concatenate([mine(rows, 1), came], axis=0), 1, 0)

    def split_images(rows):
        local = rows.shape[1] // 2
        came = swap(rows[:, local:])
        return jnp.moveaxis(in_order(rows[:, :local], came, 0), 0, 1)[None]

    qkv_own = jnp.moveaxis(qkv_weight[0], 1, 0)
    w_qkv = (qkv_own, swap(qkv_own))
    w_out = (out_weight[0], swap(out_weight[0]))
    w_up = (up_weight[0], swap(up_weight[0]))
    w_down = (down_weight[0], swap(down_weight[0]))
    weights = (*w_qkv, *w_out, *w_up, *w_down)

    condition = jnp.take(label_table, labels, axis=0).astype(F32) + time_embed(timesteps, width)
    silu_cond, silu_back = jax.vjp(jax.nn.silu, condition)
    silu_b = silu_cond.astype(BF)
    mod_local = (
        jnp.dot(silu_b, ada_weight[0], preferred_element_type=F32) + ada_bias[0].astype(F32)[None]
    )
    modulation = in_order(mine(mod_local, 0), swap(others(mod_local, 0)), 1).reshape(images, 6, width)
    slot_no = core * images + jnp.arange(images, dtype=jnp.int32)
    valid = (slot_no < counts[0]).astype(F32)
    mods = jnp.concatenate(
        [modulation, jnp.broadcast_to(valid[:, None, None], (images, 2, width))], axis=1
    )
    pair_bias = jnp.concatenate([qkv_bias[0, 0], qkv_bias[0, 1], up_bias[0]])[None]
    pair_bias = jnp.concatenate([pair_bias, swap(pair_bias)], axis=0).astype(F32)
    zero_row = jnp.zeros((half,), F32)
    bqv = jnp.stack([
        pair_bias[0, :half], zero_row, pair_bias[0, half : 2 * half],
        pair_bias[1, :half], zero_row, pair_bias[1, half : 2 * half], zero_row, zero_row])
    bup = pair_bias[:, 2 * half :]
    bod = jnp.concatenate([out_bias, down_bias], axis=0).astype(F32)

    rows_in = whole_images(images_in)
    cotangent = whole_images(out_cotangent)

    saved, received, results = (None, None, [])
    for turn in range(images + 1):
        early, later = min(turn, images - 1), max(turn - 1, 0)
        index = by_section(jnp.int32(early), jnp.int32(later)).reshape(1)
        layer_in = rows_in[early] if received is None else by_section(rows_in[early], received)
        answer = layer_call(index, layer_in, mods, bqv, bup, bod, weights, saved, images)
        result, saved = answer[0], answer[1:]
        results.append(result)
        if turn < images:
            received = lax.ppermute(result, "section", [(0, 1)])
    layer_out = split_images(
        jnp.stack([by_section(results[i], results[i + 1]) for i in range(images)])
    )
    xs, h1s, qkvo, qkvt, atts, aos, h2s, preo, pret, acto, actt, mos = saved

    mlp_kept, attn_kept, received, turns = (None, None, None, [])
    for turn in range(images + 1):
        early, later = min(turn, images - 1), max(turn - 1, 0)
        index = by_section(jnp.int32(later), jnp.int32(early)).reshape(1)
        grad = cotangent[early] if received is None else by_section(received, cotangent[early])
        answer = mlp_back_call(
            index, grad, mods, (xs, aos, mos, preo, pret), (*w_up, *w_down), mlp_kept, images
        )
        middle_grad, mlp_sums, up_sums, mlp_kept = answer[0], answer[1], answer[2], answer[3:]
        answer = attn_back_call(
            index, middle_grad, mods, (xs, aos, qkvo, qkvt), (*w_qkv, *w_out), attn_kept, images
        )
        row_grad, attn_sums, qkv_sums, attn_kept = answer[0], answer[1], answer[2], answer[3:]
        turns.append((row_grad, mlp_sums, up_sums, attn_sums, qkv_sums))
        if turn < images:
            received = lax.ppermute(row_grad, "section", [(1, 0)])
    by_image = [
        jax.tree.map(by_section, turns[i + 1], turns[i]) if i < images - 1 else turns[i + 1]
        for i in range(images)
    ]
    in_grad = split_images(jnp.stack([item[0] for item in by_image]))
    down_ins, pre_grads_o, pre_grads_t = mlp_kept
    out_ins, qkv_grads_o, qkv_grads_t = attn_kept

    down_w = folded(outer(actt, down_ins), outer(acto, down_ins))
    up_w = folded(outer(h2s, pre_grads_t), outer(h2s, pre_grads_o))
    stacked = 3 * half
    attn_w = folded(
        jnp.concatenate([outers(qkv_grads_t, h1s).reshape(stacked, width), outer(atts[:, 1], out_ins)]),
        jnp.concatenate([outers(qkv_grads_o, h1s).reshape(stacked, width), outer(atts[:, 0], out_ins)]),
    )
    down_w_sum, up_w_sum, attn_w_sum = ring_sum(down_w), ring_sum(up_w), ring_sum(attn_w)
    qkv_w_sum = jnp.moveaxis(attn_w_sum[:stacked].reshape(3, half, width), 2, 0)
    out_w_sum = attn_w_sum[stacked:]

    mod_grad = jnp.stack([
        jnp.concatenate([item[3][0], item[3][1], item[3][2], item[1][0], item[1][1], item[1][2]])
        for item in by_image
    ]).astype(BF)
    columns = mod_grad.reshape(images, 2, 3 * width)
    own_cols = lax.dynamic_index_in_dim(columns, core, 1, keepdims=False)
    other_cols = lax.dynamic_index_in_dim(columns, 1 - core, 1, keepdims=False)
    mod_cols = in_order(own_cols, swap(other_cols), 0)
    silu_grad = jnp.einsum("sk,dk->sd", mod_cols, ada_weight[0], preferred_element_type=F32)
    silu_grad = silu_grad + swap(silu_grad)
    silu_grad = silu_grad + lax.ppermute(silu_grad, "section", [(0, 1), (1, 0)])
    cond_grad = silu_back(silu_grad)[0]

    def spread(array):
        return lax.all_gather(array, "dp", axis=0, tiled=True)

    silu_all, mod_all, cond_all = spread(silu_b), spread(mod_cols), spread(cond_grad)
    ada_w_sum = jnp.einsum("sd,sk->dk", silu_all, mod_all, preferred_element_type=F32)
    ada_b_sum = jnp.sum(mod_all, axis=0, dtype=F32)

    total = jax.tree.map(lambda *items: sum(items), *by_image)
    own_bias = jnp.concatenate([total[4][0], total[4][2], total[2][0]])
    other_bias = jnp.concatenate([total[4][3], total[4][5], total[2][1]])
    both_bias = jnp.concatenate([total[3][3], total[1][3]])
    own_bias = own_bias + swap(other_bias)
    both_bias = both_bias + swap(both_bias)
    gathered = spread(jnp.concatenate([own_bias, both_bias, labels.astype(F32)])[None])
    biases = jnp.sum(gathered, axis=0)
    labels_all = gathered[:, -slots:].reshape(-1)
    onehot = (labels_all[None] == jnp.arange(label_table.shape[0], dtype=F32)[:, None]).astype(F32)
    table_grad = jnp.dot(onehot, cond_all, precision=lax.Precision.HIGHEST, preferred_element_type=F32)
    qkv_b_sum = biases[: 2 * half].reshape(2, half)
    up_b_sum = biases[2 * half : 2 * half + hidden]
    out_b_sum = biases[2 * half + hidden : 2 * half + hidden + width]
    down_b_sum = biases[2 * half + hidden + width : 2 * half + hidden + 2 * width]
    return (
        layer_out,
        in_grad,
        cond_grad,
        table_grad,
        ada_w_sum[None],
        ada_b_sum[None],
        qkv_w_sum[None],
        qkv_b_sum[None],
        out_w_sum[None],
        out_b_sum[None],
        up_w_sum[None],
        up_b_sum[None],
        down_w_sum[None],
        down_b_sum[None],
    )


def solution(mesh):
    placed = (
        P("tensor", "dp", None),
        P("dp"),
        P("dp"),
        P("dp"),
        P(),
        P("section", None, "tensor"),
        P("section", "tensor"),
        P("section", None, None, "tensor"),
        P("section", None, "tensor"),
        P("section", "tensor", None),
        P("section", None),
        P("section", None, "tensor"),
        P("section", "tensor"),
        P("section", "tensor", None),
        P("section", None),
        P("tensor", "dp", None),
    )
    return jax.shard_map(
        shards,
        mesh=mesh,
        in_specs=placed,
        out_specs=(
            P("section", "tensor", "dp", None),
            P("section", "tensor", "dp", None),
            P("dp", None),
            P(),
            P("section", None, "tensor"),
            P("section", "tensor"),
            P("section", None, None, "tensor"),
            P("section", None, "tensor"),
            P("section", "tensor", None),
            P("section", None),
            P("section", None, "tensor"),
            P("section", "tensor"),
            P("section", "tensor", None),
            P("section", None),
        ),
        check_vma=False,
    )
```

```python
import functools
import math
import jax
import jax.numpy as jnp
from jax import lax
from jax.experimental import pallas as pl
from jax.experimental.pallas import tpu as pltpu
from jax.sharding import PartitionSpec as P

HEADS = 16
eps_norm = 1e-06
BF, F32 = jnp.bfloat16, jnp.float32
ANY = pl.BlockSpec(memory_space=pl.ANY)
VM = pl.BlockSpec(memory_space=pltpu.VMEM)
LIMIT = 60 * 1024 * 1024
DEPTH = 4
ROOT = math.sqrt(2.0 / math.pi)
CUBE = 0.044715


def nt(left, right):
    return lax.dot_general(left, right, (((1,), (1,)), ((), ())), preferred_element_type=F32)


def tn(left, right):
    return lax.dot_general(left, right, (((0,), (0,)), ((), ())), preferred_element_type=F32)


def nn(left, right):
    return jnp.dot(left, right, preferred_element_type=F32)


def norm_parts(rows):
    centered = rows - jnp.mean(rows, axis=-1, keepdims=True)
    inverse = lax.rsqrt(jnp.mean(centered * centered, axis=-1, keepdims=True) + eps_norm)
    return centered * inverse, inverse


def windows(width, size):
    spans = []
    for head in range(width // size):
        low, high = head * size, (head + 1) * size
        spans.append((low, high, low // 128 * 128, min(width, (high + 127) // 128 * 128)))
    return spans


def head_mask(span):
    low, high, start, stop = span
    lanes = lax.broadcasted_iota(jnp.int32, (1, stop - start), 1) + start
    return (lanes >= low) & (lanes < high)


class Copies:
    def __init__(self, sems):
        self.sems, self.used = sems, 0

    def start(self, source, target):
        copy = pltpu.make_async_copy(source, target, self.sems.at[self.used])
        self.used += 1
        copy.start()
        return copy


class Stream:
    def __init__(self, copies, depth, pairs):
        self.copies, self.depth, self.pairs, self.begun, self.taken = copies, depth, pairs, [], 0
        self.fill()

    def fill(self):
        while len(self.begun) < min(len(self.pairs), self.taken + self.depth):
            self.begun.append(self.copies.start(*self.pairs[len(self.begun)]))

    def take(self, count=1):
        for _ in range(count):
            self.begun[self.taken].wait()
            self.taken += 1
            self.fill()


def three_kinds(sources, target):
    return [(source.at[kind], target.at[side, kind]) for side, source in enumerate(sources) for kind in range(3)]


def soft(scores, scale):
    top = jnp.max(scores, axis=-1, keepdims=True)
    powers = jnp.exp2((scores - top) * (scale * math.log2(math.e)))
    return powers * (1.0 / jnp.sum(powers, axis=-1, keepdims=True))


def layer_kernel(chunks, index_ref, mod_ref, bqv_ref, bup_ref, bod_ref, x_in,
                 wqo, wqt, woo, wot, wuo, wut, wdo, wdt, *rest):
    rest = rest[len(rest) - 30:]
    (y_out, ys, xs, h1s, qkvo, qkvt, atts, aos, h2s, preo, pret, acto, actt, mos,
     wq, wo, wu, wd, x, y, h1, qkv, att, attf, ao, h2, pre, act, mo, sems) = rest

    @pl.when(index_ref[1] == 1)
    def _():
        copies = Copies(sems)
        img = index_ref[0]
        step = wu.shape[2] // chunks
        spots = [(side, slice(place * step, (place + 1) * step)) for side in range(2) for place in range(chunks)]
        pairs = [(x_in, x), *three_kinds((wqo, wqt), wq), (woo, wo.at[0]), (wot, wo.at[1])]
        for side, spot in spots:
            up, down = ((wuo, wdo), (wut, wdt))[side]
            pairs += [(up.at[:, spot], wu.at[side, :, spot]), (down.at[spot, :], wd.at[side, spot, :])]
        stream = Stream(copies, DEPTH, pairs)
        half = att.shape[2]
        size = 2 * half // HEADS
        scale = size ** (-0.5)
        mods = mod_ref[img]
        stream.take()
        pending = [copies.start(x, xs.at[img])]
        normed, _ = norm_parts(x[...].astype(F32))
        h1[...] = (normed * (1.0 + mods[1:2]) + mods[0:1]).astype(BF)
        pending.append(copies.start(h1, h1s.at[img]))
        for part in range(6):
            side, kind = part // 3, part % 3
            stream.take()
            mixed = nn(h1[...], wq[side, kind])
            qkv[side, kind] = (mixed + bqv_ref[part : part + 1]).astype(BF)
        pending += [copies.start(qkv.at[0], qkvo.at[img]), copies.start(qkv.at[1], qkvt.at[img])]

        def attend(side, carry):
            attf[...] = jnp.zeros_like(attf)
            for span in windows(half, size):
                part = slice(span[2], span[3])
                mask = head_mask(span)
                zero = jnp.zeros((), BF)
                queries = jnp.where(mask, qkv[side, 0, :, part], zero)
                scores = nt(queries, qkv[side, 1, :, part])
                probs = soft(scores, scale).astype(BF)
                attf[:, part] += nn(probs, jnp.where(mask, qkv[side, 2, :, part], zero))
            att[side] = attf[...].astype(BF)
            return carry

        lax.fori_loop(0, 2, attend, 0)
        pending.append(copies.start(att, atts.at[img]))
        stream.take(2)
        ao[...] = nn(att[0], wo[0]) + nn(att[1], wo[1]) + bod_ref[0:1]
        pending.append(copies.start(ao, aos.at[img]))
        normed, _ = norm_parts(x[...].astype(F32) + mods[2:3] * ao[...])
        h2[...] = (normed * (1.0 + mods[4:5]) + mods[3:4]).astype(BF)
        pending.append(copies.start(h2, h2s.at[img]))
        for number, (side, spot) in enumerate(spots):
            stream.take()
            values = nn(h2[...], wu[side, :, spot]) + bup_ref[side : side + 1, spot]
            pre[side, :, spot] = values.astype(BF)
            inner = jnp.tanh(values * (ROOT + ROOT * CUBE * values * values))
            act[side, :, spot] = (0.5 * values * (1.0 + inner)).astype(BF)
            stream.take()
            term = nn(act[side, :, spot], wd[side, spot, :])
            mo[...] = term + (bod_ref[1:2] if number == 0 else mo[...])
            pre_out, act_out = ((preo, acto), (pret, actt))[side]
            pending += [copies.start(pre.at[side, :, spot], pre_out.at[img, :, spot]),
                        copies.start(act.at[side, :, spot], act_out.at[img, :, spot])]
        pending.append(copies.start(mo, mos.at[img]))
        y[...] = (mods[6:7] * (x[...].astype(F32) + mods[2:3] * ao[...] + mods[5:6] * mo[...])).astype(BF)
        pending += [copies.start(y, y_out), copies.start(y, ys.at[img])]
        for copy in pending:
            copy.wait()


def cost(tokens, weight_count):
    return pl.CostEstimate(
        flops=2 * tokens * weight_count, bytes_accessed=2 * weight_count, transcendentals=0)


def layer_call(index, x, mods, bqv, bup, bod, weights, saved, images):
    tokens, width = x.shape
    half, hidden = width // 2, bup.shape[1]
    chunks = 3 if hidden % 384 == 0 else 1
    sd = jax.ShapeDtypeStruct
    outs = (
        sd((tokens, width), BF),
        sd((images, tokens, width), BF),
        sd((images, tokens, width), BF),
        sd((images, tokens, width), BF),
        sd((images, 3, tokens, half), BF),
        sd((images, 3, tokens, half), BF),
        sd((images, 2, tokens, half), BF),
        sd((images, tokens, width), F32),
        sd((images, tokens, width), BF),
        sd((images, tokens, hidden), BF),
        sd((images, tokens, hidden), BF),
        sd((images, tokens, hidden), BF),
        sd((images, tokens, hidden), BF),
        sd((images, tokens, width), F32),
    )
    saved = tuple(saved) if saved is not None else ()
    aliases = {14 + i: 1 + i for i in range(len(saved))}
    scratch = [
        pltpu.VMEM((2, 3, width, half), BF),
        pltpu.VMEM((2, half, width), BF),
        pltpu.VMEM((2, width, hidden), BF),
        pltpu.VMEM((2, hidden, width), BF),
        pltpu.VMEM((tokens, width), BF),
        pltpu.VMEM((tokens, width), BF),
        pltpu.VMEM((tokens, width), BF),
        pltpu.VMEM((2, 3, tokens, half), BF),
        pltpu.VMEM((2, tokens, half), BF),
        pltpu.VMEM((tokens, half), F32),
        pltpu.VMEM((tokens, width), F32),
        pltpu.VMEM((tokens, width), BF),
        pltpu.VMEM((2, tokens, hidden), BF),
        pltpu.VMEM((2, tokens, hidden), BF),
        pltpu.VMEM((tokens, width), F32),
        pltpu.SemaphoreType.DMA((64,)),
    ]
    return pl.pallas_call(
        functools.partial(layer_kernel, chunks),
        out_shape=outs,
        in_specs=[pl.BlockSpec(memory_space=pltpu.SMEM)] + [VM] * 4 + [ANY] * (9 + len(saved)),
        out_specs=[ANY] * 14,
        scratch_shapes=scratch,
        input_output_aliases=aliases,
        compiler_params=pltpu.CompilerParams(vmem_limit_bytes=LIMIT),
        cost_estimate=cost(tokens, width * (8 * half + 4 * hidden)),
        name="layer",
    )(index, mods, bqv, bup, bod, x, *weights, *saved)


def mlp_back_kernel(chunks, index_ref, mod_ref, g_in, xs, aos, mos, preo, pret, wuo, wut, wdo, wdt, *rest):
    rest = rest[len(rest) - 20:]
    (mg_out, sums, bus, dis, pgo, pgt, wu, wd, g, mg, x, ao, mo, pre, di, pg, ng, total, bu, sems) = rest

    @pl.when(index_ref[1] == 1)
    def _():
        copies = Copies(sems)
        img = index_ref[0]
        step = pre.shape[2] // chunks
        spots = [(side, slice(place * step, (place + 1) * step)) for side in range(2) for place in range(chunks)]
        pairs = [(g_in, g)]
        for side, spot in spots:
            pre_in, up, down = ((preo, wuo, wdo), (pret, wut, wdt))[side]
            pairs += [(down.at[spot, :], wd.at[side, spot, :]), (pre_in.at[img, :, spot], pre.at[side, :, spot]),
                      (up.at[:, spot], wu.at[side, :, spot])]
        stream = Stream(copies, DEPTH, pairs + [(mos.at[img], mo), (xs.at[img], x), (aos.at[img], ao)])
        mods = mod_ref[img]
        stream.take()
        mg[...] = g[...].astype(F32) * mods[6:7]
        di[...] = (mg[...] * mods[5:6]).astype(BF)
        pending = [copies.start(di, dis.at[img])]
        for number, (side, spot) in enumerate(spots):
            stream.take(2)
            values = pre[side, :, spot].astype(F32)
            grad = nt(di[...], wd[side, spot, :])
            square = values * values
            inner = jnp.tanh(values * (ROOT + ROOT * CUBE * square))
            slope = 0.5 * (1.0 + inner) + 0.5 * values * (1.0 - inner * inner) * (ROOT + 3.0 * ROOT * CUBE * square)
            graded = (grad * slope).astype(BF)
            pg[side, :, spot] = graded
            bu[side : side + 1, spot] = jnp.sum(graded.astype(F32), axis=0, keepdims=True)
            stream.take()
            term = nt(pg[side, :, spot], wu[side, :, spot])
            ng[...] = term if number == 0 else ng[...] + term
            pending.append(copies.start(pg.at[side, :, spot], (pgo, pgt)[side].at[img, :, spot]))
        pending.append(copies.start(bu, bus.at[img]))
        stream.take()
        total[2:3] = jnp.sum(mg[...] * mo[...], axis=0, keepdims=True)
        total[3:4] = jnp.sum(di[...].astype(F32), axis=0, keepdims=True)
        stream.take(2)
        normed, inverse = norm_parts(x[...].astype(F32) + mods[2:3] * ao[...])
        total[0:1] = jnp.sum(ng[...], axis=0, keepdims=True)
        total[1:2] = jnp.sum(ng[...] * normed, axis=0, keepdims=True)
        pending.append(copies.start(total, sums.at[img]))
        dn = ng[...] * (1.0 + mods[4:5])
        mg[...] += inverse * (
            dn - jnp.mean(dn, axis=-1, keepdims=True) - normed * jnp.mean(dn * normed, axis=-1, keepdims=True))
        pending.append(copies.start(mg, mg_out))
        for copy in pending:
            copy.wait()


def mlp_back_call(index, grad, mods, saved, weights, kept, images):
    xs, aos, mos, preo, pret = saved
    tokens, width = grad.shape
    hidden = preo.shape[2]
    chunks = 3 if hidden % 384 == 0 else 1
    sd = jax.ShapeDtypeStruct
    kept = tuple(kept) if kept is not None else ()
    aliases = {12 + i: 1 + i for i in range(len(kept))}
    scratch = [
        pltpu.VMEM((2, width, hidden), BF),
        pltpu.VMEM((2, hidden, width), BF),
        pltpu.VMEM((tokens, width), BF),
        pltpu.VMEM((tokens, width), F32),
        pltpu.VMEM((tokens, width), BF),
        pltpu.VMEM((tokens, width), F32),
        pltpu.VMEM((tokens, width), F32),
        pltpu.VMEM((2, tokens, hidden), BF),
        pltpu.VMEM((tokens, width), BF),
        pltpu.VMEM((2, tokens, hidden), BF),
        pltpu.VMEM((tokens, width), F32),
        pltpu.VMEM((8, width), F32),
        pltpu.VMEM((2, hidden), F32),
        pltpu.SemaphoreType.DMA((48,)),
    ]
    return pl.pallas_call(
        functools.partial(mlp_back_kernel, chunks),
        out_shape=(
            sd((tokens, width), F32), sd((images, 8, width), F32), sd((images, 2, hidden), F32),
            sd((images, tokens, width), BF), sd((images, tokens, hidden), BF), sd((images, tokens, hidden), BF)),
        in_specs=[pl.BlockSpec(memory_space=pltpu.SMEM), VM] + [ANY] * (10 + len(kept)),
        out_specs=[ANY] * 6,
        scratch_shapes=scratch,
        input_output_aliases=aliases,
        compiler_params=pltpu.CompilerParams(vmem_limit_bytes=LIMIT),
        cost_estimate=cost(tokens, 4 * width * hidden),
        name="mlp_back",
    )(index, mods, grad, xs, aos, mos, preo, pret, *weights, *kept)


def attn_back_kernel(index_ref, mod_ref, mg_in, xs, aos, qkvo, qkvt, wqo, wqt, woo, wot, *rest):
    rest = rest[len(rest) - 22:]
    (rg_out, rgs, sums, bqvs, ois, qgo, qgt, wq, wo, mg, rg, x, ao, qkv, oi, qg, da, acc, ng, total, bqv, sems) = rest

    @pl.when(index_ref[1] == 1)
    def _():
        copies = Copies(sems)
        img = index_ref[0]
        stream = Stream(copies, DEPTH, [
            (mg_in, mg), (woo, wo.at[0]), (wot, wo.at[1]), (qkvo.at[img], qkv.at[0]), (qkvt.at[img], qkv.at[1]),
            *three_kinds((wqo, wqt), wq), (aos.at[img], ao), (xs.at[img], x)])
        half = wo.shape[1]
        size = 2 * half // HEADS
        scale = size ** (-0.5)
        mods = mod_ref[img]
        stream.take()
        oi[...] = (mg[...] * mods[2:3]).astype(BF)
        pending = [copies.start(oi, ois.at[img])]
        for side in range(2):
            stream.take()
            da[side] = nt(oi[...], wo[side]).astype(BF)
        stream.take(2)

        def attend(side, carry):
            for kind in range(3):
                acc[kind] = jnp.zeros_like(acc[kind])
            for span in windows(half, size):
                part = slice(span[2], span[3])
                mask = head_mask(span)
                zero = jnp.zeros((), BF)
                queries = jnp.where(mask, qkv[side, 0, :, part], zero)
                keys = jnp.where(mask, qkv[side, 1, :, part], zero)
                outer = jnp.where(mask, da[side, :, part], zero)
                probs = soft(nt(queries, keys), scale)
                grads = nt(outer, qkv[side, 2, :, part])
                inner = jnp.sum(grads * probs, axis=-1, keepdims=True)
                spread = (probs * (grads - inner)).astype(BF)
                acc[2, :, part] += tn(probs.astype(BF), outer)
                acc[0, :, part] += nn(spread, keys)
                acc[1, :, part] += tn(spread, queries)
            for kind in range(3):
                factor = 1.0 if kind == 2 else scale
                qg[side, kind] = (acc[kind] * factor).astype(BF)
            return carry

        lax.fori_loop(0, 2, attend, 0)
        for side, target in enumerate((qgo, qgt)):
            pending += [copies.start(qg.at[side, kind], target.at[kind, img]) for kind in range(3)]
        for part in range(6):
            side, kind = part // 3, part % 3
            stream.take()
            term = nt(qg[side, kind], wq[side, kind])
            ng[...] = term if part == 0 else ng[...] + term
            bqv[part : part + 1] = jnp.sum(qg[side, kind].astype(F32), axis=0, keepdims=True)
        pending.append(copies.start(bqv, bqvs.at[img]))
        stream.take()
        total[2:3] = jnp.sum(mg[...] * ao[...], axis=0, keepdims=True)
        total[3:4] = jnp.sum(oi[...].astype(F32), axis=0, keepdims=True)
        stream.take()
        normed, inverse = norm_parts(x[...].astype(F32))
        total[0:1] = jnp.sum(ng[...], axis=0, keepdims=True)
        total[1:2] = jnp.sum(ng[...] * normed, axis=0, keepdims=True)
        pending.append(copies.start(total, sums.at[img]))
        dn = ng[...] * (1.0 + mods[1:2])
        rg[...] = (mg[...] + inverse * (
            dn - jnp.mean(dn, axis=-1, keepdims=True) - normed * jnp.mean(dn * normed, axis=-1, keepdims=True))).astype(BF)
        pending += [copies.start(rg, rg_out), copies.start(rg, rgs.at[img])]
        for copy in pending:
            copy.wait()


def attn_back_call(index, grad, mods, saved, weights, kept, images):
    xs, aos, qkvo, qkvt = saved
    tokens, width = grad.shape
    half = width // 2
    sd = jax.ShapeDtypeStruct
    kept = tuple(kept) if kept is not None else ()
    aliases = {11 + i: 1 + i for i in range(len(kept))}
    scratch = [
        pltpu.VMEM((2, 3, width, half), BF),
        pltpu.VMEM((2, half, width), BF),
        pltpu.VMEM((tokens, width), F32),
        pltpu.VMEM((tokens, width), BF),
        pltpu.VMEM((tokens, width), BF),
        pltpu.VMEM((tokens, width), F32),
        pltpu.VMEM((2, 3, tokens, half), BF),
        pltpu.VMEM((tokens, width), BF),
        pltpu.VMEM((2, 3, tokens, half), BF),
        pltpu.VMEM((2, tokens, half), BF),
        pltpu.VMEM((3, tokens, half), F32),
        pltpu.VMEM((tokens, width), F32),
        pltpu.VMEM((8, width), F32),
        pltpu.VMEM((8, half), F32),
        pltpu.SemaphoreType.DMA((32,)),
    ]
    return pl.pallas_call(
        attn_back_kernel,
        out_shape=(
            sd((tokens, width), BF), sd((images, tokens, width), BF), sd((images, 8, width), F32),
            sd((images, 8, half), F32), sd((images, tokens, width), BF),
            sd((3, images, tokens, half), BF), sd((3, images, tokens, half), BF)),
        in_specs=[pl.BlockSpec(memory_space=pltpu.SMEM), VM] + [ANY] * (9 + len(kept)),
        out_specs=[ANY] * 7,
        scratch_shapes=scratch,
        input_output_aliases=aliases,
        compiler_params=pltpu.CompilerParams(vmem_limit_bytes=LIMIT),
        cost_estimate=cost(tokens, 8 * width * half),
        name="attn_back",
    )(index, mods, grad, xs, aos, qkvo, qkvt, *weights, *kept)


def time_embed(timesteps, width_all):
    half_width = width_all // 2
    frequencies = jnp.exp(-math.log(10000.0) * jnp.arange(half_width, dtype=F32) / half_width)
    angles = timesteps.astype(F32)[:, None] * frequencies[None, :]
    return jnp.concatenate([jnp.cos(angles), jnp.sin(angles)], axis=1)


def swap(array):
    return lax.ppermute(array, "tensor", [(0, 1), (1, 0)])


def partners():
    peers = lax.axis_size("dp")
    place = lax.axis_index("dp")
    bit = 1
    while bit < peers:
        yield [(i, i ^ bit) for i in range(peers)], (place & bit) == 0
        bit *= 2


def gather_all(array):
    for pairs, is_low in partners():
        came = lax.ppermute(array, "dp", pairs)
        array = jnp.where(is_low, jnp.concatenate([array, came]), jnp.concatenate([came, array]))
    return array


def add_all(array):
    for pairs, _ in partners():
        array = array + lax.ppermute(array, "dp", pairs)
    return array


def ring_order(peers):
    order = list(range(0, peers, 2)) + list(range(1, peers, 2))[::-1]
    place = [order.index(peer) for peer in range(peers)]
    ahead = [(order[i], order[(i + 1) % peers]) for i in range(peers)]
    return place, ahead, [(b, a) for a, b in ahead]


def ring_sum(terms):
    peers = lax.axis_size("dp")
    place, ahead, behind = ring_order(peers)
    here = jnp.asarray(place, jnp.int32)[lax.axis_index("dp")]
    count, width = terms.shape
    part = count // (2 * peers)
    blocks = terms.reshape(2, peers, part, width)
    total = jnp.zeros((2, peers, part, width), F32)
    lanes = ((ahead, 1), (behind, -1))

    def block(side, number):
        return lax.dynamic_slice(blocks, (side, number % peers, 0, 0), (1, 1, part, width))

    moving = [block(side, here) for side in range(2)]
    for step in range(1, peers):
        for side, (pairs, sign) in enumerate(lanes):
            came = lax.ppermute(moving[side], "dp", pairs)
            mine = block(side, here - sign * step)
            moving[side] = (came.astype(F32) + mine.astype(F32)).astype(BF)
    for step in range(peers):
        for side, (pairs, sign) in enumerate(lanes):
            owner = (here - sign * (peers - 1 + step)) % peers
            total = lax.dynamic_update_slice(total, moving[side].astype(F32), (side, owner, 0, 0))
            if step < peers - 1:
                moving[side] = lax.ppermute(moving[side], "dp", pairs)
    return total.reshape(count, width)


def folded(other, own):
    came = swap(other.astype(BF))
    return (own + came.astype(F32)).astype(BF)


def outer(left, right):
    return jnp.einsum("btk,btd->kd", left, right, preferred_element_type=F32)


def outers(left, right):
    return jnp.einsum("jbtk,btd->jkd", left, right, preferred_element_type=F32)


def shards(images_in, timesteps, labels, counts, label_table, ada_weight, ada_bias, qkv_weight,
           qkv_bias, out_weight, out_bias, up_weight, up_bias, down_weight, down_bias, out_cotangent):
    is_first = lax.axis_index("section") == 0
    core = lax.axis_index("tensor")
    slots = images_in.shape[1]
    images = slots // 2
    width = images_in.shape[2]
    hidden = up_weight.shape[2]
    half = out_weight.shape[1]

    def by_section(first_val, later_val):
        return jnp.where(is_first, first_val, later_val)

    def by_core(first_val, later_val):
        return jnp.where(core == 0, first_val, later_val)

    def mine(array, axis):
        return lax.dynamic_slice_in_dim(array, core * images, images, axis)

    def others(array, axis):
        return lax.dynamic_slice_in_dim(array, (1 - core) * images, images, axis)

    def in_order(own, came, axis):
        return by_core(jnp.concatenate([own, came], axis), jnp.concatenate([came, own], axis))

    def whole_images(rows):
        came = swap(others(rows, 1))
        return jnp.moveaxis(jnp.concatenate([mine(rows, 1), came], axis=0), 1, 0)

    def split_images(rows):
        local = rows.shape[1] // 2
        came = swap(rows[:, local:])
        return jnp.moveaxis(in_order(rows[:, :local], came, 0), 0, 1)[None]

    qkv_own = lax.optimization_barrier(jnp.moveaxis(qkv_weight[0], 1, 0))
    w_qkv = (qkv_own, swap(qkv_own))
    w_out = (out_weight[0], swap(out_weight[0]))
    w_up = (up_weight[0], swap(up_weight[0]))
    w_down = (down_weight[0], swap(down_weight[0]))
    weights = (*w_qkv, *w_out, *w_up, *w_down)

    condition = jnp.take(label_table, labels, axis=0).astype(F32) + time_embed(timesteps, width)
    silu_cond, silu_back = jax.vjp(jax.nn.silu, condition)
    silu_b = silu_cond.astype(BF)
    mod_local = (
        jnp.dot(silu_b, ada_weight[0], preferred_element_type=F32) + ada_bias[0].astype(F32)[None]
    )
    modulation = in_order(mine(mod_local, 0), swap(others(mod_local, 0)), 1).reshape(images, 6, width)
    slot_no = core * images + jnp.arange(images, dtype=jnp.int32)
    valid = (slot_no < counts[0]).astype(F32)
    mods = jnp.concatenate(
        [modulation, jnp.broadcast_to(valid[:, None, None], (images, 2, width))], axis=1
    )
    pair_bias = jnp.concatenate([qkv_bias[0, 0], qkv_bias[0, 1], up_bias[0]])[None]
    pair_bias = jnp.concatenate([pair_bias, swap(pair_bias)], axis=0).astype(F32)
    zero_row = jnp.zeros((half,), F32)
    bqv = jnp.stack([
        pair_bias[0, :half], zero_row, pair_bias[0, half : 2 * half],
        pair_bias[1, :half], zero_row, pair_bias[1, half : 2 * half], zero_row, zero_row])
    bup = pair_bias[:, 2 * half :]
    bod = jnp.concatenate([out_bias, down_bias], axis=0).astype(F32)

    rows_in = whole_images(images_in)
    cotangent = whole_images(out_cotangent)

    def turn_index(number, is_active):
        return jnp.stack([jnp.int32(number), is_active.astype(jnp.int32)])

    inputs, saved = [rows_in[i] for i in range(images)], None
    for turn in range(2 * images):
        number, is_early = turn % images, turn < images
        answer = layer_call(
            turn_index(number, is_first == is_early), inputs[turn], mods, bqv, bup, bod, weights, saved, images
        )
        saved = answer[1:]
        if is_early:
            inputs.append(lax.ppermute(answer[0], "section", [(0, 1)]))
    ys, xs, h1s, qkvo, qkvt, atts, aos, h2s, preo, pret, acto, actt, mos = saved
    layer_out = split_images(ys)

    inputs, mlp_kept, attn_kept = [cotangent[i] for i in range(images)], None, None
    for turn in range(2 * images):
        number, is_early = turn % images, turn < images
        index = turn_index(number, is_first != is_early)
        answer = mlp_back_call(
            index, inputs[turn], mods, (xs, aos, mos, preo, pret), (*w_up, *w_down), mlp_kept, images
        )
        middle_grad, mlp_kept = answer[0], answer[1:]
        answer = attn_back_call(
            index, middle_grad, mods, (xs, aos, qkvo, qkvt), (*w_qkv, *w_out), attn_kept, images
        )
        attn_kept = answer[1:]
        if is_early:
            inputs.append(lax.ppermute(answer[0], "section", [(1, 0)]))
    mlp_sums, up_sums, down_ins, pre_grads_o, pre_grads_t = mlp_kept
    row_grads, attn_sums, qkv_sums, out_ins, qkv_grads_o, qkv_grads_t = attn_kept
    in_grad = split_images(row_grads)

    down_w = folded(outer(actt, down_ins), outer(acto, down_ins))
    up_w = folded(outer(h2s, pre_grads_t), outer(h2s, pre_grads_o))
    stacked = 3 * half
    attn_w = folded(
        jnp.concatenate([outers(qkv_grads_t, h1s).reshape(stacked, width), outer(atts[:, 1], out_ins)]),
        jnp.concatenate([outers(qkv_grads_o, h1s).reshape(stacked, width), outer(atts[:, 0], out_ins)]),
    )
    down_w_sum, up_w_sum, attn_w_sum = ring_sum(down_w), ring_sum(up_w), ring_sum(attn_w)
    qkv_w_sum = jnp.moveaxis(attn_w_sum[:stacked].reshape(3, half, width), 2, 0)
    out_w_sum = attn_w_sum[stacked:]

    mod_grad = jnp.concatenate([attn_sums[:, :3], mlp_sums[:, :3]], axis=1).astype(BF)
    columns = mod_grad.reshape(images, 2, 3 * width)
    own_cols = lax.dynamic_index_in_dim(columns, core, 1, keepdims=False)
    other_cols = lax.dynamic_index_in_dim(columns, 1 - core, 1, keepdims=False)
    mod_cols = in_order(own_cols, swap(other_cols), 0)
    silu_grad = jnp.einsum("sk,dk->sd", mod_cols, ada_weight[0], preferred_element_type=F32)
    silu_grad = silu_grad + swap(silu_grad)
    silu_grad = silu_grad + lax.ppermute(silu_grad, "section", [(0, 1), (1, 0)])
    cond_grad = silu_back(silu_grad)[0]

    silu_all = gather_all(silu_b)
    mod_all = gather_all(mod_cols)
    kept_rows = jnp.concatenate([cond_grad.reshape(1, -1), labels.astype(F32)[None]], axis=1)
    gathered = gather_all(kept_rows)
    cond_all = gathered[:, : slots * width].reshape(-1, width)
    labels_all = gathered[:, slots * width :].reshape(-1)
    ada_w_sum = jnp.einsum("sd,sk->dk", silu_all, mod_all, preferred_element_type=F32)
    ada_b_sum = jnp.sum(mod_all, axis=0, dtype=F32)
    onehot = (labels_all[None] == jnp.arange(label_table.shape[0], dtype=F32)[:, None]).astype(F32)
    table_grad = jnp.dot(onehot, cond_all, precision=lax.Precision.HIGHEST, preferred_element_type=F32)

    qkv_total, up_total = jnp.sum(qkv_sums, axis=0), jnp.sum(up_sums, axis=0)
    own_bias = jnp.concatenate([qkv_total[0], qkv_total[2], up_total[0]])
    other_bias = jnp.concatenate([qkv_total[3], qkv_total[5], up_total[1]])
    both_bias = jnp.concatenate([jnp.sum(attn_sums[:, 3], axis=0), jnp.sum(mlp_sums[:, 3], axis=0)])
    came_bias = swap(jnp.concatenate([other_bias, both_bias]))
    biases = add_all(jnp.concatenate([own_bias, both_bias]) + came_bias)
    qkv_b_sum = biases[: 2 * half].reshape(2, half)
    up_b_sum = biases[2 * half : 2 * half + hidden]
    out_b_sum = biases[2 * half + hidden : 2 * half + hidden + width]
    down_b_sum = biases[2 * half + hidden + width :]
    return (
        layer_out,
        in_grad,
        cond_grad,
        table_grad,
        ada_w_sum[None],
        ada_b_sum[None],
        qkv_w_sum[None],
        qkv_b_sum[None],
        out_w_sum[None],
        out_b_sum[None],
        up_w_sum[None],
        up_b_sum[None],
        down_w_sum[None],
        down_b_sum[None],
    )


def solution(mesh):
    placed = (
        P("tensor", "dp", None),
        P("dp"),
        P("dp"),
        P("dp"),
        P(),
        P("section", None, "tensor"),
        P("section", "tensor"),
        P("section", None, None, "tensor"),
        P("section", None, "tensor"),
        P("section", "tensor", None),
        P("section", None),
        P("section", None, "tensor"),
        P("section", "tensor"),
        P("section", "tensor", None),
        P("section", None),
        P("tensor", "dp", None),
    )
    return jax.shard_map(
        shards,
        mesh=mesh,
        in_specs=placed,
        out_specs=(
            P("section", "tensor", "dp", None),
            P("section", "tensor", "dp", None),
            P("dp", None),
            P(),
            P("section", None, "tensor"),
            P("section", "tensor"),
            P("section", None, None, "tensor"),
            P("section", None, "tensor"),
            P("section", "tensor", None),
            P("section", None),
            P("section", None, "tensor"),
            P("section", "tensor"),
            P("section", "tensor", None),
            P("section", None),
        ),
        check_vma=False,
    )
```

```python
import functools
import math
import jax
import jax.numpy as jnp
from jax import lax
from jax.experimental import pallas as pl
from jax.experimental.pallas import tpu as pltpu
from jax.sharding import PartitionSpec as P

HEADS = 16
eps_norm = 1e-06
BF, F32 = jnp.bfloat16, jnp.float32
ANY = pl.BlockSpec(memory_space=pl.ANY)
VM = pl.BlockSpec(memory_space=pltpu.VMEM)
LIMIT = 60 * 1024 * 1024
DEPTH = 4
ROOT = math.sqrt(2.0 / math.pi)
CUBE = 0.044715


def nt(left, right):
    return lax.dot_general(left, right, (((1,), (1,)), ((), ())), preferred_element_type=F32)


def tn(left, right):
    return lax.dot_general(left, right, (((0,), (0,)), ((), ())), preferred_element_type=F32)


def nn(left, right):
    return jnp.dot(left, right, preferred_element_type=F32)


def norm_parts(rows):
    centered = rows - jnp.mean(rows, axis=-1, keepdims=True)
    inverse = lax.rsqrt(jnp.mean(centered * centered, axis=-1, keepdims=True) + eps_norm)
    return centered * inverse, inverse


def windows(width, size):
    spans = []
    for head in range(width // size):
        low, high = head * size, (head + 1) * size
        spans.append((low, high, low // 128 * 128, min(width, (high + 127) // 128 * 128)))
    return spans


def head_mask(span):
    low, high, start, stop = span
    lanes = lax.broadcasted_iota(jnp.int32, (1, stop - start), 1) + start
    return (lanes >= low) & (lanes < high)


class Copies:
    def __init__(self, sems):
        self.sems, self.used = sems, 0

    def start(self, source, target):
        copy = pltpu.make_async_copy(source, target, self.sems.at[self.used])
        self.used += 1
        copy.start()
        return copy


class Stream:
    def __init__(self, copies, depth, pairs):
        self.copies, self.depth, self.pairs, self.begun, self.taken = copies, depth, pairs, [], 0
        self.fill()

    def fill(self):
        while len(self.begun) < min(len(self.pairs), self.taken + self.depth):
            self.begun.append(self.copies.start(*self.pairs[len(self.begun)]))

    def take(self, count=1):
        for _ in range(count):
            self.begun[self.taken].wait()
            self.taken += 1
            self.fill()


def three_kinds(sources, target):
    return [(source.at[kind], target.at[side, kind]) for side, source in enumerate(sources) for kind in range(3)]


def soft(scores, scale):
    top = jnp.max(scores, axis=-1, keepdims=True)
    powers = jnp.exp2((scores - top) * (scale * math.log2(math.e)))
    return powers * (1.0 / jnp.sum(powers, axis=-1, keepdims=True))


def layer_kernel(chunks, index_ref, mod_ref, bqv_ref, bup_ref, bod_ref, x_in,
                 *rest):
    wqs, (woo, wot, wuo, wut, wdo, wdt) = rest[:2], rest[2:8]
    rest = rest[len(rest) - 30:]
    (y_out, ys, xs, h1s, qkvo, qkvt, atts, aos, h2s, preo, pret, acto, actt, mos,
     wq, wo, wu, wd, x, y, h1, qkv, att, attf, ao, h2, pre, act, mo, sems) = rest

    @pl.when(index_ref[1] == 1)
    def _():
        copies = Copies(sems)
        img = index_ref[0]
        step = wu.shape[2] // chunks
        spots = [(side, slice(place * step, (place + 1) * step)) for side in range(2) for place in range(chunks)]
        pairs = [(x_in, x), *three_kinds(wqs, wq), (woo, wo.at[0]), (wot, wo.at[1])]
        for side, spot in spots:
            up, down = ((wuo, wdo), (wut, wdt))[side]
            pairs += [(up.at[:, spot], wu.at[side, :, spot]), (down.at[spot, :], wd.at[side, spot, :])]
        stream = Stream(copies, DEPTH, pairs)
        half = att.shape[2]
        size = 2 * half // HEADS
        scale = size ** (-0.5)
        mods = mod_ref[img]
        stream.take()
        pending = [copies.start(x, xs.at[img])]
        normed, _ = norm_parts(x[...].astype(F32))
        h1[...] = (normed * (1.0 + mods[1:2]) + mods[0:1]).astype(BF)
        pending.append(copies.start(h1, h1s.at[img]))
        for part in range(6):
            side, kind = part // 3, part % 3
            stream.take()
            mixed = nt(h1[...], wq[side, kind])
            qkv[side, kind] = (mixed + bqv_ref[part : part + 1]).astype(BF)
        pending += [copies.start(qkv.at[0], qkvo.at[img]), copies.start(qkv.at[1], qkvt.at[img])]

        def attend(side, carry):
            attf[...] = jnp.zeros_like(attf)
            for span in windows(half, size):
                part = slice(span[2], span[3])
                mask = head_mask(span)
                zero = jnp.zeros((), BF)
                queries = jnp.where(mask, qkv[side, 0, :, part], zero)
                scores = nt(queries, qkv[side, 1, :, part])
                probs = soft(scores, scale).astype(BF)
                attf[:, part] += nn(probs, jnp.where(mask, qkv[side, 2, :, part], zero))
            att[side] = attf[...].astype(BF)
            return carry

        lax.fori_loop(0, 2, attend, 0)
        pending.append(copies.start(att, atts.at[img]))
        stream.take(2)
        ao[...] = nn(att[0], wo[0]) + nn(att[1], wo[1]) + bod_ref[0:1]
        pending.append(copies.start(ao, aos.at[img]))
        normed, _ = norm_parts(x[...].astype(F32) + mods[2:3] * ao[...])
        h2[...] = (normed * (1.0 + mods[4:5]) + mods[3:4]).astype(BF)
        pending.append(copies.start(h2, h2s.at[img]))
        for number, (side, spot) in enumerate(spots):
            stream.take()
            values = nn(h2[...], wu[side, :, spot]) + bup_ref[side : side + 1, spot]
            pre[side, :, spot] = values.astype(BF)
            inner = jnp.tanh(values * (ROOT + ROOT * CUBE * values * values))
            act[side, :, spot] = (0.5 * values * (1.0 + inner)).astype(BF)
            stream.take()
            term = nn(act[side, :, spot], wd[side, spot, :])
            mo[...] = term + (bod_ref[1:2] if number == 0 else mo[...])
            pre_out, act_out = ((preo, acto), (pret, actt))[side]
            pending += [copies.start(pre.at[side, :, spot], pre_out.at[img, :, spot]),
                        copies.start(act.at[side, :, spot], act_out.at[img, :, spot])]
        pending.append(copies.start(mo, mos.at[img]))
        y[...] = (mods[6:7] * (x[...].astype(F32) + mods[2:3] * ao[...] + mods[5:6] * mo[...])).astype(BF)
        pending += [copies.start(y, y_out), copies.start(y, ys.at[img])]
        for copy in pending:
            copy.wait()


def cost(tokens, weight_count):
    return pl.CostEstimate(
        flops=2 * tokens * weight_count, bytes_accessed=2 * weight_count, transcendentals=0)


def layer_call(index, x, mods, bqv, bup, bod, weights, saved, images):
    tokens, width = x.shape
    half, hidden = width // 2, bup.shape[1]
    chunks = 3 if hidden % 384 == 0 else 1
    sd = jax.ShapeDtypeStruct
    outs = (
        sd((tokens, width), BF),
        sd((images, tokens, width), BF),
        sd((images, tokens, width), BF),
        sd((images, tokens, width), BF),
        sd((images, 3, tokens, half), BF),
        sd((images, 3, tokens, half), BF),
        sd((images, 2, tokens, half), BF),
        sd((images, tokens, width), F32),
        sd((images, tokens, width), BF),
        sd((images, tokens, hidden), BF),
        sd((images, tokens, hidden), BF),
        sd((images, tokens, hidden), BF),
        sd((images, tokens, hidden), BF),
        sd((images, tokens, width), F32),
    )
    saved = tuple(saved) if saved is not None else ()
    aliases = {14 + i: 1 + i for i in range(len(saved))}
    scratch = [
        pltpu.VMEM((2, 3, half, width), BF),
        pltpu.VMEM((2, half, width), BF),
        pltpu.VMEM((2, width, hidden), BF),
        pltpu.VMEM((2, hidden, width), BF),
        pltpu.VMEM((tokens, width), BF),
        pltpu.VMEM((tokens, width), BF),
        pltpu.VMEM((tokens, width), BF),
        pltpu.VMEM((2, 3, tokens, half), BF),
        pltpu.VMEM((2, tokens, half), BF),
        pltpu.VMEM((tokens, half), F32),
        pltpu.VMEM((tokens, width), F32),
        pltpu.VMEM((tokens, width), BF),
        pltpu.VMEM((2, tokens, hidden), BF),
        pltpu.VMEM((2, tokens, hidden), BF),
        pltpu.VMEM((tokens, width), F32),
        pltpu.SemaphoreType.DMA((64,)),
    ]
    return pl.pallas_call(
        functools.partial(layer_kernel, chunks),
        out_shape=outs,
        in_specs=[pl.BlockSpec(memory_space=pltpu.SMEM)] + [VM] * 4 + [ANY] * (9 + len(saved)),
        out_specs=[ANY] * 14,
        scratch_shapes=scratch,
        input_output_aliases=aliases,
        compiler_params=pltpu.CompilerParams(vmem_limit_bytes=LIMIT),
        cost_estimate=cost(tokens, width * (8 * half + 4 * hidden)),
        name="layer",
    )(index, mods, bqv, bup, bod, x, *weights, *saved)


def mlp_back_kernel(chunks, index_ref, mod_ref, g_in, xs, aos, mos, preo, pret, wuo, wut, wdo, wdt, *rest):
    rest = rest[len(rest) - 20:]
    (mg_out, sums, bus, dis, pgo, pgt, wu, wd, g, mg, x, ao, mo, pre, di, pg, ng, total, bu, sems) = rest

    @pl.when(index_ref[1] == 1)
    def _():
        copies = Copies(sems)
        img = index_ref[0]
        step = pre.shape[2] // chunks
        spots = [(side, slice(place * step, (place + 1) * step)) for side in range(2) for place in range(chunks)]
        pairs = [(g_in, g)]
        for side, spot in spots:
            pre_in, up, down = ((preo, wuo, wdo), (pret, wut, wdt))[side]
            pairs += [(down.at[spot, :], wd.at[side, spot, :]), (pre_in.at[img, :, spot], pre.at[side, :, spot]),
                      (up.at[:, spot], wu.at[side, :, spot])]
        stream = Stream(copies, DEPTH, pairs + [(mos.at[img], mo), (xs.at[img], x), (aos.at[img], ao)])
        mods = mod_ref[img]
        stream.take()
        mg[...] = g[...].astype(F32) * mods[6:7]
        di[...] = (mg[...] * mods[5:6]).astype(BF)
        pending = [copies.start(di, dis.at[img])]
        for number, (side, spot) in enumerate(spots):
            stream.take(2)
            values = pre[side, :, spot].astype(F32)
            grad = nt(di[...], wd[side, spot, :])
            square = values * values
            inner = jnp.tanh(values * (ROOT + ROOT * CUBE * square))
            slope = 0.5 * (1.0 + inner) + 0.5 * values * (1.0 - inner * inner) * (ROOT + 3.0 * ROOT * CUBE * square)
            graded = (grad * slope).astype(BF)
            pg[side, :, spot] = graded
            bu[side : side + 1, spot] = jnp.sum(graded.astype(F32), axis=0, keepdims=True)
            stream.take()
            term = nt(pg[side, :, spot], wu[side, :, spot])
            ng[...] = term if number == 0 else ng[...] + term
            pending.append(copies.start(pg.at[side, :, spot], (pgo, pgt)[side].at[img, :, spot]))
        pending.append(copies.start(bu, bus.at[img]))
        stream.take()
        total[2:3] = jnp.sum(mg[...] * mo[...], axis=0, keepdims=True)
        total[3:4] = jnp.sum(di[...].astype(F32), axis=0, keepdims=True)
        stream.take(2)
        normed, inverse = norm_parts(x[...].astype(F32) + mods[2:3] * ao[...])
        total[0:1] = jnp.sum(ng[...], axis=0, keepdims=True)
        total[1:2] = jnp.sum(ng[...] * normed, axis=0, keepdims=True)
        pending.append(copies.start(total, sums.at[img]))
        dn = ng[...] * (1.0 + mods[4:5])
        mg[...] += inverse * (
            dn - jnp.mean(dn, axis=-1, keepdims=True) - normed * jnp.mean(dn * normed, axis=-1, keepdims=True))
        pending.append(copies.start(mg, mg_out))
        for copy in pending:
            copy.wait()


def mlp_back_call(index, grad, mods, saved, weights, kept, images):
    xs, aos, mos, preo, pret = saved
    tokens, width = grad.shape
    hidden = preo.shape[2]
    chunks = 3 if hidden % 384 == 0 else 1
    sd = jax.ShapeDtypeStruct
    kept = tuple(kept) if kept is not None else ()
    aliases = {12 + i: 1 + i for i in range(len(kept))}
    scratch = [
        pltpu.VMEM((2, width, hidden), BF),
        pltpu.VMEM((2, hidden, width), BF),
        pltpu.VMEM((tokens, width), BF),
        pltpu.VMEM((tokens, width), F32),
        pltpu.VMEM((tokens, width), BF),
        pltpu.VMEM((tokens, width), F32),
        pltpu.VMEM((tokens, width), F32),
        pltpu.VMEM((2, tokens, hidden), BF),
        pltpu.VMEM((tokens, width), BF),
        pltpu.VMEM((2, tokens, hidden), BF),
        pltpu.VMEM((tokens, width), F32),
        pltpu.VMEM((8, width), F32),
        pltpu.VMEM((2, hidden), F32),
        pltpu.SemaphoreType.DMA((48,)),
    ]
    return pl.pallas_call(
        functools.partial(mlp_back_kernel, chunks),
        out_shape=(
            sd((tokens, width), F32), sd((images, 8, width), F32), sd((images, 2, hidden), F32),
            sd((images, tokens, width), BF), sd((images, tokens, hidden), BF), sd((images, tokens, hidden), BF)),
        in_specs=[pl.BlockSpec(memory_space=pltpu.SMEM), VM] + [ANY] * (10 + len(kept)),
        out_specs=[ANY] * 6,
        scratch_shapes=scratch,
        input_output_aliases=aliases,
        compiler_params=pltpu.CompilerParams(vmem_limit_bytes=LIMIT),
        cost_estimate=cost(tokens, 4 * width * hidden),
        name="mlp_back",
    )(index, mods, grad, xs, aos, mos, preo, pret, *weights, *kept)


def attn_back_kernel(index_ref, mod_ref, mg_in, xs, aos, qkvo, qkvt, *rest):
    wqs, (woo, wot) = rest[:2], rest[2:4]
    rest = rest[len(rest) - 22:]
    (rg_out, rgs, sums, bqvs, ois, qgo, qgt, wq, wo, mg, rg, x, ao, qkv, oi, qg, da, acc, ng, total, bqv, sems) = rest

    @pl.when(index_ref[1] == 1)
    def _():
        copies = Copies(sems)
        img = index_ref[0]
        stream = Stream(copies, DEPTH, [
            (mg_in, mg), (woo, wo.at[0]), (wot, wo.at[1]), (qkvo.at[img], qkv.at[0]), (qkvt.at[img], qkv.at[1]),
            *three_kinds(wqs, wq), (aos.at[img], ao), (xs.at[img], x)])
        half = wo.shape[1]
        size = 2 * half // HEADS
        scale = size ** (-0.5)
        mods = mod_ref[img]
        stream.take()
        oi[...] = (mg[...] * mods[2:3]).astype(BF)
        pending = [copies.start(oi, ois.at[img])]
        for side in range(2):
            stream.take()
            da[side] = nt(oi[...], wo[side]).astype(BF)
        stream.take(2)

        def attend(side, carry):
            for kind in range(3):
                acc[kind] = jnp.zeros_like(acc[kind])
            for span in windows(half, size):
                part = slice(span[2], span[3])
                mask = head_mask(span)
                zero = jnp.zeros((), BF)
                queries = jnp.where(mask, qkv[side, 0, :, part], zero)
                keys = jnp.where(mask, qkv[side, 1, :, part], zero)
                outer = jnp.where(mask, da[side, :, part], zero)
                probs = soft(nt(queries, keys), scale)
                grads = nt(outer, qkv[side, 2, :, part])
                inner = jnp.sum(grads * probs, axis=-1, keepdims=True)
                spread = (probs * (grads - inner)).astype(BF)
                acc[2, :, part] += tn(probs.astype(BF), outer)
                acc[0, :, part] += nn(spread, keys)
                acc[1, :, part] += tn(spread, queries)
            for kind in range(3):
                factor = 1.0 if kind == 2 else scale
                qg[side, kind] = (acc[kind] * factor).astype(BF)
            return carry

        lax.fori_loop(0, 2, attend, 0)
        for side, target in enumerate((qgo, qgt)):
            pending += [copies.start(qg.at[side, kind], target.at[kind, img]) for kind in range(3)]
        for part in range(6):
            side, kind = part // 3, part % 3
            stream.take()
            term = nn(qg[side, kind], wq[side, kind])
            ng[...] = term if part == 0 else ng[...] + term
            bqv[part : part + 1] = jnp.sum(qg[side, kind].astype(F32), axis=0, keepdims=True)
        pending.append(copies.start(bqv, bqvs.at[img]))
        stream.take()
        total[2:3] = jnp.sum(mg[...] * ao[...], axis=0, keepdims=True)
        total[3:4] = jnp.sum(oi[...].astype(F32), axis=0, keepdims=True)
        stream.take()
        normed, inverse = norm_parts(x[...].astype(F32))
        total[0:1] = jnp.sum(ng[...], axis=0, keepdims=True)
        total[1:2] = jnp.sum(ng[...] * normed, axis=0, keepdims=True)
        pending.append(copies.start(total, sums.at[img]))
        dn = ng[...] * (1.0 + mods[1:2])
        rg[...] = (mg[...] + inverse * (
            dn - jnp.mean(dn, axis=-1, keepdims=True) - normed * jnp.mean(dn * normed, axis=-1, keepdims=True))).astype(BF)
        pending += [copies.start(rg, rg_out), copies.start(rg, rgs.at[img])]
        for copy in pending:
            copy.wait()


def attn_back_call(index, grad, mods, saved, weights, kept, images):
    xs, aos, qkvo, qkvt = saved
    tokens, width = grad.shape
    half = width // 2
    sd = jax.ShapeDtypeStruct
    kept = tuple(kept) if kept is not None else ()
    aliases = {11 + i: 1 + i for i in range(len(kept))}
    scratch = [
        pltpu.VMEM((2, 3, half, width), BF),
        pltpu.VMEM((2, half, width), BF),
        pltpu.VMEM((tokens, width), F32),
        pltpu.VMEM((tokens, width), BF),
        pltpu.VMEM((tokens, width), BF),
        pltpu.VMEM((tokens, width), F32),
        pltpu.VMEM((2, 3, tokens, half), BF),
        pltpu.VMEM((tokens, width), BF),
        pltpu.VMEM((2, 3, tokens, half), BF),
        pltpu.VMEM((2, tokens, half), BF),
        pltpu.VMEM((3, tokens, half), F32),
        pltpu.VMEM((tokens, width), F32),
        pltpu.VMEM((8, width), F32),
        pltpu.VMEM((8, half), F32),
        pltpu.SemaphoreType.DMA((32,)),
    ]
    return pl.pallas_call(
        attn_back_kernel,
        out_shape=(
            sd((tokens, width), BF), sd((images, tokens, width), BF), sd((images, 8, width), F32),
            sd((images, 8, half), F32), sd((images, tokens, width), BF),
            sd((3, images, tokens, half), BF), sd((3, images, tokens, half), BF)),
        in_specs=[pl.BlockSpec(memory_space=pltpu.SMEM), VM] + [ANY] * (9 + len(kept)),
        out_specs=[ANY] * 7,
        scratch_shapes=scratch,
        input_output_aliases=aliases,
        compiler_params=pltpu.CompilerParams(vmem_limit_bytes=LIMIT),
        cost_estimate=cost(tokens, 8 * width * half),
        name="attn_back",
    )(index, mods, grad, xs, aos, qkvo, qkvt, *weights, *kept)


def time_embed(timesteps, width_all):
    half_width = width_all // 2
    frequencies = jnp.exp(-math.log(10000.0) * jnp.arange(half_width, dtype=F32) / half_width)
    angles = timesteps.astype(F32)[:, None] * frequencies[None, :]
    return jnp.concatenate([jnp.cos(angles), jnp.sin(angles)], axis=1)


def swap(array):
    return lax.ppermute(array, "tensor", [(0, 1), (1, 0)])


def partners():
    peers = lax.axis_size("dp")
    place = lax.axis_index("dp")
    bit = 1
    while bit < peers:
        yield [(i, i ^ bit) for i in range(peers)], (place & bit) == 0
        bit *= 2


def gather_all(array):
    for pairs, is_low in partners():
        came = lax.ppermute(array, "dp", pairs)
        array = jnp.where(is_low, jnp.concatenate([array, came]), jnp.concatenate([came, array]))
    return array


def add_all(array):
    for pairs, _ in partners():
        array = array + lax.ppermute(array, "dp", pairs)
    return array


def ring_pairs(peers):
    order = list(range(0, peers, 2)) + list(range(1, peers, 2))[::-1]
    ahead = [(order[i], order[(i + 1) % peers]) for i in range(peers)]
    return ahead, [(b, a) for a, b in ahead]


def ring_spots():
    peers = lax.axis_size("dp")
    device = lax.axis_index("dp").astype(jnp.uint32)
    here = jnp.where(device % 2 == 0, device // 2, peers - 1 - device // 2)
    return [(here + step) & jnp.uint32(peers - 1) for step in range(peers)]


def ring_sum(terms, spots, totals, write):
    peers = len(spots)
    count, width = terms.shape
    part = count // (2 * peers)
    blocks = terms.reshape(2, peers, part, width)
    lanes = tuple(zip(ring_pairs(peers), (1, -1)))
    none = jnp.uint32(0)

    def block(side, step):
        start = (jnp.uint32(side), spots[step % peers], none, none)
        return lax.dynamic_slice(blocks, start, (1, 1, part, width))[0]

    moving = [block(side, 0) for side in range(2)]
    for step in range(1, peers):
        for side, (pairs, sign) in enumerate(lanes):
            came = lax.ppermute(moving[side], "dp", pairs)
            mine = block(side, -sign * step)
            moving[side] = (came.astype(F32) + mine.astype(F32)).astype(BF)
    for step in range(peers):
        for side, (pairs, sign) in enumerate(lanes):
            spot = spots[-sign * (peers - 1 + step) % peers]
            totals = write(totals, side, spot, moving[side].astype(F32))
            if step < peers - 1:
                moving[side] = lax.ppermute(moving[side], "dp", pairs)
    return totals


def put(total, block, spot):
    none = jnp.uint32(0)
    return lax.dynamic_update_slice(total, block, (spot, none, none))


def put_if(total, block, spot, keep):
    none = jnp.uint32(0)
    old = lax.dynamic_slice(total, (spot, none, none), block.shape)
    return put(total, jnp.where(keep, block, old), spot)


def ring_plain(terms, spots):
    peers = len(spots)
    count, width = terms.shape

    def write(total, side, spot, block):
        return put(total, block, spot + jnp.uint32(side * peers))

    total = jnp.zeros((2 * peers, count // (2 * peers), width), F32)
    return ring_sum(terms, spots, total, write).reshape(count, width)


def ring_attn(terms, spots):
    peers = len(spots)
    count, width = terms.shape
    part, quarter = count // (2 * peers), jnp.uint32(peers // 2)

    def write(totals, side, spot, block):
        qkv, out = totals
        if side == 0:
            return put(qkv, block, spot), out
        early = spot < quarter
        qkv = put_if(qkv, block, jnp.uint32(peers) + jnp.minimum(spot, quarter - 1), early)
        return qkv, put_if(out, block, jnp.maximum(spot, quarter) - quarter, ~early)

    totals = (jnp.zeros((3 * peers // 2, part, width), F32), jnp.zeros((peers // 2, part, width), F32))
    qkv, out = ring_sum(terms, spots, totals, write)
    return qkv.reshape(3, count // 4, width), out.reshape(count // 4, width)


def folded(other, own):
    came = swap(other.astype(BF))
    return (own + came.astype(F32)).astype(BF)


def outer(left, right):
    return jnp.einsum("btk,btd->kd", left, right, preferred_element_type=F32)


def outers(left, right):
    return jnp.einsum("jbtk,btd->jkd", left, right, preferred_element_type=F32)


def shards(images_in, timesteps, labels, counts, label_table, ada_weight, ada_bias, qkv_weight,
           qkv_bias, out_weight, out_bias, up_weight, up_bias, down_weight, down_bias, out_cotangent):
    is_first = lax.axis_index("section") == 0
    core = lax.axis_index("tensor")
    slots = images_in.shape[1]
    images = slots // 2
    width = images_in.shape[2]
    hidden = up_weight.shape[2]
    half = out_weight.shape[1]

    def by_section(first_val, later_val):
        return jnp.where(is_first, first_val, later_val)

    def by_core(first_val, later_val):
        return jnp.where(core == 0, first_val, later_val)

    def in_order(own, came, axis):
        return by_core(jnp.concatenate([own, came], axis), jnp.concatenate([came, own], axis))

    def whole_images(rows):
        for i in range(images):
            early, later = rows[:, i], rows[:, images + i]
            yield jnp.concatenate([by_core(early, later), swap(by_core(later, early))], axis=0)

    def split_images(rows):
        local = rows.shape[1] // 2
        came = swap(rows[:, local:])
        return jnp.moveaxis(in_order(rows[:, :local], came, 0), 0, 1)[None]

    qkv_own = jnp.transpose(qkv_weight[0], (1, 2, 0))
    w_qkv = (qkv_own, swap(qkv_own))
    w_out = (out_weight[0], swap(out_weight[0]))
    w_up = (up_weight[0], swap(up_weight[0]))
    w_down = (down_weight[0], swap(down_weight[0]))
    weights = (*w_qkv, *w_out, *w_up, *w_down)

    condition = jnp.take(label_table, labels, axis=0).astype(F32) + time_embed(timesteps, width)
    silu_cond, silu_back = jax.vjp(jax.nn.silu, condition)
    silu_b = silu_cond.astype(BF)
    mod_local = (
        jnp.dot(silu_b, ada_weight[0], preferred_element_type=F32) + ada_bias[0].astype(F32)[None]
    )
    early, later = mod_local[:images], mod_local[images:]
    modulation = in_order(by_core(early, later), swap(by_core(later, early)), 1).reshape(images, 6, width)
    slot_no = core * images + jnp.arange(images, dtype=jnp.int32)
    valid = (slot_no < counts[0]).astype(F32)
    mods = jnp.concatenate(
        [modulation, jnp.broadcast_to(valid[:, None, None], (images, 2, width))], axis=1
    )
    pair_bias = jnp.concatenate([qkv_bias[0, 0], qkv_bias[0, 1], up_bias[0]])[None]
    pair_bias = jnp.concatenate([pair_bias, swap(pair_bias)], axis=0).astype(F32)
    zero_row = jnp.zeros((half,), F32)
    bqv = jnp.stack([
        pair_bias[0, :half], zero_row, pair_bias[0, half : 2 * half],
        pair_bias[1, :half], zero_row, pair_bias[1, half : 2 * half], zero_row, zero_row])
    bup = pair_bias[:, 2 * half :]
    bod = jnp.concatenate([out_bias, down_bias], axis=0).astype(F32)

    rows_in = list(whole_images(images_in))
    cotangent = list(whole_images(out_cotangent))

    def turn_index(number, is_active):
        return jnp.stack([jnp.int32(number), is_active.astype(jnp.int32)])

    inputs, saved = list(rows_in), None
    for turn in range(2 * images):
        number, is_early = turn % images, turn < images
        answer = layer_call(
            turn_index(number, is_first == is_early), inputs[turn], mods, bqv, bup, bod, weights, saved, images
        )
        saved = answer[1:]
        if is_early:
            inputs.append(lax.ppermute(answer[0], "section", [(0, 1)]))
    ys, xs, h1s, qkvo, qkvt, atts, aos, h2s, preo, pret, acto, actt, mos = saved
    layer_out = split_images(ys)

    inputs, mlp_kept, attn_kept = list(cotangent), None, None
    spots = ring_spots()
    for turn in range(2 * images):
        number, is_early = turn % images, turn < images
        index = turn_index(number, is_first != is_early)
        grad = inputs[turn]
        if attn_kept is not None:
            grad, attn_kept[1] = lax.optimization_barrier((grad, attn_kept[1]))
        answer = mlp_back_call(
            index, grad, mods, (xs, aos, mos, preo, pret), (*w_up, *w_down), mlp_kept, images
        )
        middle_grad, mlp_kept = answer[0], answer[1:]
        if turn == 2 * images - 1:
            mlp_sums, up_sums, down_ins, pre_grads_o, pre_grads_t = mlp_kept
            down_w = folded(outer(actt, down_ins), outer(acto, down_ins))
            up_w = folded(outer(h2s, pre_grads_t), outer(h2s, pre_grads_o))
            middle_grad, down_w = lax.optimization_barrier((middle_grad, down_w))
        answer = attn_back_call(
            index, middle_grad, mods, (xs, aos, qkvo, qkvt), (*w_qkv, *w_out), attn_kept, images
        )
        attn_kept = list(answer[1:])
        if is_early:
            inputs.append(lax.ppermute(answer[0], "section", [(1, 0)]))
    row_grads, attn_sums, qkv_sums, out_ins, qkv_grads_o, qkv_grads_t = attn_kept
    in_grad = split_images(row_grads)

    stacked = 3 * half
    attn_w = folded(
        jnp.concatenate([outers(qkv_grads_t, h1s).reshape(stacked, width), outer(atts[:, 1], out_ins)]),
        jnp.concatenate([outers(qkv_grads_o, h1s).reshape(stacked, width), outer(atts[:, 0], out_ins)]),
    )
    down_w_sum, up_w_sum = ring_plain(down_w, spots), ring_plain(up_w, spots)
    qkv_w_sum, out_w_sum = ring_attn(attn_w, spots)
    qkv_w_sum = jnp.transpose(qkv_w_sum, (2, 0, 1))

    mod_grad = jnp.concatenate([attn_sums[:, :3], mlp_sums[:, :3]], axis=1).astype(BF)
    columns = mod_grad.reshape(images, 2, 3 * width)
    own_cols = lax.dynamic_index_in_dim(columns, core, 1, keepdims=False)
    other_cols = lax.dynamic_index_in_dim(columns, 1 - core, 1, keepdims=False)
    mod_cols = in_order(own_cols, swap(other_cols), 0)
    silu_grad = jnp.einsum("sk,dk->sd", mod_cols, ada_weight[0], preferred_element_type=F32)
    silu_grad = silu_grad + swap(silu_grad)
    silu_grad = silu_grad + lax.ppermute(silu_grad, "section", [(0, 1), (1, 0)])
    cond_grad = silu_back(silu_grad)[0]

    silu_all = gather_all(silu_b)
    mod_all = gather_all(mod_cols)
    kept_rows = jnp.concatenate([cond_grad.reshape(1, -1), labels.astype(F32)[None]], axis=1)
    gathered = gather_all(kept_rows)
    cond_all = gathered[:, : slots * width].reshape(-1, width)
    labels_all = gathered[:, slots * width :].reshape(-1)
    ada_w_sum = jnp.einsum("sd,sk->dk", silu_all, mod_all, preferred_element_type=F32)
    ada_b_sum = jnp.sum(mod_all, axis=0, dtype=F32)
    onehot = (labels_all[None] == jnp.arange(label_table.shape[0], dtype=F32)[:, None]).astype(F32)
    table_grad = jnp.dot(onehot, cond_all, precision=lax.Precision.HIGHEST, preferred_element_type=F32)

    qkv_total, up_total = jnp.sum(qkv_sums, axis=0), jnp.sum(up_sums, axis=0)
    own_bias = jnp.concatenate([qkv_total[0], qkv_total[2], up_total[0]])
    other_bias = jnp.concatenate([qkv_total[3], qkv_total[5], up_total[1]])
    both_bias = jnp.concatenate([jnp.sum(attn_sums[:, 3], axis=0), jnp.sum(mlp_sums[:, 3], axis=0)])
    came_bias = swap(jnp.concatenate([other_bias, both_bias]))
    biases = add_all(jnp.concatenate([own_bias, both_bias]) + came_bias)
    qkv_b_sum = biases[: 2 * half].reshape(2, half)
    up_b_sum = biases[2 * half : 2 * half + hidden]
    out_b_sum = biases[2 * half + hidden : 2 * half + hidden + width]
    down_b_sum = biases[2 * half + hidden + width :]
    return (
        layer_out,
        in_grad,
        cond_grad,
        table_grad,
        ada_w_sum[None],
        ada_b_sum[None],
        qkv_w_sum[None],
        qkv_b_sum[None],
        out_w_sum[None],
        out_b_sum[None],
        up_w_sum[None],
        up_b_sum[None],
        down_w_sum[None],
        down_b_sum[None],
    )


def solution(mesh):
    placed = (
        P("tensor", "dp", None),
        P("dp"),
        P("dp"),
        P("dp"),
        P(),
        P("section", None, "tensor"),
        P("section", "tensor"),
        P("section", None, None, "tensor"),
        P("section", None, "tensor"),
        P("section", "tensor", None),
        P("section", None),
        P("section", None, "tensor"),
        P("section", "tensor"),
        P("section", "tensor", None),
        P("section", None),
        P("tensor", "dp", None),
    )
    return jax.shard_map(
        shards,
        mesh=mesh,
        in_specs=placed,
        out_specs=(
            P("section", "tensor", "dp", None),
            P("section", "tensor", "dp", None),
            P("dp", None),
            P(),
            P("section", None, "tensor"),
            P("section", "tensor"),
            P("section", None, None, "tensor"),
            P("section", None, "tensor"),
            P("section", "tensor", None),
            P("section", None),
            P("section", None, "tensor"),
            P("section", "tensor"),
            P("section", "tensor", None),
            P("section", None),
        ),
        check_vma=False,
    )
```

```python
import functools
import math
import jax
import jax.numpy as jnp
from jax import lax
from jax.experimental import pallas as pl
from jax.experimental.pallas import tpu as pltpu
from jax.sharding import PartitionSpec as P

HEADS = 16
eps_norm = 1e-06
BF, F32 = jnp.bfloat16, jnp.float32
ANY = pl.BlockSpec(memory_space=pl.ANY)
VM = pl.BlockSpec(memory_space=pltpu.VMEM)
LIMIT = 60 * 1024 * 1024
DEPTH = 4
ROOT = math.sqrt(2.0 / math.pi)
CUBE = 0.044715


def nt(left, right):
    return lax.dot_general(left, right, (((1,), (1,)), ((), ())), preferred_element_type=F32)


def tn(left, right):
    return lax.dot_general(left, right, (((0,), (0,)), ((), ())), preferred_element_type=F32)


def nn(left, right):
    return jnp.dot(left, right, preferred_element_type=F32)


def norm_parts(rows):
    centered = rows - jnp.mean(rows, axis=-1, keepdims=True)
    inverse = lax.rsqrt(jnp.mean(centered * centered, axis=-1, keepdims=True) + eps_norm)
    return centered * inverse, inverse


def windows(width, size):
    spans = []
    for head in range(width // size):
        low, high = head * size, (head + 1) * size
        spans.append((low, high, low // 128 * 128, min(width, (high + 127) // 128 * 128)))
    return spans


def head_mask(span):
    low, high, start, stop = span
    lanes = lax.broadcasted_iota(jnp.int32, (1, stop - start), 1) + start
    return (lanes >= low) & (lanes < high)


class Copies:
    def __init__(self, sems):
        self.sems, self.used = sems, 0

    def start(self, source, target):
        copy = pltpu.make_async_copy(source, target, self.sems.at[self.used])
        self.used += 1
        copy.start()
        return copy


class Stream:
    def __init__(self, copies, depth, pairs):
        self.copies, self.depth, self.pairs, self.begun, self.taken = copies, depth, pairs, [], 0
        self.fill()

    def fill(self):
        while len(self.begun) < min(len(self.pairs), self.taken + self.depth):
            self.begun.append(self.copies.start(*self.pairs[len(self.begun)]))

    def take(self, count=1):
        for _ in range(count):
            self.begun[self.taken].wait()
            self.taken += 1
            self.fill()


def three_kinds(sources, target):
    return [(source.at[kind], target.at[side, kind]) for side, source in enumerate(sources) for kind in range(3)]


def soft(scores, scale):
    top = jnp.max(scores, axis=-1, keepdims=True)
    powers = jnp.exp2((scores - top) * (scale * math.log2(math.e)))
    return powers * (1.0 / jnp.sum(powers, axis=-1, keepdims=True))


def layer_kernel(chunks, index_ref, mod_ref, bqv_ref, bup_ref, bod_ref, x_in,
                 *rest):
    wqs, (woo, wot, wuo, wut, wdo, wdt) = rest[:2], rest[2:8]
    rest = rest[len(rest) - 30:]
    (y_out, ys, xs, h1s, qkvo, qkvt, atts, aos, h2s, preo, pret, acto, actt, mos,
     wq, wo, wu, wd, x, y, h1, qkv, att, attf, ao, h2, pre, act, mo, sems) = rest

    @pl.when(index_ref[1] == 1)
    def _():
        copies = Copies(sems)
        img = index_ref[0]
        step = wu.shape[2] // chunks
        spots = [(side, slice(place * step, (place + 1) * step)) for side in range(2) for place in range(chunks)]
        pairs = [(x_in, x), *three_kinds(wqs, wq), (woo, wo.at[0]), (wot, wo.at[1])]
        for side, spot in spots:
            up, down = ((wuo, wdo), (wut, wdt))[side]
            pairs += [(up.at[:, spot], wu.at[side, :, spot]), (down.at[spot, :], wd.at[side, spot, :])]
        stream = Stream(copies, DEPTH, pairs)
        half = att.shape[2]
        size = 2 * half // HEADS
        scale = size ** (-0.5)
        mods = mod_ref[img]
        stream.take()
        pending = [copies.start(x, xs.at[img])]
        normed, _ = norm_parts(x[...].astype(F32))
        h1[...] = (normed * (1.0 + mods[1:2]) + mods[0:1]).astype(BF)
        pending.append(copies.start(h1, h1s.at[img]))
        for part in range(6):
            side, kind = part // 3, part % 3
            stream.take()
            mixed = nt(h1[...], wq[side, kind])
            qkv[side, kind] = (mixed + bqv_ref[part : part + 1]).astype(BF)
        pending += [copies.start(qkv.at[0], qkvo.at[img]), copies.start(qkv.at[1], qkvt.at[img])]

        def attend(side, carry):
            attf[...] = jnp.zeros_like(attf)
            for span in windows(half, size):
                part = slice(span[2], span[3])
                mask = head_mask(span)
                zero = jnp.zeros((), BF)
                queries = jnp.where(mask, qkv[side, 0, :, part], zero)
                scores = nt(queries, qkv[side, 1, :, part])
                probs = soft(scores, scale).astype(BF)
                attf[:, part] += nn(probs, jnp.where(mask, qkv[side, 2, :, part], zero))
            att[side] = attf[...].astype(BF)
            return carry

        lax.fori_loop(0, 2, attend, 0)
        pending.append(copies.start(att, atts.at[img]))
        stream.take(2)
        ao[...] = nn(att[0], wo[0]) + nn(att[1], wo[1]) + bod_ref[0:1]
        pending.append(copies.start(ao, aos.at[img]))
        normed, _ = norm_parts(x[...].astype(F32) + mods[2:3] * ao[...])
        h2[...] = (normed * (1.0 + mods[4:5]) + mods[3:4]).astype(BF)
        pending.append(copies.start(h2, h2s.at[img]))
        for number, (side, spot) in enumerate(spots):
            stream.take()
            values = nn(h2[...], wu[side, :, spot]) + bup_ref[side : side + 1, spot]
            pre[side, :, spot] = values.astype(BF)
            inner = jnp.tanh(values * (ROOT + ROOT * CUBE * values * values))
            act[side, :, spot] = (0.5 * values * (1.0 + inner)).astype(BF)
            stream.take()
            term = nn(act[side, :, spot], wd[side, spot, :])
            mo[...] = term + (bod_ref[1:2] if number == 0 else mo[...])
            pre_out, act_out = ((preo, acto), (pret, actt))[side]
            pending += [copies.start(pre.at[side, :, spot], pre_out.at[img, :, spot]),
                        copies.start(act.at[side, :, spot], act_out.at[img, :, spot])]
        pending.append(copies.start(mo, mos.at[img]))
        y[...] = (mods[6:7] * (x[...].astype(F32) + mods[2:3] * ao[...] + mods[5:6] * mo[...])).astype(BF)
        pending += [copies.start(y, y_out), copies.start(y, ys.at[img])]
        for copy in pending:
            copy.wait()


SMALL = pl.CostEstimate(flops=1000, bytes_accessed=1000, transcendentals=0)


def layer_call(index, x, mods, bqv, bup, bod, weights, saved, images):
    tokens, width = x.shape
    half, hidden = width // 2, bup.shape[1]
    chunks = 3 if hidden % 384 == 0 else 1
    sd = jax.ShapeDtypeStruct
    outs = (
        sd((tokens, width), BF),
        sd((images, tokens, width), BF),
        sd((images, tokens, width), BF),
        sd((images, tokens, width), BF),
        sd((images, 3, tokens, half), BF),
        sd((images, 3, tokens, half), BF),
        sd((images, 2, tokens, half), BF),
        sd((images, tokens, width), F32),
        sd((images, tokens, width), BF),
        sd((images, tokens, hidden), BF),
        sd((images, tokens, hidden), BF),
        sd((images, tokens, hidden), BF),
        sd((images, tokens, hidden), BF),
        sd((images, tokens, width), F32),
    )
    saved = tuple(saved) if saved is not None else ()
    aliases = {14 + i: 1 + i for i in range(len(saved))}
    scratch = [
        pltpu.VMEM((2, 3, half, width), BF),
        pltpu.VMEM((2, half, width), BF),
        pltpu.VMEM((2, width, hidden), BF),
        pltpu.VMEM((2, hidden, width), BF),
        pltpu.VMEM((tokens, width), BF),
        pltpu.VMEM((tokens, width), BF),
        pltpu.VMEM((tokens, width), BF),
        pltpu.VMEM((2, 3, tokens, half), BF),
        pltpu.VMEM((2, tokens, half), BF),
        pltpu.VMEM((tokens, half), F32),
        pltpu.VMEM((tokens, width), F32),
        pltpu.VMEM((tokens, width), BF),
        pltpu.VMEM((2, tokens, hidden), BF),
        pltpu.VMEM((2, tokens, hidden), BF),
        pltpu.VMEM((tokens, width), F32),
        pltpu.SemaphoreType.DMA((64,)),
    ]
    return pl.pallas_call(
        functools.partial(layer_kernel, chunks),
        out_shape=outs,
        in_specs=[pl.BlockSpec(memory_space=pltpu.SMEM)] + [VM] * 4 + [ANY] * (9 + len(saved)),
        out_specs=[ANY] * 14,
        scratch_shapes=scratch,
        input_output_aliases=aliases,
        compiler_params=pltpu.CompilerParams(vmem_limit_bytes=LIMIT),
        cost_estimate=SMALL,
        name="layer",
    )(index, mods, bqv, bup, bod, x, *weights, *saved)


def mlp_back_kernel(chunks, index_ref, mod_ref, g_in, xs, aos, mos, preo, pret, wuo, wut, wdo, wdt, *rest):
    rest = rest[len(rest) - 20:]
    (mg_out, sums, bus, dis, pgo, pgt, wu, wd, g, mg, x, ao, mo, pre, di, pg, ng, total, bu, sems) = rest

    @pl.when(index_ref[1] == 1)
    def _():
        copies = Copies(sems)
        img = index_ref[0]
        step = pre.shape[2] // chunks
        spots = [(side, slice(place * step, (place + 1) * step)) for side in range(2) for place in range(chunks)]
        pairs = [(g_in, g)]
        for side, spot in spots:
            pre_in, up, down = ((preo, wuo, wdo), (pret, wut, wdt))[side]
            pairs += [(down.at[spot, :], wd.at[side, spot, :]), (pre_in.at[img, :, spot], pre.at[side, :, spot]),
                      (up.at[:, spot], wu.at[side, :, spot])]
        stream = Stream(copies, DEPTH, pairs + [(mos.at[img], mo), (xs.at[img], x), (aos.at[img], ao)])
        mods = mod_ref[img]
        stream.take()
        mg[...] = g[...].astype(F32) * mods[6:7]
        di[...] = (mg[...] * mods[5:6]).astype(BF)
        pending = [copies.start(di, dis.at[img])]
        for number, (side, spot) in enumerate(spots):
            stream.take(2)
            values = pre[side, :, spot].astype(F32)
            grad = nt(di[...], wd[side, spot, :])
            square = values * values
            inner = jnp.tanh(values * (ROOT + ROOT * CUBE * square))
            slope = 0.5 * (1.0 + inner) + 0.5 * values * (1.0 - inner * inner) * (ROOT + 3.0 * ROOT * CUBE * square)
            graded = (grad * slope).astype(BF)
            pg[side, :, spot] = graded
            bu[side : side + 1, spot] = jnp.sum(graded.astype(F32), axis=0, keepdims=True)
            stream.take()
            term = nt(pg[side, :, spot], wu[side, :, spot])
            ng[...] = term if number == 0 else ng[...] + term
            pending.append(copies.start(pg.at[side, :, spot], (pgo, pgt)[side].at[img, :, spot]))
        pending.append(copies.start(bu, bus.at[img]))
        stream.take()
        total[2:3] = jnp.sum(mg[...] * mo[...], axis=0, keepdims=True)
        total[3:4] = jnp.sum(di[...].astype(F32), axis=0, keepdims=True)
        stream.take(2)
        normed, inverse = norm_parts(x[...].astype(F32) + mods[2:3] * ao[...])
        total[0:1] = jnp.sum(ng[...], axis=0, keepdims=True)
        total[1:2] = jnp.sum(ng[...] * normed, axis=0, keepdims=True)
        pending.append(copies.start(total, sums.at[img]))
        dn = ng[...] * (1.0 + mods[4:5])
        mg[...] += inverse * (
            dn - jnp.mean(dn, axis=-1, keepdims=True) - normed * jnp.mean(dn * normed, axis=-1, keepdims=True))
        pending.append(copies.start(mg, mg_out))
        for copy in pending:
            copy.wait()


def mlp_back_call(index, grad, mods, saved, weights, kept, images, deps=()):
    xs, aos, mos, preo, pret = saved
    tokens, width = grad.shape
    hidden = preo.shape[2]
    chunks = 3 if hidden % 384 == 0 else 1
    sd = jax.ShapeDtypeStruct
    kept = tuple(kept) if kept is not None else ()
    aliases = {12 + i: 1 + i for i in range(len(kept))}
    scratch = [
        pltpu.VMEM((2, width, hidden), BF),
        pltpu.VMEM((2, hidden, width), BF),
        pltpu.VMEM((tokens, width), BF),
        pltpu.VMEM((tokens, width), F32),
        pltpu.VMEM((tokens, width), BF),
        pltpu.VMEM((tokens, width), F32),
        pltpu.VMEM((tokens, width), F32),
        pltpu.VMEM((2, tokens, hidden), BF),
        pltpu.VMEM((tokens, width), BF),
        pltpu.VMEM((2, tokens, hidden), BF),
        pltpu.VMEM((tokens, width), F32),
        pltpu.VMEM((8, width), F32),
        pltpu.VMEM((2, hidden), F32),
        pltpu.SemaphoreType.DMA((48,)),
    ]
    return pl.pallas_call(
        functools.partial(mlp_back_kernel, chunks),
        out_shape=(
            sd((tokens, width), F32), sd((images, 8, width), F32), sd((images, 2, hidden), F32),
            sd((images, tokens, width), BF), sd((images, tokens, hidden), BF), sd((images, tokens, hidden), BF)),
        in_specs=[pl.BlockSpec(memory_space=pltpu.SMEM), VM] + [ANY] * (10 + len(kept) + len(deps)),
        out_specs=[ANY] * 6,
        scratch_shapes=scratch,
        input_output_aliases=aliases,
        compiler_params=pltpu.CompilerParams(vmem_limit_bytes=LIMIT),
        cost_estimate=SMALL,
        name="mlp_back",
    )(index, mods, grad, xs, aos, mos, preo, pret, *weights, *kept, *deps)


def attn_back_kernel(index_ref, mod_ref, mg_in, xs, aos, qkvo, qkvt, *rest):
    wqs, (woo, wot) = rest[:2], rest[2:4]
    rest = rest[len(rest) - 22:]
    (rg_out, rgs, sums, bqvs, ois, qgo, qgt, wq, wo, mg, rg, x, ao, qkv, oi, qg, da, acc, ng, total, bqv, sems) = rest

    @pl.when(index_ref[1] == 1)
    def _():
        copies = Copies(sems)
        img = index_ref[0]
        stream = Stream(copies, DEPTH, [
            (mg_in, mg), (woo, wo.at[0]), (wot, wo.at[1]), (qkvo.at[img], qkv.at[0]), (qkvt.at[img], qkv.at[1]),
            *three_kinds(wqs, wq), (aos.at[img], ao), (xs.at[img], x)])
        half = wo.shape[1]
        size = 2 * half // HEADS
        scale = size ** (-0.5)
        mods = mod_ref[img]
        stream.take()
        oi[...] = (mg[...] * mods[2:3]).astype(BF)
        pending = [copies.start(oi, ois.at[img])]
        for side in range(2):
            stream.take()
            da[side] = nt(oi[...], wo[side]).astype(BF)
        stream.take(2)

        def attend(side, carry):
            for kind in range(3):
                acc[kind] = jnp.zeros_like(acc[kind])
            for span in windows(half, size):
                part = slice(span[2], span[3])
                mask = head_mask(span)
                zero = jnp.zeros((), BF)
                queries = jnp.where(mask, qkv[side, 0, :, part], zero)
                keys = jnp.where(mask, qkv[side, 1, :, part], zero)
                outer = jnp.where(mask, da[side, :, part], zero)
                probs = soft(nt(queries, keys), scale)
                grads = nt(outer, qkv[side, 2, :, part])
                inner = jnp.sum(grads * probs, axis=-1, keepdims=True)
                spread = (probs * (grads - inner)).astype(BF)
                acc[2, :, part] += tn(probs.astype(BF), outer)
                acc[0, :, part] += nn(spread, keys)
                acc[1, :, part] += tn(spread, queries)
            for kind in range(3):
                factor = 1.0 if kind == 2 else scale
                qg[side, kind] = (acc[kind] * factor).astype(BF)
            return carry

        lax.fori_loop(0, 2, attend, 0)
        for side, target in enumerate((qgo, qgt)):
            pending += [copies.start(qg.at[side, kind], target.at[kind, img]) for kind in range(3)]
        for part in range(6):
            side, kind = part // 3, part % 3
            stream.take()
            term = nn(qg[side, kind], wq[side, kind])
            ng[...] = term if part == 0 else ng[...] + term
            bqv[part : part + 1] = jnp.sum(qg[side, kind].astype(F32), axis=0, keepdims=True)
        pending.append(copies.start(bqv, bqvs.at[img]))
        stream.take()
        total[2:3] = jnp.sum(mg[...] * ao[...], axis=0, keepdims=True)
        total[3:4] = jnp.sum(oi[...].astype(F32), axis=0, keepdims=True)
        stream.take()
        normed, inverse = norm_parts(x[...].astype(F32))
        total[0:1] = jnp.sum(ng[...], axis=0, keepdims=True)
        total[1:2] = jnp.sum(ng[...] * normed, axis=0, keepdims=True)
        pending.append(copies.start(total, sums.at[img]))
        dn = ng[...] * (1.0 + mods[1:2])
        rg[...] = (mg[...] + inverse * (
            dn - jnp.mean(dn, axis=-1, keepdims=True) - normed * jnp.mean(dn * normed, axis=-1, keepdims=True))).astype(BF)
        pending += [copies.start(rg, rg_out), copies.start(rg, rgs.at[img])]
        for copy in pending:
            copy.wait()


def attn_back_call(index, grad, mods, saved, weights, kept, images, deps=()):
    xs, aos, qkvo, qkvt = saved
    tokens, width = grad.shape
    half = width // 2
    sd = jax.ShapeDtypeStruct
    kept = tuple(kept) if kept is not None else ()
    aliases = {11 + i: 1 + i for i in range(len(kept))}
    scratch = [
        pltpu.VMEM((2, 3, half, width), BF),
        pltpu.VMEM((2, half, width), BF),
        pltpu.VMEM((tokens, width), F32),
        pltpu.VMEM((tokens, width), BF),
        pltpu.VMEM((tokens, width), BF),
        pltpu.VMEM((tokens, width), F32),
        pltpu.VMEM((2, 3, tokens, half), BF),
        pltpu.VMEM((tokens, width), BF),
        pltpu.VMEM((2, 3, tokens, half), BF),
        pltpu.VMEM((2, tokens, half), BF),
        pltpu.VMEM((3, tokens, half), F32),
        pltpu.VMEM((tokens, width), F32),
        pltpu.VMEM((8, width), F32),
        pltpu.VMEM((8, half), F32),
        pltpu.SemaphoreType.DMA((32,)),
    ]
    return pl.pallas_call(
        attn_back_kernel,
        out_shape=(
            sd((tokens, width), BF), sd((images, tokens, width), BF), sd((images, 8, width), F32),
            sd((images, 8, half), F32), sd((images, tokens, width), BF),
            sd((3, images, tokens, half), BF), sd((3, images, tokens, half), BF)),
        in_specs=[pl.BlockSpec(memory_space=pltpu.SMEM), VM] + [ANY] * (9 + len(kept) + len(deps)),
        out_specs=[ANY] * 7,
        scratch_shapes=scratch,
        input_output_aliases=aliases,
        compiler_params=pltpu.CompilerParams(vmem_limit_bytes=LIMIT),
        cost_estimate=SMALL,
        name="attn_back",
    )(index, mods, grad, xs, aos, qkvo, qkvt, *weights, *kept, *deps)


def time_embed(timesteps, width_all):
    half_width = width_all // 2
    frequencies = jnp.exp(-math.log(10000.0) * jnp.arange(half_width, dtype=F32) / half_width)
    angles = timesteps.astype(F32)[:, None] * frequencies[None, :]
    return jnp.concatenate([jnp.cos(angles), jnp.sin(angles)], axis=1)


def swap(array):
    return lax.ppermute(array, "tensor", [(0, 1), (1, 0)])


def partners():
    peers = lax.axis_size("dp")
    place = lax.axis_index("dp")
    bit = 1
    while bit < peers:
        yield [(i, i ^ bit) for i in range(peers)], (place & bit) == 0
        bit *= 2


def gather_all(array):
    for pairs, is_low in partners():
        came = lax.ppermute(array, "dp", pairs)
        array = jnp.where(is_low, jnp.concatenate([array, came]), jnp.concatenate([came, array]))
    return array


def in_halves(values):
    high = lax.reduce_precision(values, 8, 7)
    return [high.astype(BF), (values - high).astype(BF)]


def ring_pairs(peers):
    order = list(range(0, peers, 2)) + list(range(1, peers, 2))[::-1]
    ahead = [(order[i], order[(i + 1) % peers]) for i in range(peers)]
    return ahead, [(b, a) for a, b in ahead]


def add_kernel(step, here_ref, blocks, *rest):
    came, (first, second, mine, sems) = rest[:2], rest[len(rest) - 4:]
    peers = blocks.shape[1]
    copies = []
    for side, sign in enumerate((1, -1)):
        spot = (here_ref[0] + (-sign * step) % peers) & (peers - 1)
        copies.append(pltpu.make_async_copy(blocks.at[side, spot], mine.at[side], sems.at[side]))
        copies[-1].start()
    for side, out in enumerate((first, second)):
        copies[side].wait()
        out[...] = (came[side][...].astype(F32) + mine[side].astype(F32)).astype(BF)


def write_kernel(step, peers, split, here_ref, *rest):
    whole_count = 2 if split else 1
    came, passed, rows, sems = rest[:2], rest[-4:-2], rest[-2], rest[-1]
    whole = rest[len(rest) - 4 - whole_count : -4]
    for side, sign in enumerate((1, -1)):
        spot = (here_ref[0] + (-sign * step) % peers) & (peers - 1)
        rows[side] = came[side][...].astype(F32)
        passed[side][...] = came[side][...]

        def send(target):
            copy = pltpu.make_async_copy(rows.at[side], target, sems.at[side])
            copy.start()
            return copy

        if split and side == 1:
            quarter = peers // 2

            @pl.when(spot < quarter)
            def _():
                send(whole[0].at[peers + spot]).wait()

            @pl.when(spot >= quarter)
            def _():
                send(whole[1].at[spot - quarter]).wait()
        elif split:
            waiting = send(whole[0].at[spot])
        else:
            copy = send(whole[0].at[side * peers + spot])
            if side == 0:
                waiting = copy
            else:
                copy.wait()
    waiting.wait()


class Ring:
    def __init__(self, terms, here, split):
        self.peers, self.here, self.split, self.step = lax.axis_size("dp"), here, split, 0
        self.count, self.width = terms.shape
        self.part = self.count // (2 * self.peers)
        self.blocks = terms.reshape(2, self.peers, self.part, self.width)
        self.pairs = ring_pairs(self.peers)
        self.moving = [self.block(side) for side in range(2)]
        self.totals = ()

    def block(self, side):
        none = jnp.uint32(0)
        start = (jnp.uint32(side), self.here[0].astype(jnp.uint32), none, none)
        return lax.dynamic_slice(self.blocks, start, (1, 1, self.part, self.width))[0, 0]

    def advance(self, deps=()):
        self.step += 1
        deps = list(deps)
        self.moving = [lax.ppermute(array, "dp", pairs) for array, pairs in zip(self.moving, self.pairs)]
        if self.step < self.peers:
            self.moving = self.add(deps)
        if self.step >= self.peers - 1:
            *self.totals, first, second = self.write(deps if self.step >= self.peers else [])
            self.moving = [first, second]

    def add(self, deps):
        part = jax.ShapeDtypeStruct((self.part, self.width), BF)
        return pl.pallas_call(
            functools.partial(add_kernel, self.step),
            out_shape=(part, part),
            in_specs=[pl.BlockSpec(memory_space=pltpu.SMEM), ANY, VM, VM] + [ANY] * len(deps),
            out_specs=(VM, VM),
            scratch_shapes=[pltpu.VMEM((2, self.part, self.width), BF), pltpu.SemaphoreType.DMA((2,))],
            cost_estimate=SMALL,
            name="ring_add",
        )(self.here, self.blocks, *self.moving, *deps)

    def write(self, deps):
        blocks = (3 * self.peers // 2, self.peers // 2) if self.split else (2 * self.peers,)
        outs = tuple(jax.ShapeDtypeStruct((count, self.part, self.width), F32) for count in blocks)
        part = jax.ShapeDtypeStruct((self.part, self.width), BF)
        return pl.pallas_call(
            functools.partial(write_kernel, self.step, self.peers, self.split),
            out_shape=(*outs, part, part),
            in_specs=[pl.BlockSpec(memory_space=pltpu.SMEM), VM, VM] + [ANY] * (len(self.totals) + len(deps)),
            out_specs=(ANY,) * len(outs) + (VM, VM),
            scratch_shapes=[pltpu.VMEM((2, self.part, self.width), F32), pltpu.SemaphoreType.DMA((2,))],
            input_output_aliases={3 + i: i for i in range(len(self.totals))},
            cost_estimate=SMALL,
            name="ring_write",
        )(self.here, *self.moving, *self.totals, *deps)


def flat(block):
    return block.reshape(-1, block.shape[-1])


def product_kernel(has_came, left_ref, right_ref, *rest):
    total = tn(flat(left_ref[...]), flat(right_ref[...]))
    if has_came:
        total = total + rest[0][...].astype(F32)
    rest[-1][...] = total.astype(BF)


def product(left, right, came=(), deps=()):
    images, tokens, rows = left.shape
    width = right.shape[2]
    block = 384 if rows % 384 == 0 else rows
    out = pl.BlockSpec((block, width), lambda i: (i, 0))
    return pl.pallas_call(
        functools.partial(product_kernel, bool(came)),
        out_shape=jax.ShapeDtypeStruct((rows, width), BF),
        grid=(rows // block,),
        in_specs=[
            pl.BlockSpec((images, tokens, block), lambda i: (0, 0, i)),
            pl.BlockSpec((images, tokens, width), lambda i: (0, 0, 0)),
        ] + [out] * len(came) + [ANY] * len(deps),
        out_specs=out,
        compiler_params=pltpu.CompilerParams(vmem_limit_bytes=LIMIT),
        cost_estimate=SMALL,
        name="product",
    )(left, right, *came, *deps)


def attn_product_kernel(has_came, qg_ref, h_ref, att_ref, oi_ref, *rest):
    def finish(total):
        if has_came:
            total = total + rest[0][...].astype(F32)
        rest[-1][...] = total.astype(BF)

    step = pl.program_id(0)

    @pl.when(step < 3)
    def _():
        finish(tn(flat(qg_ref[...]), flat(h_ref[...])))

    @pl.when(step == 3)
    def _():
        finish(tn(flat(att_ref[...]), flat(oi_ref[...])))


def attn_product(side, qkv_grads, h1s, atts, out_ins, came=(), deps=()):
    _, images, tokens, half = qkv_grads.shape
    width = h1s.shape[2]
    out = pl.BlockSpec((half, width), lambda i: (i, 0))
    whole = pl.BlockSpec((images, tokens, width), lambda i: (0, 0, 0))
    return pl.pallas_call(
        functools.partial(attn_product_kernel, bool(came)),
        out_shape=jax.ShapeDtypeStruct((4 * half, width), BF),
        grid=(4,),
        in_specs=[
            pl.BlockSpec((1, images, tokens, half), lambda i: (jnp.minimum(i, 2), 0, 0, 0)),
            whole,
            pl.BlockSpec((images, 1, tokens, half), lambda i: (0, side, 0, 0)),
            whole,
        ] + [out] * len(came) + [ANY] * len(deps),
        out_specs=out,
        compiler_params=pltpu.CompilerParams(vmem_limit_bytes=LIMIT),
        cost_estimate=SMALL,
        name="attn_product",
    )(qkv_grads, h1s, atts, out_ins, *came, *deps)


def shards(images_in, timesteps, labels, counts, label_table, ada_weight, ada_bias, qkv_weight,
           qkv_bias, out_weight, out_bias, up_weight, up_bias, down_weight, down_bias, out_cotangent):
    is_first = lax.axis_index("section") == 0
    core = lax.axis_index("tensor")
    slots = images_in.shape[1]
    images = slots // 2
    width = images_in.shape[2]
    hidden = up_weight.shape[2]
    half = out_weight.shape[1]

    def by_section(first_val, later_val):
        return jnp.where(is_first, first_val, later_val)

    def by_core(first_val, later_val):
        return jnp.where(core == 0, first_val, later_val)

    def in_order(own, came, axis):
        return by_core(jnp.concatenate([own, came], axis), jnp.concatenate([came, own], axis))

    def whole_images(rows):
        flat = rows.reshape(rows.shape[0], slots * width)
        early, later = flat[:, : images * width], flat[:, images * width :]
        own, came = by_core(early, later), swap(by_core(later, early))
        spans = [slice(i * width, (i + 1) * width) for i in range(images)]
        return [jnp.concatenate([own[:, span], came[:, span]], axis=0) for span in spans]

    qkv_own = jnp.transpose(qkv_weight[0], (1, 2, 0))
    w_qkv = (qkv_own, swap(qkv_own))
    w_out = (out_weight[0], swap(out_weight[0]))
    w_up = (up_weight[0], swap(up_weight[0]))
    w_down = (down_weight[0], swap(down_weight[0]))
    weights = (*w_qkv, *w_out, *w_up, *w_down)

    condition = jnp.take(label_table, labels, axis=0).astype(F32) + time_embed(timesteps, width)
    silu_cond, silu_back = jax.vjp(jax.nn.silu, condition)
    silu_b = silu_cond.astype(BF)
    mod_local = (
        jnp.dot(silu_b, ada_weight[0], preferred_element_type=F32) + ada_bias[0].astype(F32)[None]
    )
    early, later = mod_local[:images], mod_local[images:]
    modulation = in_order(by_core(early, later), swap(by_core(later, early)), 1).reshape(images, 6, width)
    slot_no = core * images + jnp.arange(images, dtype=jnp.int32)
    valid = (slot_no < counts[0]).astype(F32)
    mods = jnp.concatenate(
        [modulation, jnp.broadcast_to(valid[:, None, None], (images, 2, width))], axis=1
    )
    pair_bias = jnp.concatenate([qkv_bias[0, 0], qkv_bias[0, 1], up_bias[0]])[None]
    pair_bias = jnp.concatenate([pair_bias, swap(pair_bias)], axis=0).astype(F32)
    zero_row = jnp.zeros((half,), F32)
    bqv = jnp.stack([
        pair_bias[0, :half], zero_row, pair_bias[0, half : 2 * half],
        pair_bias[1, :half], zero_row, pair_bias[1, half : 2 * half], zero_row, zero_row])
    bup = pair_bias[:, 2 * half :]
    bod = jnp.concatenate([out_bias, down_bias], axis=0).astype(F32)

    def turn_index(number, is_active):
        return jnp.stack([jnp.int32(number), is_active.astype(jnp.int32)])

    inputs, cotangent, saved = whole_images(images_in), whole_images(out_cotangent), None
    for turn in range(2 * images):
        number, is_early = turn % images, turn < images
        answer = layer_call(
            turn_index(number, is_first == is_early), inputs[turn], mods, bqv, bup, bod, weights, saved, images
        )
        saved = answer[1:]
        if is_early:
            inputs.append(lax.ppermute(answer[0], "section", [(0, 1)]))
    ys, xs, h1s, qkvo, qkvt, atts, aos, h2s, preo, pret, acto, actt, mos = saved

    inputs, mlp_kept, attn_kept = cotangent, None, None
    peers, device = lax.axis_size("dp"), lax.axis_index("dp")
    here = jnp.where((device & 1) == 0, device >> 1, peers - 1 - (device >> 1)).astype(jnp.int32).reshape(1)
    deps = []
    for turn in range(2 * images):
        number, is_early = turn % images, turn < images
        index = turn_index(number, is_first != is_early)
        answer = mlp_back_call(
            index, inputs[turn], mods, (xs, aos, mos, preo, pret), (*w_up, *w_down), mlp_kept, images, deps
        )
        middle_grad, mlp_kept, deps = answer[0], answer[1:], []
        if turn == 2 * images - 1:
            mlp_sums, up_sums, down_ins, pre_grads_o, pre_grads_t = mlp_kept
            down_t = product(actt, down_ins)
            up_t = product(h2s, pre_grads_t, deps=[down_t])
            down_w = product(acto, down_ins, [swap(down_t)], [up_t])
            rings = [Ring(down_w, here, False)]
            up_w = product(h2s, pre_grads_o, [swap(up_t)], rings[0].moving)
            rings.append(Ring(up_w, here, False))
            rings[0].advance([up_w])
            deps = [*rings[0].moving, *rings[1].moving]
        answer = attn_back_call(
            index, middle_grad, mods, (xs, aos, qkvo, qkvt), (*w_qkv, *w_out), attn_kept, images, deps
        )
        attn_kept = list(answer[1:])
        deps = [attn_kept[1]]
        if is_early:
            inputs.append(lax.ppermute(answer[0], "section", [(1, 0)]))
    row_grads, attn_sums, qkv_sums, out_ins, qkv_grads_o, qkv_grads_t = attn_kept

    for ring in rings:
        ring.advance([attn_sums])
    deps = [*rings[0].moving, *rings[1].moving]
    attn_t = attn_product(1, qkv_grads_t, h1s, atts, out_ins, deps=deps)
    for ring in rings:
        ring.advance([attn_t])
    deps = [*rings[0].moving, *rings[1].moving]
    attn_w = attn_product(0, qkv_grads_o, h1s, atts, out_ins, [swap(attn_t)], deps)
    rings.append(Ring(attn_w, here, True))
    for ring in rings[:2]:
        ring.advance(rings[2].moving)
    attn_sums, mlp_sums, qkv_sums, up_sums, row_grads, ys, _ = lax.optimization_barrier(
        (attn_sums, mlp_sums, qkv_sums, up_sums, row_grads, ys, rings[1].moving))
    mod_grad = jnp.concatenate([attn_sums[:, :3], mlp_sums[:, :3]], axis=1).astype(BF)
    columns = mod_grad.reshape(images, 2 * 3 * width)
    early, later = columns[:, : 3 * width], columns[:, 3 * width :]
    mod_cols = in_order(by_core(early, later), swap(by_core(later, early)), 0)
    qkv_total, up_total = jnp.sum(qkv_sums, axis=0), jnp.sum(up_sums, axis=0)
    own_bias = jnp.concatenate([qkv_total[0], qkv_total[2], up_total[0]])
    other_bias = jnp.concatenate([qkv_total[3], qkv_total[5], up_total[1]])
    both_bias = jnp.concatenate([jnp.sum(attn_sums[:, 3], axis=0), jnp.sum(mlp_sums[:, 3], axis=0)])
    bias = jnp.concatenate([own_bias, both_bias]) + swap(jnp.concatenate([other_bias, both_bias]))
    silu_grad = jnp.einsum("sk,dk->sd", mod_cols, ada_weight[0], preferred_element_type=F32)
    silu_grad = silu_grad + swap(silu_grad)
    silu_grad = silu_grad + lax.ppermute(silu_grad, "section", [(0, 1), (1, 0)])
    cond_grad = silu_back(silu_grad)[0]
    packed = jnp.concatenate(
        [silu_b.reshape(-1), mod_cols.reshape(-1), *in_halves(cond_grad.reshape(-1)), *in_halves(bias),
         *in_halves(labels.astype(F32))])
    packed = gather_all(packed[None])
    sizes = [slots * width, slots * 3 * width] + [slots * width] * 2 + [bias.shape[0]] * 2 + [slots] * 2
    ends = [sum(sizes[: i + 1]) for i in range(len(sizes))]
    parts = [packed[:, end - size : end] for size, end in zip(sizes, ends)]
    silu_all, mod_all = parts[0].reshape(-1, width), parts[1].reshape(-1, 3 * width)
    cond_all = (parts[2].astype(F32) + parts[3].astype(F32)).reshape(-1, width)
    biases = jnp.sum(parts[4].astype(F32) + parts[5].astype(F32), axis=0)
    labels_all = (parts[6].astype(F32) + parts[7].astype(F32)).reshape(-1)
    ada_w_sum = jnp.einsum("sd,sk->dk", silu_all, mod_all, preferred_element_type=F32)
    ada_b_sum = jnp.sum(mod_all, axis=0, dtype=F32)
    classes = jnp.arange(label_table.shape[0], dtype=F32)
    onehot = (labels_all[None] == classes[:, None]).astype(F32)
    table_grad = jnp.dot(onehot, cond_all, precision=lax.Precision.HIGHEST, preferred_element_type=F32)

    def split_images(rows):
        own, other = jnp.split(rows, 2, axis=1)
        return jnp.moveaxis(in_order(own, swap(other), 0), 0, 1)[None]

    in_grad, layer_out = split_images(row_grads), split_images(ys)
    total_steps = 2 * peers - 2
    while rings[2].step < total_steps:
        before = rings[2].moving
        rings[2].advance(rings[1].moving if rings[1].step < total_steps else ())
        for ring in rings[:2]:
            if ring.step < total_steps:
                ring.advance(before)
    down_w_sum, up_w_sum = (ring.totals[0].reshape(ring.count, ring.width) for ring in rings[:2])
    qkv_w_sum = rings[2].totals[0].reshape(3, half, width)
    out_w_sum = rings[2].totals[1].reshape(half, width)
    qkv_w_sum = jnp.transpose(qkv_w_sum, (2, 0, 1))
    qkv_b_sum = biases[: 2 * half].reshape(2, half)
    up_b_sum = biases[2 * half : 2 * half + hidden]
    out_b_sum = biases[2 * half + hidden : 2 * half + hidden + width]
    down_b_sum = biases[2 * half + hidden + width :]
    return (
        layer_out,
        in_grad,
        cond_grad,
        table_grad,
        ada_w_sum[None],
        ada_b_sum[None],
        qkv_w_sum[None],
        qkv_b_sum[None],
        out_w_sum[None],
        out_b_sum[None],
        up_w_sum[None],
        up_b_sum[None],
        down_w_sum[None],
        down_b_sum[None],
    )


def solution(mesh):
    placed = (
        P("tensor", "dp", None),
        P("dp"),
        P("dp"),
        P("dp"),
        P(),
        P("section", None, "tensor"),
        P("section", "tensor"),
        P("section", None, None, "tensor"),
        P("section", None, "tensor"),
        P("section", "tensor", None),
        P("section", None),
        P("section", None, "tensor"),
        P("section", "tensor"),
        P("section", "tensor", None),
        P("section", None),
        P("tensor", "dp", None),
    )
    return jax.shard_map(
        shards,
        mesh=mesh,
        in_specs=placed,
        out_specs=(
            P("section", "tensor", "dp", None),
            P("section", "tensor", "dp", None),
            P("dp", None),
            P(),
            P("section", None, "tensor"),
            P("section", "tensor"),
            P("section", None, None, "tensor"),
            P("section", None, "tensor"),
            P("section", "tensor", None),
            P("section", None),
            P("section", None, "tensor"),
            P("section", "tensor"),
            P("section", "tensor", None),
            P("section", None),
        ),
        check_vma=False,
    )
```

```python
import functools
import math
import jax
import jax.numpy as jnp
from jax import lax
from jax.experimental import pallas as pl
from jax.experimental.pallas import tpu as pltpu
from jax.sharding import PartitionSpec as P

HEADS = 16
eps_norm = 1e-06
BF, F32 = jnp.bfloat16, jnp.float32
ANY = pl.BlockSpec(memory_space=pl.ANY)
HBM = pl.BlockSpec(memory_space=pltpu.HBM)
VM = pl.BlockSpec(memory_space=pltpu.VMEM)
LIMIT = 60 * 1024 * 1024
DEPTH = 4
ROOT = math.sqrt(2.0 / math.pi)
CUBE = 0.044715


def nt(left, right):
    return lax.dot_general(left, right, (((1,), (1,)), ((), ())), preferred_element_type=F32)


def tn(left, right):
    return lax.dot_general(left, right, (((0,), (0,)), ((), ())), preferred_element_type=F32)


def nn(left, right):
    return jnp.dot(left, right, preferred_element_type=F32)


def norm_parts(rows):
    centered = rows - jnp.mean(rows, axis=-1, keepdims=True)
    inverse = lax.rsqrt(jnp.mean(centered * centered, axis=-1, keepdims=True) + eps_norm)
    return centered * inverse, inverse


def windows(width, size):
    spans = []
    for head in range(width // size):
        low, high = head * size, (head + 1) * size
        spans.append((low, high, low // 128 * 128, min(width, (high + 127) // 128 * 128)))
    return spans


def head_mask(span):
    low, high, start, stop = span
    lanes = lax.broadcasted_iota(jnp.int32, (1, stop - start), 1) + start
    return (lanes >= low) & (lanes < high)


class Copies:
    def __init__(self, sems):
        self.sems, self.used = sems, 0

    def start(self, source, target):
        copy = pltpu.make_async_copy(source, target, self.sems.at[self.used])
        self.used += 1
        copy.start()
        return copy


class Stream:
    def __init__(self, copies, depth, pairs):
        self.copies, self.depth, self.pairs, self.begun, self.taken = copies, depth, pairs, [], 0
        self.fill()

    def fill(self):
        while len(self.begun) < min(len(self.pairs), self.taken + self.depth):
            self.begun.append(self.copies.start(*self.pairs[len(self.begun)]))

    def take(self, count=1):
        for _ in range(count):
            self.begun[self.taken].wait()
            self.taken += 1
            self.fill()


def three_kinds(sources, target):
    return [(source.at[kind], target.at[side, kind]) for side, source in enumerate(sources) for kind in range(3)]


def soft(scores, scale):
    top = jnp.max(scores, axis=-1, keepdims=True)
    powers = jnp.exp2((scores - top) * (scale * math.log2(math.e)))
    return powers * (1.0 / jnp.sum(powers, axis=-1, keepdims=True))


def layer_kernel(chunks, index_ref, mod_ref, bqv_ref, bup_ref, bod_ref, x_in,
                 *rest):
    wqs, (woo, wot, wuo, wut, wdo, wdt) = rest[:2], rest[2:8]
    rest = rest[len(rest) - 30:]
    (y_out, ys, xs, h1s, qkvo, qkvt, atts, aos, h2s, preo, pret, acto, actt, mos,
     wq, wo, wu, wd, x, y, h1, qkv, att, attf, ao, h2, pre, act, mo, sems) = rest

    @pl.when(index_ref[1] == 1)
    def _():
        copies = Copies(sems)
        img = index_ref[0]
        step = wu.shape[2] // chunks
        spots = [(side, slice(place * step, (place + 1) * step)) for side in range(2) for place in range(chunks)]
        pairs = [(x_in, x), *three_kinds(wqs, wq), (woo, wo.at[0]), (wot, wo.at[1])]
        for side, spot in spots:
            up, down = ((wuo, wdo), (wut, wdt))[side]
            pairs += [(up.at[:, spot], wu.at[side, :, spot]), (down.at[spot, :], wd.at[side, spot, :])]
        stream = Stream(copies, DEPTH, pairs)
        half = att.shape[2]
        size = 2 * half // HEADS
        scale = size ** (-0.5)
        mods = mod_ref[img]
        stream.take()
        pending = [copies.start(x, xs.at[img])]
        normed, _ = norm_parts(x[...].astype(F32))
        h1[...] = (normed * (1.0 + mods[1:2]) + mods[0:1]).astype(BF)
        pending.append(copies.start(h1, h1s.at[img]))
        for part in range(6):
            side, kind = part // 3, part % 3
            stream.take()
            mixed = nt(h1[...], wq[side, kind])
            qkv[side, kind] = (mixed + bqv_ref[part : part + 1]).astype(BF)
        pending += [copies.start(qkv.at[0], qkvo.at[img]), copies.start(qkv.at[1], qkvt.at[img])]

        def attend(side, carry):
            attf[...] = jnp.zeros_like(attf)
            for span in windows(half, size):
                part = slice(span[2], span[3])
                mask = head_mask(span)
                zero = jnp.zeros((), BF)
                queries = jnp.where(mask, qkv[side, 0, :, part], zero)
                scores = nt(queries, qkv[side, 1, :, part])
                probs = soft(scores, scale).astype(BF)
                attf[:, part] += nn(probs, jnp.where(mask, qkv[side, 2, :, part], zero))
            att[side] = attf[...].astype(BF)
            return carry

        lax.fori_loop(0, 2, attend, 0)
        pending.append(copies.start(att, atts.at[img]))
        stream.take(2)
        ao[...] = nn(att[0], wo[0]) + nn(att[1], wo[1]) + bod_ref[0:1]
        pending.append(copies.start(ao, aos.at[img]))
        normed, _ = norm_parts(x[...].astype(F32) + mods[2:3] * ao[...])
        h2[...] = (normed * (1.0 + mods[4:5]) + mods[3:4]).astype(BF)
        pending.append(copies.start(h2, h2s.at[img]))
        stream.take()
        values = nn(h2[...], wu[0, :, spots[0][1]])
        for number, (side, spot) in enumerate(spots):
            stream.take(2 if number + 1 < len(spots) else 1)
            if number + 1 < len(spots):
                later = nn(h2[...], wu[spots[number + 1][0], :, spots[number + 1][1]])
            values = values + bup_ref[side : side + 1, spot]
            pre[side, :, spot] = values.astype(BF)
            inner = jnp.tanh(values * (ROOT + ROOT * CUBE * values * values))
            act[side, :, spot] = (0.5 * values * (1.0 + inner)).astype(BF)
            term = nn(act[side, :, spot], wd[side, spot, :])
            mo[...] = term + (bod_ref[1:2] if number == 0 else mo[...])
            pre_out, act_out = ((preo, acto), (pret, actt))[side]
            pending += [copies.start(pre.at[side, :, spot], pre_out.at[img, :, spot]),
                        copies.start(act.at[side, :, spot], act_out.at[img, :, spot])]
            values = later
        pending.append(copies.start(mo, mos.at[img]))
        y[...] = (mods[6:7] * (x[...].astype(F32) + mods[2:3] * ao[...] + mods[5:6] * mo[...])).astype(BF)
        pending += [copies.start(y, y_out), copies.start(y, ys.at[img])]
        for copy in pending:
            copy.wait()


TOKEN = jax.ShapeDtypeStruct((8, 128), F32)
SMALL = pl.CostEstimate(flops=1000, bytes_accessed=1000, transcendentals=0)


def layer_call(index, x, mods, bqv, bup, bod, weights, saved, images):
    tokens, width = x.shape
    half, hidden = width // 2, bup.shape[1]
    chunks = 3 if hidden % 384 == 0 else 1
    sd = jax.ShapeDtypeStruct
    outs = (
        sd((tokens, width), BF),
        sd((images, tokens, width), BF),
        sd((images, tokens, width), BF),
        sd((images, tokens, width), BF),
        sd((images, 3, tokens, half), BF),
        sd((images, 3, tokens, half), BF),
        sd((images, 2, tokens, half), BF),
        sd((images, tokens, width), F32),
        sd((images, tokens, width), BF),
        sd((images, tokens, hidden), BF),
        sd((images, tokens, hidden), BF),
        sd((images, tokens, hidden), BF),
        sd((images, tokens, hidden), BF),
        sd((images, tokens, width), F32),
    )
    saved = tuple(saved) if saved is not None else ()
    aliases = {14 + i: 1 + i for i in range(len(saved))}
    scratch = [
        pltpu.VMEM((2, 3, half, width), BF),
        pltpu.VMEM((2, half, width), BF),
        pltpu.VMEM((2, width, hidden), BF),
        pltpu.VMEM((2, hidden, width), BF),
        pltpu.VMEM((tokens, width), BF),
        pltpu.VMEM((tokens, width), BF),
        pltpu.VMEM((tokens, width), BF),
        pltpu.VMEM((2, 3, tokens, half), BF),
        pltpu.VMEM((2, tokens, half), BF),
        pltpu.VMEM((tokens, half), F32),
        pltpu.VMEM((tokens, width), F32),
        pltpu.VMEM((tokens, width), BF),
        pltpu.VMEM((2, tokens, hidden), BF),
        pltpu.VMEM((2, tokens, hidden), BF),
        pltpu.VMEM((tokens, width), F32),
        pltpu.SemaphoreType.DMA((64,)),
    ]
    return pl.pallas_call(
        functools.partial(layer_kernel, chunks),
        out_shape=outs,
        in_specs=[pl.BlockSpec(memory_space=pltpu.SMEM)] + [VM] * 4 + [ANY] * (9 + len(saved)),
        out_specs=[ANY] * 14,
        scratch_shapes=scratch,
        input_output_aliases=aliases,
        compiler_params=pltpu.CompilerParams(vmem_limit_bytes=LIMIT),
        cost_estimate=SMALL,
        name="layer",
    )(index, mods, bqv, bup, bod, x, *weights, *saved)


def mlp_back_kernel(chunks, index_ref, mod_ref, g_in, xs, aos, mos, preo, pret, wuo, wut, wdo, wdt, *rest):
    rest = rest[len(rest) - 20:]
    (mg_out, sums, bus, dis, pgo, pgt, wu, wd, g, mg, x, ao, mo, pre, di, pg, ng, total, bu, sems) = rest

    @pl.when(index_ref[1] == 1)
    def _():
        copies = Copies(sems)
        img = index_ref[0]
        step = pre.shape[2] // chunks
        spots = [(side, slice(place * step, (place + 1) * step)) for side in range(2) for place in range(chunks)]
        pairs, ups = [(g_in, g)], []
        for side, spot in spots:
            pre_in, up, down = ((preo, wuo, wdo), (pret, wut, wdt))[side]
            pairs += [(down.at[spot, :], wd.at[side, spot, :]), *ups]
            ups = [(pre_in.at[img, :, spot], pre.at[side, :, spot]), (up.at[:, spot], wu.at[side, :, spot])]
        pairs += ups
        stream = Stream(copies, DEPTH, pairs + [(mos.at[img], mo), (xs.at[img], x), (aos.at[img], ao)])
        mods = mod_ref[img]
        stream.take()
        mg[...] = g[...].astype(F32) * mods[6:7]
        di[...] = (mg[...] * mods[5:6]).astype(BF)
        pending = [copies.start(di, dis.at[img])]
        stream.take()
        grad = nt(di[...], wd[0, spots[0][1], :])
        for number, (side, spot) in enumerate(spots):
            stream.take(3 if number + 1 < len(spots) else 2)
            if number + 1 < len(spots):
                later = nt(di[...], wd[spots[number + 1][0], spots[number + 1][1], :])
            values = pre[side, :, spot].astype(F32)
            square = values * values
            inner = jnp.tanh(values * (ROOT + ROOT * CUBE * square))
            slope = 0.5 * (1.0 + inner) + 0.5 * values * (1.0 - inner * inner) * (ROOT + 3.0 * ROOT * CUBE * square)
            graded = (grad * slope).astype(BF)
            pg[side, :, spot] = graded
            bu[side : side + 1, spot] = jnp.sum(graded.astype(F32), axis=0, keepdims=True)
            term = nt(pg[side, :, spot], wu[side, :, spot])
            ng[...] = term if number == 0 else ng[...] + term
            pending.append(copies.start(pg.at[side, :, spot], (pgo, pgt)[side].at[img, :, spot]))
            grad = later
        pending.append(copies.start(bu, bus.at[img]))
        stream.take()
        total[2:3] = jnp.sum(mg[...] * mo[...], axis=0, keepdims=True)
        total[3:4] = jnp.sum(di[...].astype(F32), axis=0, keepdims=True)
        stream.take(2)
        normed, inverse = norm_parts(x[...].astype(F32) + mods[2:3] * ao[...])
        total[0:1] = jnp.sum(ng[...], axis=0, keepdims=True)
        total[1:2] = jnp.sum(ng[...] * normed, axis=0, keepdims=True)
        pending.append(copies.start(total, sums.at[img]))
        dn = ng[...] * (1.0 + mods[4:5])
        mg[...] += inverse * (
            dn - jnp.mean(dn, axis=-1, keepdims=True) - normed * jnp.mean(dn * normed, axis=-1, keepdims=True))
        pending.append(copies.start(mg, mg_out))
        for copy in pending:
            copy.wait()


def mlp_back_call(index, grad, mods, saved, weights, kept, images, deps=()):
    xs, aos, mos, preo, pret = saved
    tokens, width = grad.shape
    hidden = preo.shape[2]
    chunks = 3 if hidden % 384 == 0 else 1
    sd = jax.ShapeDtypeStruct
    kept = tuple(kept) if kept is not None else ()
    aliases = {12 + i: 1 + i for i in range(len(kept))}
    scratch = [
        pltpu.VMEM((2, width, hidden), BF),
        pltpu.VMEM((2, hidden, width), BF),
        pltpu.VMEM((tokens, width), BF),
        pltpu.VMEM((tokens, width), F32),
        pltpu.VMEM((tokens, width), BF),
        pltpu.VMEM((tokens, width), F32),
        pltpu.VMEM((tokens, width), F32),
        pltpu.VMEM((2, tokens, hidden), BF),
        pltpu.VMEM((tokens, width), BF),
        pltpu.VMEM((2, tokens, hidden), BF),
        pltpu.VMEM((tokens, width), F32),
        pltpu.VMEM((8, width), F32),
        pltpu.VMEM((2, hidden), F32),
        pltpu.SemaphoreType.DMA((48,)),
    ]
    return pl.pallas_call(
        functools.partial(mlp_back_kernel, chunks),
        out_shape=(
            sd((tokens, width), F32), sd((images, 8, width), F32), sd((images, 2, hidden), F32),
            sd((images, tokens, width), BF), sd((images, tokens, hidden), BF), sd((images, tokens, hidden), BF)),
        in_specs=[pl.BlockSpec(memory_space=pltpu.SMEM), VM] + [ANY] * (10 + len(kept)) + [HBM] * len(deps),
        out_specs=[ANY] * 6,
        scratch_shapes=scratch,
        input_output_aliases=aliases,
        compiler_params=pltpu.CompilerParams(vmem_limit_bytes=LIMIT),
        cost_estimate=SMALL,
        name="mlp_back",
    )(index, mods, grad, xs, aos, mos, preo, pret, *weights, *kept, *deps)


def attn_back_kernel(index_ref, mod_ref, mg_in, xs, aos, qkvo, qkvt, *rest):
    wqs, (woo, wot) = rest[:2], rest[2:4]
    rest = rest[len(rest) - 22:]
    (rg_out, rgs, sums, bqvs, ois, qgo, qgt, wq, wo, mg, rg, x, ao, qkv, oi, qg, da, acc, ng, total, bqv, sems) = rest

    @pl.when(index_ref[1] == 1)
    def _():
        copies = Copies(sems)
        img = index_ref[0]
        stream = Stream(copies, DEPTH, [
            (mg_in, mg), (woo, wo.at[0]), (wot, wo.at[1]), (qkvo.at[img], qkv.at[0]), (qkvt.at[img], qkv.at[1]),
            *three_kinds(wqs, wq), (aos.at[img], ao), (xs.at[img], x)])
        half = wo.shape[1]
        size = 2 * half // HEADS
        scale = size ** (-0.5)
        mods = mod_ref[img]
        stream.take()
        oi[...] = (mg[...] * mods[2:3]).astype(BF)
        pending = [copies.start(oi, ois.at[img])]
        for side in range(2):
            stream.take()
            da[side] = nt(oi[...], wo[side]).astype(BF)
        stream.take(2)

        def attend(side, carry):
            for kind in range(3):
                acc[kind] = jnp.zeros_like(acc[kind])
            for span in windows(half, size):
                part = slice(span[2], span[3])
                mask = head_mask(span)
                zero = jnp.zeros((), BF)
                queries = jnp.where(mask, qkv[side, 0, :, part], zero)
                keys = jnp.where(mask, qkv[side, 1, :, part], zero)
                outer = jnp.where(mask, da[side, :, part], zero)
                probs = soft(nt(queries, keys), scale)
                grads = nt(outer, qkv[side, 2, :, part])
                inner = jnp.sum(grads * probs, axis=-1, keepdims=True)
                spread = (probs * (grads - inner)).astype(BF)
                acc[2, :, part] += tn(probs.astype(BF), outer)
                acc[0, :, part] += nn(spread, keys)
                acc[1, :, part] += tn(spread, queries)
            for kind in range(3):
                factor = 1.0 if kind == 2 else scale
                qg[side, kind] = (acc[kind] * factor).astype(BF)
            return carry

        lax.fori_loop(0, 2, attend, 0)
        for side, target in enumerate((qgo, qgt)):
            pending += [copies.start(qg.at[side, kind], target.at[kind, img]) for kind in range(3)]
        for part in range(6):
            side, kind = part // 3, part % 3
            stream.take()
            term = nn(qg[side, kind], wq[side, kind])
            ng[...] = term if part == 0 else ng[...] + term
            bqv[part : part + 1] = jnp.sum(qg[side, kind].astype(F32), axis=0, keepdims=True)
        pending.append(copies.start(bqv, bqvs.at[img]))
        stream.take()
        total[2:3] = jnp.sum(mg[...] * ao[...], axis=0, keepdims=True)
        total[3:4] = jnp.sum(oi[...].astype(F32), axis=0, keepdims=True)
        stream.take()
        normed, inverse = norm_parts(x[...].astype(F32))
        total[0:1] = jnp.sum(ng[...], axis=0, keepdims=True)
        total[1:2] = jnp.sum(ng[...] * normed, axis=0, keepdims=True)
        pending.append(copies.start(total, sums.at[img]))
        dn = ng[...] * (1.0 + mods[1:2])
        rg[...] = (mg[...] + inverse * (
            dn - jnp.mean(dn, axis=-1, keepdims=True) - normed * jnp.mean(dn * normed, axis=-1, keepdims=True))).astype(BF)
        pending += [copies.start(rg, rg_out), copies.start(rg, rgs.at[img])]
        for copy in pending:
            copy.wait()


def attn_back_call(index, grad, mods, saved, weights, kept, images, deps=()):
    xs, aos, qkvo, qkvt = saved
    tokens, width = grad.shape
    half = width // 2
    sd = jax.ShapeDtypeStruct
    kept = tuple(kept) if kept is not None else ()
    aliases = {11 + i: 1 + i for i in range(len(kept))}
    scratch = [
        pltpu.VMEM((2, 3, half, width), BF),
        pltpu.VMEM((2, half, width), BF),
        pltpu.VMEM((tokens, width), F32),
        pltpu.VMEM((tokens, width), BF),
        pltpu.VMEM((tokens, width), BF),
        pltpu.VMEM((tokens, width), F32),
        pltpu.VMEM((2, 3, tokens, half), BF),
        pltpu.VMEM((tokens, width), BF),
        pltpu.VMEM((2, 3, tokens, half), BF),
        pltpu.VMEM((2, tokens, half), BF),
        pltpu.VMEM((3, tokens, half), F32),
        pltpu.VMEM((tokens, width), F32),
        pltpu.VMEM((8, width), F32),
        pltpu.VMEM((8, half), F32),
        pltpu.SemaphoreType.DMA((32,)),
    ]
    return pl.pallas_call(
        attn_back_kernel,
        out_shape=(
            sd((tokens, width), BF), sd((images, tokens, width), BF), sd((images, 8, width), F32),
            sd((images, 8, half), F32), sd((images, tokens, width), BF),
            sd((3, images, tokens, half), BF), sd((3, images, tokens, half), BF)),
        in_specs=[pl.BlockSpec(memory_space=pltpu.SMEM), VM] + [ANY] * (9 + len(kept)) + [HBM] * len(deps),
        out_specs=[ANY] * 7,
        scratch_shapes=scratch,
        input_output_aliases=aliases,
        compiler_params=pltpu.CompilerParams(vmem_limit_bytes=LIMIT),
        cost_estimate=SMALL,
        name="attn_back",
    )(index, mods, grad, xs, aos, qkvo, qkvt, *weights, *kept, *deps)


def time_embed(timesteps, width_all):
    half_width = width_all // 2
    frequencies = jnp.exp(-math.log(10000.0) * jnp.arange(half_width, dtype=F32) / half_width)
    angles = timesteps.astype(F32)[:, None] * frequencies[None, :]
    return jnp.concatenate([jnp.cos(angles), jnp.sin(angles)], axis=1)


def swap(array):
    return lax.ppermute(array, "tensor", [(0, 1), (1, 0)])


def partners():
    peers = lax.axis_size("dp")
    place = lax.axis_index("dp")
    bit = 1
    while bit < peers:
        yield [(i, i ^ bit) for i in range(peers)], (place & bit) == 0
        bit *= 2


def gather_all(array):
    for pairs, is_low in partners():
        came = lax.ppermute(array, "dp", pairs)
        array = jnp.where(is_low, jnp.concatenate([array, came]), jnp.concatenate([came, array]))
    return array


def in_halves(values):
    high = lax.reduce_precision(values, 8, 7)
    return [high.astype(BF), (values - high).astype(BF)]


def ring_pairs(peers):
    order = list(range(0, peers, 2)) + list(range(1, peers, 2))[::-1]
    ahead = [(order[i], order[(i + 1) % peers]) for i in range(peers)]
    return ahead, [(b, a) for a, b in ahead]


def add_kernel(step, here_ref, blocks, *rest):
    came, (first, second, _, mine, theirs, sems) = rest[:2], rest[len(rest) - 6:]
    peers = blocks.shape[1]
    copies = []
    for side, sign in enumerate((1, -1)):
        spot = (here_ref[0] + (-sign * step) % peers) & (peers - 1)
        copies.append(pltpu.make_async_copy(blocks.at[side, spot], mine.at[side], sems.at[side]))
        copies.append(pltpu.make_async_copy(came[side], theirs.at[side], sems.at[2 + side]))
    for copy in copies:
        copy.start()
    for side, out in enumerate((first, second)):
        copies[2 * side].wait()
        copies[2 * side + 1].wait()
        out[...] = (theirs[side].astype(F32) + mine[side].astype(F32)).astype(BF)


def write_kernel(steps, peers, split, passes, here_ref, *rest):
    count, passed_count, whole_count = 2 * len(steps), 2 if passes else 0, 2 if split else 1
    came, (blocks, rows, sems) = rest[:count], rest[-3:]
    outs = rest[len(rest) - 4 - passed_count - whole_count : -4]
    whole, passed = outs[:whole_count], outs[whole_count:]
    quarter = peers // 2
    arrivals = [pltpu.make_async_copy(came[i], blocks.at[i], sems.at[0, i]) for i in range(count)]
    for copy in arrivals:
        copy.start()

    def targets(number):
        step, side = steps[number // 2], number % 2
        spot = (here_ref[0] + (-(1 - 2 * side) * step) % peers) & (peers - 1)
        if not split:
            return [(None, whole[0].at[side * peers + spot])]
        if side == 0:
            return [(None, whole[0].at[spot])]
        return [
            (spot < quarter, whole[0].at[peers + jnp.minimum(spot, quarter - 1)]),
            (spot >= quarter, whole[1].at[jnp.maximum(spot - quarter, 0)]),
        ]

    def each(number, act):
        for test, target in targets(number):
            copy = pltpu.make_async_copy(rows.at[number], target, sems.at[1, number])
            if test is None:
                act(copy)
            else:
                pl.when(test)(functools.partial(act, copy))

    for number in range(count):
        arrivals[number].wait()
        rows[number] = blocks[number].astype(F32)
        each(number, lambda copy: copy.start())
        if passes and number >= count - 2:
            passed[number - count][...] = blocks[number]
    for number in range(count):
        each(number, lambda copy: copy.wait())


class Ring:
    def __init__(self, terms, here, split):
        self.peers, self.here, self.split, self.step = lax.axis_size("dp"), here, split, 0
        self.count, self.width = terms.shape
        self.part = self.count // (2 * self.peers)
        self.blocks = terms.reshape(2, self.peers, self.part, self.width)
        self.pairs = ring_pairs(self.peers)
        self.moving = [self.block(side) for side in range(2)]
        self.totals, self.kept, self.token = (), [], terms

    def block(self, side):
        none = jnp.uint32(0)
        start = (jnp.uint32(side), self.here[0].astype(jnp.uint32), none, none)
        return lax.dynamic_slice(self.blocks, start, (1, 1, self.part, self.width))[0, 0]

    def advance(self, deps=()):
        self.step += 1
        deps = list(deps)
        self.moving = [lax.ppermute(array, "dp", pairs) for array, pairs in zip(self.moving, self.pairs)]
        if self.step < self.peers:
            *self.moving, self.token = self.add(deps)
        if self.step >= self.peers - 1:
            self.kept.append((self.step, self.moving))
            last = self.step == 2 * self.peers - 2
            if last or len(self.kept) == max(5, self.peers // 4):
                self.write(deps if self.step >= self.peers else [], not last)

    def add(self, deps):
        part = jax.ShapeDtypeStruct((self.part, self.width), BF)
        scratch = pltpu.VMEM((2, self.part, self.width), BF)
        return pl.pallas_call(
            functools.partial(add_kernel, self.step),
            out_shape=(part, part, TOKEN),
            in_specs=[pl.BlockSpec(memory_space=pltpu.SMEM)] + [HBM] * (3 + len(deps)),
            out_specs=(VM, VM, HBM),
            scratch_shapes=[scratch, scratch, pltpu.SemaphoreType.DMA((4,))],
            cost_estimate=SMALL,
            name="ring_add",
        )(self.here, self.blocks, *self.moving, *deps)

    def write(self, deps, passes):
        steps = tuple(step for step, _ in self.kept)
        came = [array for _, moving in self.kept for array in moving]
        blocks = (3 * self.peers // 2, self.peers // 2) if self.split else (2 * self.peers,)
        outs = tuple(jax.ShapeDtypeStruct((count, self.part, self.width), F32) for count in blocks)
        part = jax.ShapeDtypeStruct((self.part, self.width), BF)
        scratch = (len(came), self.part, self.width)
        answer = pl.pallas_call(
            functools.partial(write_kernel, steps, self.peers, self.split, passes),
            out_shape=(*outs, *((part, part) if passes else ()), TOKEN),
            in_specs=[pl.BlockSpec(memory_space=pltpu.SMEM)] + [HBM] * (len(came) + len(self.totals) + len(deps)),
            out_specs=(HBM,) * len(outs) + ((VM, VM) if passes else ()) + (HBM,),
            scratch_shapes=[
                pltpu.VMEM(scratch, BF), pltpu.VMEM(scratch, F32), pltpu.SemaphoreType.DMA((2, len(came)))],
            input_output_aliases={1 + len(came) + i: i for i in range(len(self.totals))},
            compiler_params=pltpu.CompilerParams(vmem_limit_bytes=LIMIT // 2),
            cost_estimate=SMALL,
            name="ring_write",
        )(self.here, *came, *self.totals, *deps)
        self.totals, self.kept, self.token = answer[: len(outs)], [], answer[-1]
        if passes:
            self.moving = list(answer[len(outs) : -1])


def flat(block):
    return block.reshape(-1, block.shape[-1])


def product_kernel(has_came, left_ref, right_ref, *rest):
    total = tn(flat(left_ref[...]), flat(right_ref[...]))
    if has_came:
        total = total + rest[0][...].astype(F32)
    rest[-1][...] = total.astype(BF)


def product(left, right, came=(), deps=()):
    images, tokens, rows = left.shape
    width = right.shape[2]
    block = 384 if rows % 384 == 0 else rows
    out = pl.BlockSpec((block, width), lambda i: (i, 0))
    return pl.pallas_call(
        functools.partial(product_kernel, bool(came)),
        out_shape=jax.ShapeDtypeStruct((rows, width), BF),
        grid=(rows // block,),
        in_specs=[
            pl.BlockSpec((images, tokens, block), lambda i: (0, 0, i)),
            pl.BlockSpec((images, tokens, width), lambda i: (0, 0, 0)),
        ] + [out] * len(came) + [HBM] * len(deps),
        out_specs=out,
        compiler_params=pltpu.CompilerParams(vmem_limit_bytes=LIMIT),
        cost_estimate=SMALL,
        name="product",
    )(left, right, *came, *deps)


def attn_product_kernel(has_came, qg_ref, h_ref, att_ref, oi_ref, *rest):
    def finish(total):
        if has_came:
            total = total + rest[0][...].astype(F32)
        rest[-1][...] = total.astype(BF)

    step = pl.program_id(0)

    @pl.when(step < 3)
    def _():
        finish(tn(flat(qg_ref[...]), flat(h_ref[...])))

    @pl.when(step == 3)
    def _():
        finish(tn(flat(att_ref[...]), flat(oi_ref[...])))


def attn_product(side, qkv_grads, h1s, atts, out_ins, came=(), deps=()):
    _, images, tokens, half = qkv_grads.shape
    width = h1s.shape[2]
    out = pl.BlockSpec((half, width), lambda i: (i, 0))
    whole = pl.BlockSpec((images, tokens, width), lambda i: (0, 0, 0))
    return pl.pallas_call(
        functools.partial(attn_product_kernel, bool(came)),
        out_shape=jax.ShapeDtypeStruct((4 * half, width), BF),
        grid=(4,),
        in_specs=[
            pl.BlockSpec((1, images, tokens, half), lambda i: (jnp.minimum(i, 2), 0, 0, 0)),
            whole,
            pl.BlockSpec((images, 1, tokens, half), lambda i: (0, side, 0, 0)),
            whole,
        ] + [out] * len(came) + [HBM] * len(deps),
        out_specs=out,
        compiler_params=pltpu.CompilerParams(vmem_limit_bytes=LIMIT),
        cost_estimate=SMALL,
        name="attn_product",
    )(qkv_grads, h1s, atts, out_ins, *came, *deps)


def shards(images_in, timesteps, labels, counts, label_table, ada_weight, ada_bias, qkv_weight,
           qkv_bias, out_weight, out_bias, up_weight, up_bias, down_weight, down_bias, out_cotangent):
    is_first = lax.axis_index("section") == 0
    core = lax.axis_index("tensor")
    slots = images_in.shape[1]
    images = slots // 2
    width = images_in.shape[2]
    hidden = up_weight.shape[2]
    half = out_weight.shape[1]

    def by_section(first_val, later_val):
        return jnp.where(is_first, first_val, later_val)

    def by_core(first_val, later_val):
        return jnp.where(core == 0, first_val, later_val)

    def in_order(own, came, axis):
        return by_core(jnp.concatenate([own, came], axis), jnp.concatenate([came, own], axis))

    def whole_images(rows):
        flat = rows.reshape(rows.shape[0], slots * width)
        early, later = flat[:, : images * width], flat[:, images * width :]
        own, came = by_core(early, later), swap(by_core(later, early))
        spans = [slice(i * width, (i + 1) * width) for i in range(images)]
        return [jnp.concatenate([own[:, span], came[:, span]], axis=0) for span in spans]

    qkv_own = jnp.transpose(qkv_weight[0], (1, 2, 0))
    w_qkv = (qkv_own, swap(qkv_own))
    w_out = (out_weight[0], swap(out_weight[0]))
    w_up = (up_weight[0], swap(up_weight[0]))
    w_down = (down_weight[0], swap(down_weight[0]))
    weights = (*w_qkv, *w_out, *w_up, *w_down)

    condition = jnp.take(label_table, labels, axis=0).astype(F32) + time_embed(timesteps, width)
    silu_cond, silu_back = jax.vjp(jax.nn.silu, condition)
    silu_b = silu_cond.astype(BF)
    mod_local = (
        jnp.dot(silu_b, ada_weight[0], preferred_element_type=F32) + ada_bias[0].astype(F32)[None]
    )
    early, later = mod_local[:images], mod_local[images:]
    modulation = in_order(by_core(early, later), swap(by_core(later, early)), 1).reshape(images, 6, width)
    slot_no = core * images + jnp.arange(images, dtype=jnp.int32)
    valid = (slot_no < counts[0]).astype(F32)
    mods = jnp.concatenate(
        [modulation, jnp.broadcast_to(valid[:, None, None], (images, 2, width))], axis=1
    )
    pair_bias = jnp.concatenate([qkv_bias[0, 0], qkv_bias[0, 1], up_bias[0]])[None]
    pair_bias = jnp.concatenate([pair_bias, swap(pair_bias)], axis=0).astype(F32)
    zero_row = jnp.zeros((half,), F32)
    bqv = jnp.stack([
        pair_bias[0, :half], zero_row, pair_bias[0, half : 2 * half],
        pair_bias[1, :half], zero_row, pair_bias[1, half : 2 * half], zero_row, zero_row])
    bup = pair_bias[:, 2 * half :]
    bod = jnp.concatenate([out_bias, down_bias], axis=0).astype(F32)

    def turn_index(number, is_active):
        return jnp.stack([jnp.int32(number), is_active.astype(jnp.int32)])

    inputs, cotangent, saved = whole_images(images_in), whole_images(out_cotangent), None
    for turn in range(2 * images):
        number, is_early = turn % images, turn < images
        answer = layer_call(
            turn_index(number, is_first == is_early), inputs[turn], mods, bqv, bup, bod, weights, saved, images
        )
        saved = answer[1:]
        if is_early:
            inputs.append(lax.ppermute(answer[0], "section", [(0, 1)]))
    ys, xs, h1s, qkvo, qkvt, atts, aos, h2s, preo, pret, acto, actt, mos = saved

    inputs, mlp_kept, attn_kept = cotangent, None, None
    peers, device = lax.axis_size("dp"), lax.axis_index("dp")
    here = jnp.where((device & 1) == 0, device >> 1, peers - 1 - (device >> 1)).astype(jnp.int32).reshape(1)
    deps = []
    for turn in range(2 * images):
        number, is_early = turn % images, turn < images
        index = turn_index(number, is_first != is_early)
        answer = mlp_back_call(
            index, inputs[turn], mods, (xs, aos, mos, preo, pret), (*w_up, *w_down), mlp_kept, images, deps
        )
        middle_grad, mlp_kept, deps = answer[0], answer[1:], []
        if turn == 2 * images - 1:
            mlp_sums, up_sums, down_ins, pre_grads_o, pre_grads_t = mlp_kept
            down_t = product(actt, down_ins)
            up_t = product(h2s, pre_grads_t, deps=[down_t])
            down_w = product(acto, down_ins, [swap(down_t)], [up_t])
            rings = [Ring(down_w, here, False)]
            up_w = product(h2s, pre_grads_o, [swap(up_t)], [rings[0].token])
            rings.append(Ring(up_w, here, False))
            rings[0].advance([up_w])
            deps = [rings[0].token, rings[1].token]
        answer = attn_back_call(
            index, middle_grad, mods, (xs, aos, qkvo, qkvt), (*w_qkv, *w_out), attn_kept, images, deps
        )
        attn_kept = list(answer[1:])
        deps = [attn_kept[1]]
        if is_early:
            inputs.append(lax.ppermute(answer[0], "section", [(1, 0)]))
    row_grads, attn_sums, qkv_sums, out_ins, qkv_grads_o, qkv_grads_t = attn_kept

    for ring in rings:
        ring.advance([attn_sums])
    deps = [rings[0].token, rings[1].token]
    attn_t = attn_product(1, qkv_grads_t, h1s, atts, out_ins, deps=deps)
    for ring in rings:
        ring.advance([attn_t])
    deps = [rings[0].token, rings[1].token]
    attn_w = attn_product(0, qkv_grads_o, h1s, atts, out_ins, [swap(attn_t)], deps)
    rings.append(Ring(attn_w, here, True))
    for ring in rings[:2]:
        ring.advance([attn_w])
    attn_sums, mlp_sums, qkv_sums, up_sums, row_grads, ys, _ = lax.optimization_barrier(
        (attn_sums, mlp_sums, qkv_sums, up_sums, row_grads, ys, rings[1].moving))
    mod_grad = jnp.concatenate([attn_sums[:, :3], mlp_sums[:, :3]], axis=1).astype(BF)
    columns = mod_grad.reshape(images, 2 * 3 * width)
    early, later = columns[:, : 3 * width], columns[:, 3 * width :]
    mod_cols = in_order(by_core(early, later), swap(by_core(later, early)), 0)
    qkv_total, up_total = jnp.sum(qkv_sums, axis=0), jnp.sum(up_sums, axis=0)
    own_bias = jnp.concatenate([qkv_total[0], qkv_total[2], up_total[0]])
    other_bias = jnp.concatenate([qkv_total[3], qkv_total[5], up_total[1]])
    both_bias = jnp.concatenate([jnp.sum(attn_sums[:, 3], axis=0), jnp.sum(mlp_sums[:, 3], axis=0)])
    bias = jnp.concatenate([own_bias, both_bias]) + swap(jnp.concatenate([other_bias, both_bias]))
    silu_grad = jnp.einsum("sk,dk->sd", mod_cols, ada_weight[0], preferred_element_type=F32)
    silu_grad = silu_grad + swap(silu_grad)
    silu_grad = silu_grad + lax.ppermute(silu_grad, "section", [(0, 1), (1, 0)])
    cond_grad = silu_back(silu_grad)[0]
    packed = jnp.concatenate(
        [silu_b.reshape(-1), mod_cols.reshape(-1), *in_halves(cond_grad.reshape(-1)), *in_halves(bias),
         *in_halves(labels.astype(F32))])
    packed = gather_all(packed[None])
    sizes = [slots * width, slots * 3 * width] + [slots * width] * 2 + [bias.shape[0]] * 2 + [slots] * 2
    ends = [sum(sizes[: i + 1]) for i in range(len(sizes))]
    parts = [packed[:, end - size : end] for size, end in zip(sizes, ends)]
    silu_all, mod_all = parts[0].reshape(-1, width), parts[1].reshape(-1, 3 * width)
    cond_all = (parts[2].astype(F32) + parts[3].astype(F32)).reshape(-1, width)
    biases = jnp.sum(parts[4].astype(F32) + parts[5].astype(F32), axis=0)
    labels_all = (parts[6].astype(F32) + parts[7].astype(F32)).reshape(-1)
    ada_w_sum = jnp.einsum("sd,sk->dk", silu_all, mod_all, preferred_element_type=F32)
    ada_b_sum = jnp.sum(mod_all, axis=0, dtype=F32)
    classes = jnp.arange(label_table.shape[0], dtype=F32)
    onehot = (labels_all[None] == classes[:, None]).astype(F32)
    table_grad = jnp.dot(onehot, cond_all, precision=lax.Precision.HIGHEST, preferred_element_type=F32)

    def split_images(rows):
        own, other = jnp.split(rows, 2, axis=1)
        return jnp.moveaxis(in_order(own, swap(other), 0), 0, 1)[None]

    in_grad, layer_out = split_images(row_grads), split_images(ys)
    total_steps = 2 * peers - 2
    earlier, leading = [], []
    while rings[2].step < total_steps:
        before, earlier = earlier, [rings[2].token]
        ahead = [ring.token for ring in rings[:2]]
        rings[2].advance(leading)
        leading = ahead
        for ring in rings[:2]:
            if ring.step < total_steps:
                ring.advance(before)
    down_w_sum, up_w_sum = (ring.totals[0].reshape(ring.count, ring.width) for ring in rings[:2])
    qkv_w_sum = rings[2].totals[0].reshape(3, half, width)
    out_w_sum = rings[2].totals[1].reshape(half, width)
    qkv_w_sum = jnp.transpose(qkv_w_sum, (2, 0, 1))
    qkv_b_sum = biases[: 2 * half].reshape(2, half)
    up_b_sum = biases[2 * half : 2 * half + hidden]
    out_b_sum = biases[2 * half + hidden : 2 * half + hidden + width]
    down_b_sum = biases[2 * half + hidden + width :]
    return (
        layer_out,
        in_grad,
        cond_grad,
        table_grad,
        ada_w_sum[None],
        ada_b_sum[None],
        qkv_w_sum[None],
        qkv_b_sum[None],
        out_w_sum[None],
        out_b_sum[None],
        up_w_sum[None],
        up_b_sum[None],
        down_w_sum[None],
        down_b_sum[None],
    )


def solution(mesh):
    placed = (
        P("tensor", "dp", None),
        P("dp"),
        P("dp"),
        P("dp"),
        P(),
        P("section", None, "tensor"),
        P("section", "tensor"),
        P("section", None, None, "tensor"),
        P("section", None, "tensor"),
        P("section", "tensor", None),
        P("section", None),
        P("section", None, "tensor"),
        P("section", "tensor"),
        P("section", "tensor", None),
        P("section", None),
        P("tensor", "dp", None),
    )
    return jax.shard_map(
        shards,
        mesh=mesh,
        in_specs=placed,
        out_specs=(
            P("section", "tensor", "dp", None),
            P("section", "tensor", "dp", None),
            P("dp", None),
            P(),
            P("section", None, "tensor"),
            P("section", "tensor"),
            P("section", None, None, "tensor"),
            P("section", None, "tensor"),
            P("section", "tensor", None),
            P("section", None),
            P("section", None, "tensor"),
            P("section", "tensor"),
            P("section", "tensor", None),
            P("section", None),
        ),
        check_vma=False,
    )
```

```python
import functools
import math
import jax
import jax.numpy as jnp
from jax import lax
from jax.experimental import pallas as pl
from jax.experimental.pallas import tpu as pltpu
from jax.sharding import PartitionSpec as P

HEADS = 16
eps_norm = 1e-06
BF, F32 = jnp.bfloat16, jnp.float32
ANY = pl.BlockSpec(memory_space=pl.ANY)
HBM = pl.BlockSpec(memory_space=pltpu.HBM)
VM = pl.BlockSpec(memory_space=pltpu.VMEM)
LIMIT = 60 * 1024 * 1024
DEPTH = 4
ROOT = math.sqrt(2.0 / math.pi)
CUBE = 0.044715


def nt(left, right):
    return lax.dot_general(left, right, (((1,), (1,)), ((), ())), preferred_element_type=F32)


def tn(left, right):
    return lax.dot_general(left, right, (((0,), (0,)), ((), ())), preferred_element_type=F32)


def nn(left, right):
    return jnp.dot(left, right, preferred_element_type=F32)


def norm_parts(rows):
    centered = rows - jnp.mean(rows, axis=-1, keepdims=True)
    inverse = lax.rsqrt(jnp.mean(centered * centered, axis=-1, keepdims=True) + eps_norm)
    return centered * inverse, inverse


def windows(width, size):
    spans = []
    for head in range(width // size):
        low, high = head * size, (head + 1) * size
        spans.append((low, high, low // 128 * 128, min(width, (high + 127) // 128 * 128)))
    return spans


def head_mask(span):
    low, high, start, stop = span
    lanes = lax.broadcasted_iota(jnp.int32, (1, stop - start), 1) + start
    return (lanes >= low) & (lanes < high)


class Copies:
    def __init__(self, sems):
        self.sems, self.used = sems, 0

    def start(self, source, target):
        copy = pltpu.make_async_copy(source, target, self.sems.at[self.used])
        self.used += 1
        copy.start()
        return copy


class Stream:
    def __init__(self, copies, depth, pairs):
        self.copies, self.depth, self.pairs, self.begun, self.taken = copies, depth, pairs, [], 0
        self.fill()

    def fill(self):
        while len(self.begun) < min(len(self.pairs), self.taken + self.depth):
            self.begun.append(self.copies.start(*self.pairs[len(self.begun)]))

    def take(self, count=1):
        for _ in range(count):
            self.begun[self.taken].wait()
            self.taken += 1
            self.fill()


def three_kinds(sources, target):
    return [(source.at[kind], target.at[side, kind]) for side, source in enumerate(sources) for kind in range(3)]


def soft(scores, scale):
    top = jnp.max(scores, axis=-1, keepdims=True)
    powers = jnp.exp2((scores - top) * (scale * math.log2(math.e)))
    return powers * (1.0 / jnp.sum(powers, axis=-1, keepdims=True))


def layer_kernel(chunks, index_ref, mod_ref, bqv_ref, bup_ref, bod_ref, x_in,
                 *rest):
    wqs, (woo, wot, wuo, wut, wdo, wdt) = rest[:2], rest[2:8]
    rest = rest[len(rest) - 32:]
    (y_out, ys, xs, h1s, qkvo, qkvt, atts, aos, h2s, preo, pret, acto, actt, mos,
     wq, wo, wu, wd, x, y, h1, qkv, att, attf, ao, h2, pre, act, mo, ao_b, mo_b, sems) = rest

    @pl.when(index_ref[1] == 1)
    def _():
        copies = Copies(sems)
        img = index_ref[0]
        step = wu.shape[2] // chunks
        spots = [(side, slice(place * step, (place + 1) * step)) for side in range(2) for place in range(chunks)]
        pairs = [(x_in, x), *three_kinds(wqs, wq), (woo, wo.at[0]), (wot, wo.at[1])]
        for side, spot in spots:
            up, down = ((wuo, wdo), (wut, wdt))[side]
            pairs += [(up.at[:, spot], wu.at[side, :, spot]), (down.at[spot, :], wd.at[side, spot, :])]
        stream = Stream(copies, DEPTH, pairs)
        half = att.shape[2]
        size = 2 * half // HEADS
        scale = size ** (-0.5)
        mods = mod_ref[img]
        stream.take()
        pending = [copies.start(x, xs.at[img])]
        normed, _ = norm_parts(x[...].astype(F32))
        h1[...] = (normed * (1.0 + mods[1:2]) + mods[0:1]).astype(BF)
        pending.append(copies.start(h1, h1s.at[img]))
        for part in range(6):
            side, kind = part // 3, part % 3
            stream.take()
            mixed = nt(h1[...], wq[side, kind])
            qkv[side, kind] = (mixed + bqv_ref[part : part + 1]).astype(BF)
        pending += [copies.start(qkv.at[0], qkvo.at[img]), copies.start(qkv.at[1], qkvt.at[img])]

        def attend(side, carry):
            attf[...] = jnp.zeros_like(attf)
            for span in windows(half, size):
                part = slice(span[2], span[3])
                mask = head_mask(span)
                zero = jnp.zeros((), BF)
                queries = jnp.where(mask, qkv[side, 0, :, part], zero)
                scores = nt(queries, qkv[side, 1, :, part])
                probs = soft(scores, scale).astype(BF)
                attf[:, part] += nn(probs, jnp.where(mask, qkv[side, 2, :, part], zero))
            att[side] = attf[...].astype(BF)
            return carry

        lax.fori_loop(0, 2, attend, 0)
        pending.append(copies.start(att, atts.at[img]))
        stream.take(2)
        ao[...] = nn(att[0], wo[0]) + nn(att[1], wo[1]) + bod_ref[0:1]
        ao_b[...] = ao[...].astype(BF)
        pending.append(copies.start(ao_b, aos.at[img]))
        normed, _ = norm_parts(x[...].astype(F32) + mods[2:3] * ao[...])
        h2[...] = (normed * (1.0 + mods[4:5]) + mods[3:4]).astype(BF)
        pending.append(copies.start(h2, h2s.at[img]))
        stream.take()
        values = nn(h2[...], wu[0, :, spots[0][1]])
        for number, (side, spot) in enumerate(spots):
            stream.take(2 if number + 1 < len(spots) else 1)
            if number + 1 < len(spots):
                later = nn(h2[...], wu[spots[number + 1][0], :, spots[number + 1][1]])
            values = values + bup_ref[side : side + 1, spot]
            pre[side, :, spot] = values.astype(BF)
            inner = jnp.tanh(values * (ROOT + ROOT * CUBE * values * values))
            act[side, :, spot] = (0.5 * values * (1.0 + inner)).astype(BF)
            term = nn(act[side, :, spot], wd[side, spot, :])
            mo[...] = term + (bod_ref[1:2] if number == 0 else mo[...])
            pre_out, act_out = ((preo, acto), (pret, actt))[side]
            pending += [copies.start(pre.at[side, :, spot], pre_out.at[img, :, spot]),
                        copies.start(act.at[side, :, spot], act_out.at[img, :, spot])]
            values = later
        mo_b[...] = mo[...].astype(BF)
        pending.append(copies.start(mo_b, mos.at[img]))
        y[...] = (mods[6:7] * (x[...].astype(F32) + mods[2:3] * ao[...] + mods[5:6] * mo[...])).astype(BF)
        pending += [copies.start(y, y_out), copies.start(y, ys.at[img])]
        for copy in pending:
            copy.wait()


TOKEN = jax.ShapeDtypeStruct((8, 128), F32)
SMALL = pl.CostEstimate(flops=1000, bytes_accessed=1000, transcendentals=0)


def layer_call(index, x, mods, bqv, bup, bod, weights, saved, images):
    tokens, width = x.shape
    half, hidden = width // 2, bup.shape[1]
    chunks = 3 if hidden % 384 == 0 else 1
    sd = jax.ShapeDtypeStruct
    outs = (
        sd((tokens, width), BF),
        sd((images, tokens, width), BF),
        sd((images, tokens, width), BF),
        sd((images, tokens, width), BF),
        sd((images, 3, tokens, half), BF),
        sd((images, 3, tokens, half), BF),
        sd((images, 2, tokens, half), BF),
        sd((images, tokens, width), BF),
        sd((images, tokens, width), BF),
        sd((images, tokens, hidden), BF),
        sd((images, tokens, hidden), BF),
        sd((images, tokens, hidden), BF),
        sd((images, tokens, hidden), BF),
        sd((images, tokens, width), BF),
    )
    saved = tuple(saved) if saved is not None else ()
    aliases = {14 + i: 1 + i for i in range(len(saved))}
    scratch = [
        pltpu.VMEM((2, 3, half, width), BF),
        pltpu.VMEM((2, half, width), BF),
        pltpu.VMEM((2, width, hidden), BF),
        pltpu.VMEM((2, hidden, width), BF),
        pltpu.VMEM((tokens, width), BF),
        pltpu.VMEM((tokens, width), BF),
        pltpu.VMEM((tokens, width), BF),
        pltpu.VMEM((2, 3, tokens, half), BF),
        pltpu.VMEM((2, tokens, half), BF),
        pltpu.VMEM((tokens, half), F32),
        pltpu.VMEM((tokens, width), F32),
        pltpu.VMEM((tokens, width), BF),
        pltpu.VMEM((2, tokens, hidden), BF),
        pltpu.VMEM((2, tokens, hidden), BF),
        pltpu.VMEM((tokens, width), F32),
        pltpu.VMEM((tokens, width), BF),
        pltpu.VMEM((tokens, width), BF),
        pltpu.SemaphoreType.DMA((64,)),
    ]
    return pl.pallas_call(
        functools.partial(layer_kernel, chunks),
        out_shape=outs,
        in_specs=[pl.BlockSpec(memory_space=pltpu.SMEM)] + [VM] * 4 + [ANY] * (9 + len(saved)),
        out_specs=[ANY] * 14,
        scratch_shapes=scratch,
        input_output_aliases=aliases,
        compiler_params=pltpu.CompilerParams(vmem_limit_bytes=LIMIT),
        cost_estimate=SMALL,
        name="layer",
    )(index, mods, bqv, bup, bod, x, *weights, *saved)


def mlp_back_kernel(chunks, index_ref, mod_ref, g_in, xs, aos, mos, preo, pret, wuo, wut, wdo, wdt, *rest):
    rest = rest[len(rest) - 20:]
    (mg_out, sums, bus, dis, pgo, pgt, wu, wd, g, mg, x, ao, mo, pre, di, pg, ng, total, bu, sems) = rest

    @pl.when(index_ref[1] == 1)
    def _():
        copies = Copies(sems)
        img = index_ref[0]
        step = pre.shape[2] // chunks
        spots = [(side, slice(place * step, (place + 1) * step)) for side in range(2) for place in range(chunks)]
        pairs, ups = [(g_in, g)], []
        for side, spot in spots:
            pre_in, up, down = ((preo, wuo, wdo), (pret, wut, wdt))[side]
            pairs += [(down.at[spot, :], wd.at[side, spot, :]), *ups]
            ups = [(pre_in.at[img, :, spot], pre.at[side, :, spot]), (up.at[:, spot], wu.at[side, :, spot])]
        pairs += ups
        stream = Stream(copies, DEPTH, pairs + [(mos.at[img], mo), (xs.at[img], x), (aos.at[img], ao)])
        mods = mod_ref[img]
        stream.take()
        mg[...] = g[...].astype(F32) * mods[6:7]
        di[...] = (mg[...] * mods[5:6]).astype(BF)
        pending = [copies.start(di, dis.at[img])]
        stream.take()
        grad = nt(di[...], wd[0, spots[0][1], :])
        for number, (side, spot) in enumerate(spots):
            stream.take(3 if number + 1 < len(spots) else 2)
            if number + 1 < len(spots):
                later = nt(di[...], wd[spots[number + 1][0], spots[number + 1][1], :])
            values = pre[side, :, spot].astype(F32)
            square = values * values
            inner = jnp.tanh(values * (ROOT + ROOT * CUBE * square))
            slope = 0.5 * (1.0 + inner) + 0.5 * values * (1.0 - inner * inner) * (ROOT + 3.0 * ROOT * CUBE * square)
            graded = (grad * slope).astype(BF)
            pg[side, :, spot] = graded
            bu[side : side + 1, spot] = jnp.sum(graded.astype(F32), axis=0, keepdims=True)
            term = nt(pg[side, :, spot], wu[side, :, spot])
            ng[...] = term if number == 0 else ng[...] + term
            pending.append(copies.start(pg.at[side, :, spot], (pgo, pgt)[side].at[img, :, spot]))
            grad = later
        pending.append(copies.start(bu, bus.at[img]))
        stream.take()
        total[2:3] = jnp.sum(mg[...] * mo[...].astype(F32), axis=0, keepdims=True)
        total[3:4] = jnp.sum(di[...].astype(F32), axis=0, keepdims=True)
        stream.take(2)
        normed, inverse = norm_parts(x[...].astype(F32) + mods[2:3] * ao[...].astype(F32))
        total[0:1] = jnp.sum(ng[...], axis=0, keepdims=True)
        total[1:2] = jnp.sum(ng[...] * normed, axis=0, keepdims=True)
        pending.append(copies.start(total, sums.at[img]))
        dn = ng[...] * (1.0 + mods[4:5])
        mg[...] += inverse * (
            dn - jnp.mean(dn, axis=-1, keepdims=True) - normed * jnp.mean(dn * normed, axis=-1, keepdims=True))
        pending.append(copies.start(mg, mg_out))
        for copy in pending:
            copy.wait()


def mlp_back_call(index, grad, mods, saved, weights, kept, images, deps=()):
    xs, aos, mos, preo, pret = saved
    tokens, width = grad.shape
    hidden = preo.shape[2]
    chunks = 3 if hidden % 384 == 0 else 1
    sd = jax.ShapeDtypeStruct
    kept = tuple(kept) if kept is not None else ()
    aliases = {12 + i: 1 + i for i in range(len(kept))}
    scratch = [
        pltpu.VMEM((2, width, hidden), BF),
        pltpu.VMEM((2, hidden, width), BF),
        pltpu.VMEM((tokens, width), BF),
        pltpu.VMEM((tokens, width), F32),
        pltpu.VMEM((tokens, width), BF),
        pltpu.VMEM((tokens, width), BF),
        pltpu.VMEM((tokens, width), BF),
        pltpu.VMEM((2, tokens, hidden), BF),
        pltpu.VMEM((tokens, width), BF),
        pltpu.VMEM((2, tokens, hidden), BF),
        pltpu.VMEM((tokens, width), F32),
        pltpu.VMEM((8, width), F32),
        pltpu.VMEM((2, hidden), F32),
        pltpu.SemaphoreType.DMA((48,)),
    ]
    return pl.pallas_call(
        functools.partial(mlp_back_kernel, chunks),
        out_shape=(
            sd((tokens, width), F32), sd((images, 8, width), F32), sd((images, 2, hidden), F32),
            sd((images, tokens, width), BF), sd((images, tokens, hidden), BF), sd((images, tokens, hidden), BF)),
        in_specs=[pl.BlockSpec(memory_space=pltpu.SMEM), VM] + [ANY] * (10 + len(kept)) + [HBM] * len(deps),
        out_specs=[ANY] * 6,
        scratch_shapes=scratch,
        input_output_aliases=aliases,
        compiler_params=pltpu.CompilerParams(vmem_limit_bytes=LIMIT),
        cost_estimate=SMALL,
        name="mlp_back",
    )(index, mods, grad, xs, aos, mos, preo, pret, *weights, *kept, *deps)


def attn_back_kernel(index_ref, mod_ref, mg_in, xs, aos, qkvo, qkvt, *rest):
    wqs, (woo, wot) = rest[:2], rest[2:4]
    rest = rest[len(rest) - 22:]
    (rg_out, rgs, sums, bqvs, ois, qgo, qgt, wq, wo, mg, rg, x, ao, qkv, oi, qg, da, acc, ng, total, bqv, sems) = rest

    @pl.when(index_ref[1] == 1)
    def _():
        copies = Copies(sems)
        img = index_ref[0]
        stream = Stream(copies, DEPTH, [
            (mg_in, mg), (woo, wo.at[0]), (wot, wo.at[1]), (qkvo.at[img], qkv.at[0]), (qkvt.at[img], qkv.at[1]),
            *three_kinds(wqs, wq), (aos.at[img], ao), (xs.at[img], x)])
        half = wo.shape[1]
        size = 2 * half // HEADS
        scale = size ** (-0.5)
        mods = mod_ref[img]
        stream.take()
        oi[...] = (mg[...] * mods[2:3]).astype(BF)
        pending = [copies.start(oi, ois.at[img])]
        for side in range(2):
            stream.take()
            da[side] = nt(oi[...], wo[side]).astype(BF)
        stream.take(2)

        def attend(side, carry):
            for kind in range(3):
                acc[kind] = jnp.zeros_like(acc[kind])
            for span in windows(half, size):
                part = slice(span[2], span[3])
                mask = head_mask(span)
                zero = jnp.zeros((), BF)
                queries = jnp.where(mask, qkv[side, 0, :, part], zero)
                keys = jnp.where(mask, qkv[side, 1, :, part], zero)
                outer = jnp.where(mask, da[side, :, part], zero)
                probs = soft(nt(queries, keys), scale)
                grads = nt(outer, qkv[side, 2, :, part])
                inner = jnp.sum(grads * probs, axis=-1, keepdims=True)
                spread = (probs * (grads - inner)).astype(BF)
                acc[2, :, part] += tn(probs.astype(BF), outer)
                acc[0, :, part] += nn(spread, keys)
                acc[1, :, part] += tn(spread, queries)
            for kind in range(3):
                factor = 1.0 if kind == 2 else scale
                qg[side, kind] = (acc[kind] * factor).astype(BF)
            return carry

        lax.fori_loop(0, 2, attend, 0)
        for side, target in enumerate((qgo, qgt)):
            pending += [copies.start(qg.at[side, kind], target.at[kind, img]) for kind in range(3)]
        for part in range(6):
            side, kind = part // 3, part % 3
            stream.take()
            term = nn(qg[side, kind], wq[side, kind])
            ng[...] = term if part == 0 else ng[...] + term
            bqv[part : part + 1] = jnp.sum(qg[side, kind].astype(F32), axis=0, keepdims=True)
        pending.append(copies.start(bqv, bqvs.at[img]))
        stream.take()
        total[2:3] = jnp.sum(mg[...] * ao[...].astype(F32), axis=0, keepdims=True)
        total[3:4] = jnp.sum(oi[...].astype(F32), axis=0, keepdims=True)
        stream.take()
        normed, inverse = norm_parts(x[...].astype(F32))
        total[0:1] = jnp.sum(ng[...], axis=0, keepdims=True)
        total[1:2] = jnp.sum(ng[...] * normed, axis=0, keepdims=True)
        pending.append(copies.start(total, sums.at[img]))
        dn = ng[...] * (1.0 + mods[1:2])
        rg[...] = (mg[...] + inverse * (
            dn - jnp.mean(dn, axis=-1, keepdims=True) - normed * jnp.mean(dn * normed, axis=-1, keepdims=True))).astype(BF)
        pending += [copies.start(rg, rg_out), copies.start(rg, rgs.at[img])]
        for copy in pending:
            copy.wait()


def attn_back_call(index, grad, mods, saved, weights, kept, images, deps=()):
    xs, aos, qkvo, qkvt = saved
    tokens, width = grad.shape
    half = width // 2
    sd = jax.ShapeDtypeStruct
    kept = tuple(kept) if kept is not None else ()
    aliases = {11 + i: 1 + i for i in range(len(kept))}
    scratch = [
        pltpu.VMEM((2, 3, half, width), BF),
        pltpu.VMEM((2, half, width), BF),
        pltpu.VMEM((tokens, width), F32),
        pltpu.VMEM((tokens, width), BF),
        pltpu.VMEM((tokens, width), BF),
        pltpu.VMEM((tokens, width), BF),
        pltpu.VMEM((2, 3, tokens, half), BF),
        pltpu.VMEM((tokens, width), BF),
        pltpu.VMEM((2, 3, tokens, half), BF),
        pltpu.VMEM((2, tokens, half), BF),
        pltpu.VMEM((3, tokens, half), F32),
        pltpu.VMEM((tokens, width), F32),
        pltpu.VMEM((8, width), F32),
        pltpu.VMEM((8, half), F32),
        pltpu.SemaphoreType.DMA((32,)),
    ]
    return pl.pallas_call(
        attn_back_kernel,
        out_shape=(
            sd((tokens, width), BF), sd((images, tokens, width), BF), sd((images, 8, width), F32),
            sd((images, 8, half), F32), sd((images, tokens, width), BF),
            sd((3, images, tokens, half), BF), sd((3, images, tokens, half), BF)),
        in_specs=[pl.BlockSpec(memory_space=pltpu.SMEM), VM] + [ANY] * (9 + len(kept)) + [HBM] * len(deps),
        out_specs=[ANY] * 7,
        scratch_shapes=scratch,
        input_output_aliases=aliases,
        compiler_params=pltpu.CompilerParams(vmem_limit_bytes=LIMIT),
        cost_estimate=SMALL,
        name="attn_back",
    )(index, mods, grad, xs, aos, qkvo, qkvt, *weights, *kept, *deps)


def time_embed(timesteps, width_all):
    half_width = width_all // 2
    frequencies = jnp.exp(-math.log(10000.0) * jnp.arange(half_width, dtype=F32) / half_width)
    angles = timesteps.astype(F32)[:, None] * frequencies[None, :]
    return jnp.concatenate([jnp.cos(angles), jnp.sin(angles)], axis=1)


def swap(array):
    return lax.ppermute(array, "tensor", [(0, 1), (1, 0)])


def partners():
    peers = lax.axis_size("dp")
    place = lax.axis_index("dp")
    bit = 1
    while bit < peers:
        yield [(i, i ^ bit) for i in range(peers)], (place & bit) == 0
        bit *= 2


def gather_all(array):
    for pairs, is_low in partners():
        came = lax.ppermute(array, "dp", pairs)
        array = jnp.where(is_low, jnp.concatenate([array, came]), jnp.concatenate([came, array]))
    return array


def in_halves(values):
    high = lax.reduce_precision(values, 8, 7)
    return [high.astype(BF), (values - high).astype(BF)]


def ring_pairs(peers):
    order = list(range(0, peers, 2)) + list(range(1, peers, 2))[::-1]
    ahead = [(order[i], order[(i + 1) % peers]) for i in range(peers)]
    return ahead, [(b, a) for a, b in ahead]


def add_kernel(step, here_ref, blocks, *rest):
    came, (first, second, _, mine, theirs, sems) = rest[:2], rest[len(rest) - 6:]
    peers = blocks.shape[1]
    copies = []
    for side, sign in enumerate((1, -1)):
        spot = (here_ref[0] + (-sign * step) % peers) & (peers - 1)
        copies.append(pltpu.make_async_copy(blocks.at[side, spot], mine.at[side], sems.at[side]))
        copies.append(pltpu.make_async_copy(came[side], theirs.at[side], sems.at[2 + side]))
    for copy in copies:
        copy.start()
    for side, out in enumerate((first, second)):
        copies[2 * side].wait()
        copies[2 * side + 1].wait()
        out[...] = (theirs[side].astype(F32) + mine[side].astype(F32)).astype(BF)


def write_kernel(steps, peers, split, passes, here_ref, *rest):
    count, passed_count, whole_count = 2 * len(steps), 2 if passes else 0, 2 if split else 1
    came, (blocks, rows, sems) = rest[:count], rest[-3:]
    outs = rest[len(rest) - 4 - passed_count - whole_count : -4]
    whole, passed = outs[:whole_count], outs[whole_count:]
    quarter = peers // 2
    arrivals = [pltpu.make_async_copy(came[i], blocks.at[i], sems.at[0, i]) for i in range(count)]
    for copy in arrivals:
        copy.start()

    def targets(number):
        step, side = steps[number // 2], number % 2
        spot = (here_ref[0] + (-(1 - 2 * side) * step) % peers) & (peers - 1)
        if not split:
            return [(None, whole[0].at[side * peers + spot])]
        if side == 0:
            return [(None, whole[0].at[spot])]
        return [
            (spot < quarter, whole[0].at[peers + jnp.minimum(spot, quarter - 1)]),
            (spot >= quarter, whole[1].at[jnp.maximum(spot - quarter, 0)]),
        ]

    def each(number, act):
        for test, target in targets(number):
            copy = pltpu.make_async_copy(rows.at[number], target, sems.at[1, number])
            if test is None:
                act(copy)
            else:
                pl.when(test)(functools.partial(act, copy))

    for number in range(count):
        arrivals[number].wait()
        rows[number] = blocks[number].astype(F32)
        each(number, lambda copy: copy.start())
        if passes and number >= count - 2:
            passed[number - count][...] = blocks[number]
    for number in range(count):
        each(number, lambda copy: copy.wait())


class Ring:
    def __init__(self, terms, here, split):
        self.peers, self.here, self.split, self.step = lax.axis_size("dp"), here, split, 0
        self.count, self.width = terms.shape
        self.part = self.count // (2 * self.peers)
        self.blocks = terms.reshape(2, self.peers, self.part, self.width)
        self.pairs = ring_pairs(self.peers)
        self.moving = [self.block(side) for side in range(2)]
        self.totals, self.kept, self.token = (), [], terms

    def block(self, side):
        none = jnp.uint32(0)
        start = (jnp.uint32(side), self.here[0].astype(jnp.uint32), none, none)
        return lax.dynamic_slice(self.blocks, start, (1, 1, self.part, self.width))[0, 0]

    def advance(self, deps=()):
        self.step += 1
        deps = list(deps)
        self.moving = [lax.ppermute(array, "dp", pairs) for array, pairs in zip(self.moving, self.pairs)]
        if self.step < self.peers:
            *self.moving, self.token = self.add(deps)
        if self.step >= self.peers - 1:
            self.kept.append((self.step, self.moving))
            last = self.step == 2 * self.peers - 2
            if last or len(self.kept) == max(5, self.peers // 4):
                self.write(deps if self.step >= self.peers else [], not last)

    def add(self, deps):
        part = jax.ShapeDtypeStruct((self.part, self.width), BF)
        scratch = pltpu.VMEM((2, self.part, self.width), BF)
        return pl.pallas_call(
            functools.partial(add_kernel, self.step),
            out_shape=(part, part, TOKEN),
            in_specs=[pl.BlockSpec(memory_space=pltpu.SMEM)] + [HBM] * (3 + len(deps)),
            out_specs=(VM, VM, HBM),
            scratch_shapes=[scratch, scratch, pltpu.SemaphoreType.DMA((4,))],
            cost_estimate=SMALL,
            name="ring_add",
        )(self.here, self.blocks, *self.moving, *deps)

    def write(self, deps, passes):
        steps = tuple(step for step, _ in self.kept)
        came = [array for _, moving in self.kept for array in moving]
        blocks = (3 * self.peers // 2, self.peers // 2) if self.split else (2 * self.peers,)
        outs = tuple(jax.ShapeDtypeStruct((count, self.part, self.width), F32) for count in blocks)
        part = jax.ShapeDtypeStruct((self.part, self.width), BF)
        scratch = (len(came), self.part, self.width)
        answer = pl.pallas_call(
            functools.partial(write_kernel, steps, self.peers, self.split, passes),
            out_shape=(*outs, *((part, part) if passes else ()), TOKEN),
            in_specs=[pl.BlockSpec(memory_space=pltpu.SMEM)] + [HBM] * (len(came) + len(self.totals) + len(deps)),
            out_specs=(HBM,) * len(outs) + ((VM, VM) if passes else ()) + (HBM,),
            scratch_shapes=[
                pltpu.VMEM(scratch, BF), pltpu.VMEM(scratch, F32), pltpu.SemaphoreType.DMA((2, len(came)))],
            input_output_aliases={1 + len(came) + i: i for i in range(len(self.totals))},
            compiler_params=pltpu.CompilerParams(vmem_limit_bytes=LIMIT // 2),
            cost_estimate=SMALL,
            name="ring_write",
        )(self.here, *came, *self.totals, *deps)
        self.totals, self.kept, self.token = answer[: len(outs)], [], answer[-1]
        if passes:
            self.moving = list(answer[len(outs) : -1])


def flat(block):
    return block.reshape(-1, block.shape[-1])


def product_kernel(has_came, left_ref, right_ref, *rest):
    total = tn(flat(left_ref[...]), flat(right_ref[...]))
    if has_came:
        total = total + rest[0][...].astype(F32)
    rest[-1][...] = total.astype(BF)


def product(left, right, came=(), deps=()):
    images, tokens, rows = left.shape
    width = right.shape[2]
    block = 384 if rows % 384 == 0 else rows
    out = pl.BlockSpec((block, width), lambda i: (i, 0))
    return pl.pallas_call(
        functools.partial(product_kernel, bool(came)),
        out_shape=jax.ShapeDtypeStruct((rows, width), BF),
        grid=(rows // block,),
        in_specs=[
            pl.BlockSpec((images, tokens, block), lambda i: (0, 0, i)),
            pl.BlockSpec((images, tokens, width), lambda i: (0, 0, 0)),
        ] + [out] * len(came) + [HBM] * len(deps),
        out_specs=out,
        compiler_params=pltpu.CompilerParams(vmem_limit_bytes=LIMIT),
        cost_estimate=SMALL,
        name="product",
    )(left, right, *came, *deps)


def attn_product_kernel(has_came, qg_ref, h_ref, att_ref, oi_ref, *rest):
    def finish(total):
        if has_came:
            total = total + rest[0][...].astype(F32)
        rest[-1][...] = total.astype(BF)

    step = pl.program_id(0)

    @pl.when(step < 3)
    def _():
        finish(tn(flat(qg_ref[...]), flat(h_ref[...])))

    @pl.when(step == 3)
    def _():
        finish(tn(flat(att_ref[...]), flat(oi_ref[...])))


def attn_product(side, qkv_grads, h1s, atts, out_ins, came=(), deps=()):
    _, images, tokens, half = qkv_grads.shape
    width = h1s.shape[2]
    out = pl.BlockSpec((half, width), lambda i: (i, 0))
    whole = pl.BlockSpec((images, tokens, width), lambda i: (0, 0, 0))
    return pl.pallas_call(
        functools.partial(attn_product_kernel, bool(came)),
        out_shape=jax.ShapeDtypeStruct((4 * half, width), BF),
        grid=(4,),
        in_specs=[
            pl.BlockSpec((1, images, tokens, half), lambda i: (jnp.minimum(i, 2), 0, 0, 0)),
            whole,
            pl.BlockSpec((images, 1, tokens, half), lambda i: (0, side, 0, 0)),
            whole,
        ] + [out] * len(came) + [HBM] * len(deps),
        out_specs=out,
        compiler_params=pltpu.CompilerParams(vmem_limit_bytes=LIMIT),
        cost_estimate=SMALL,
        name="attn_product",
    )(qkv_grads, h1s, atts, out_ins, *came, *deps)


def shards(images_in, timesteps, labels, counts, label_table, ada_weight, ada_bias, qkv_weight,
           qkv_bias, out_weight, out_bias, up_weight, up_bias, down_weight, down_bias, out_cotangent):
    is_first = lax.axis_index("section") == 0
    core = lax.axis_index("tensor")
    slots = images_in.shape[1]
    images = slots // 2
    width = images_in.shape[2]
    hidden = up_weight.shape[2]
    half = out_weight.shape[1]

    def by_section(first_val, later_val):
        return jnp.where(is_first, first_val, later_val)

    def by_core(first_val, later_val):
        return jnp.where(core == 0, first_val, later_val)

    def in_order(own, came, axis):
        return by_core(jnp.concatenate([own, came], axis), jnp.concatenate([came, own], axis))

    def whole_images(rows):
        flat = rows.reshape(rows.shape[0], slots * width)
        early, later = flat[:, : images * width], flat[:, images * width :]
        own, came = by_core(early, later), swap(by_core(later, early))
        spans = [slice(i * width, (i + 1) * width) for i in range(images)]
        return [jnp.concatenate([own[:, span], came[:, span]], axis=0) for span in spans]

    qkv_own = jnp.transpose(qkv_weight[0], (1, 2, 0))
    w_qkv = (qkv_own, swap(qkv_own))
    w_out = (out_weight[0], swap(out_weight[0]))
    w_up = (up_weight[0], swap(up_weight[0]))
    w_down = (down_weight[0], swap(down_weight[0]))
    weights = (*w_qkv, *w_out, *w_up, *w_down)

    condition = jnp.take(label_table, labels, axis=0).astype(F32) + time_embed(timesteps, width)
    silu_cond, silu_back = jax.vjp(jax.nn.silu, condition)
    silu_b = silu_cond.astype(BF)
    mod_local = (
        jnp.dot(silu_b, ada_weight[0], preferred_element_type=F32) + ada_bias[0].astype(F32)[None]
    )
    early, later = mod_local[:images], mod_local[images:]
    modulation = in_order(by_core(early, later), swap(by_core(later, early)), 1).reshape(images, 6, width)
    slot_no = core * images + jnp.arange(images, dtype=jnp.int32)
    valid = (slot_no < counts[0]).astype(F32)
    mods = jnp.concatenate(
        [modulation, jnp.broadcast_to(valid[:, None, None], (images, 2, width))], axis=1
    )
    pair_bias = jnp.concatenate([qkv_bias[0, 0], qkv_bias[0, 1], up_bias[0]])[None]
    pair_bias = jnp.concatenate([pair_bias, swap(pair_bias)], axis=0).astype(F32)
    zero_row = jnp.zeros((half,), F32)
    bqv = jnp.stack([
        pair_bias[0, :half], zero_row, pair_bias[0, half : 2 * half],
        pair_bias[1, :half], zero_row, pair_bias[1, half : 2 * half], zero_row, zero_row])
    bup = pair_bias[:, 2 * half :]
    bod = jnp.concatenate([out_bias, down_bias], axis=0).astype(F32)

    def turn_index(number, is_active):
        return jnp.stack([jnp.int32(number), is_active.astype(jnp.int32)])

    inputs, cotangent, saved = whole_images(images_in), whole_images(out_cotangent), None
    for turn in range(2 * images):
        number, is_early = turn % images, turn < images
        answer = layer_call(
            turn_index(number, is_first == is_early), inputs[turn], mods, bqv, bup, bod, weights, saved, images
        )
        saved = answer[1:]
        if is_early:
            inputs.append(lax.ppermute(answer[0], "section", [(0, 1)]))
    def split_images(rows):
        own, other = jnp.split(rows, 2, axis=1)
        return jnp.moveaxis(in_order(own, swap(other), 0), 0, 1)[None]

    ys, xs, h1s, qkvo, qkvt, atts, aos, h2s, preo, pret, acto, actt, mos = saved
    layer_out = split_images(ys)

    inputs, mlp_kept, attn_kept = cotangent, None, None
    peers, device = lax.axis_size("dp"), lax.axis_index("dp")
    here = jnp.where((device & 1) == 0, device >> 1, peers - 1 - (device >> 1)).astype(jnp.int32).reshape(1)
    deps = []
    for turn in range(2 * images):
        number, is_early = turn % images, turn < images
        index = turn_index(number, is_first != is_early)
        deps = deps + [layer_out] if turn == images else deps
        answer = mlp_back_call(
            index, inputs[turn], mods, (xs, aos, mos, preo, pret), (*w_up, *w_down), mlp_kept, images, deps
        )
        middle_grad, mlp_kept, deps = answer[0], answer[1:], []
        if turn == 2 * images - 1:
            mlp_sums, up_sums, down_ins, pre_grads_o, pre_grads_t = mlp_kept
            down_t = product(actt, down_ins)
            up_t = product(h2s, pre_grads_t, deps=[down_t])
            down_w = product(acto, down_ins, [swap(down_t)], [up_t])
            rings = [Ring(down_w, here, False)]
            up_w = product(h2s, pre_grads_o, [swap(up_t)], [rings[0].token])
            rings.append(Ring(up_w, here, False))
            rings[0].advance([up_w])
            deps = [rings[0].token, rings[1].token]
        answer = attn_back_call(
            index, middle_grad, mods, (xs, aos, qkvo, qkvt), (*w_qkv, *w_out), attn_kept, images, deps
        )
        attn_kept = list(answer[1:])
        deps = [attn_kept[1]]
        if is_early:
            inputs.append(lax.ppermute(answer[0], "section", [(1, 0)]))
    row_grads, attn_sums, qkv_sums, out_ins, qkv_grads_o, qkv_grads_t = attn_kept

    for ring in rings:
        ring.advance([attn_sums])
    deps = [rings[0].token, rings[1].token]
    attn_t = attn_product(1, qkv_grads_t, h1s, atts, out_ins, deps=deps)
    for ring in rings:
        ring.advance([attn_t])
    deps = [rings[0].token, rings[1].token]
    attn_w = attn_product(0, qkv_grads_o, h1s, atts, out_ins, [swap(attn_t)], deps)
    rings.append(Ring(attn_w, here, True))
    for ring in rings[:2]:
        ring.advance([attn_w])
    attn_sums, mlp_sums, qkv_sums, up_sums, row_grads, _ = lax.optimization_barrier(
        (attn_sums, mlp_sums, qkv_sums, up_sums, row_grads, rings[1].moving))
    mod_grad = jnp.concatenate([attn_sums[:, :3], mlp_sums[:, :3]], axis=1).astype(BF)
    columns = mod_grad.reshape(images, 2 * 3 * width)
    early, later = columns[:, : 3 * width], columns[:, 3 * width :]
    mod_cols = in_order(by_core(early, later), swap(by_core(later, early)), 0)
    qkv_total, up_total = jnp.sum(qkv_sums, axis=0), jnp.sum(up_sums, axis=0)
    own_bias = jnp.concatenate([qkv_total[0], qkv_total[2], up_total[0]])
    other_bias = jnp.concatenate([qkv_total[3], qkv_total[5], up_total[1]])
    both_bias = jnp.concatenate([jnp.sum(attn_sums[:, 3], axis=0), jnp.sum(mlp_sums[:, 3], axis=0)])
    bias = jnp.concatenate([own_bias, both_bias]) + swap(jnp.concatenate([other_bias, both_bias]))
    silu_grad = jnp.einsum("sk,dk->sd", mod_cols, ada_weight[0], preferred_element_type=F32)
    silu_grad = silu_grad + swap(silu_grad)
    silu_grad = silu_grad + lax.ppermute(silu_grad, "section", [(0, 1), (1, 0)])
    cond_grad = silu_back(silu_grad)[0]
    packed = jnp.concatenate(
        [silu_b.reshape(-1), mod_cols.reshape(-1), *in_halves(cond_grad.reshape(-1)), *in_halves(bias),
         *in_halves(labels.astype(F32))])
    packed = gather_all(packed[None])
    sizes = [slots * width, slots * 3 * width] + [slots * width] * 2 + [bias.shape[0]] * 2 + [slots] * 2
    ends = [sum(sizes[: i + 1]) for i in range(len(sizes))]
    parts = [packed[:, end - size : end] for size, end in zip(sizes, ends)]
    silu_all, mod_all = parts[0].reshape(-1, width), parts[1].reshape(-1, 3 * width)
    cond_all = (parts[2].astype(F32) + parts[3].astype(F32)).reshape(-1, width)
    biases = jnp.sum(parts[4].astype(F32) + parts[5].astype(F32), axis=0)
    labels_all = (parts[6].astype(F32) + parts[7].astype(F32)).reshape(-1)
    ada_w_sum = jnp.einsum("sd,sk->dk", silu_all, mod_all, preferred_element_type=F32)
    ada_b_sum = jnp.sum(mod_all, axis=0, dtype=F32)
    classes = jnp.arange(label_table.shape[0], dtype=F32)
    onehot = (labels_all[None] == classes[:, None]).astype(F32)
    table_grad = jnp.dot(onehot, cond_all, precision=lax.Precision.HIGHEST, preferred_element_type=F32)

    in_grad = split_images(row_grads)
    total_steps = 2 * peers - 2
    earlier, leading = [], []
    while rings[2].step < total_steps:
        before, earlier = earlier, [rings[2].token]
        ahead = [ring.token for ring in rings[:2]]
        rings[2].advance(leading)
        leading = ahead
        for ring in rings[:2]:
            if ring.step < total_steps:
                ring.advance(before)
    down_w_sum, up_w_sum = (ring.totals[0].reshape(ring.count, ring.width) for ring in rings[:2])
    qkv_w_sum = rings[2].totals[0].reshape(3, half, width)
    out_w_sum = rings[2].totals[1].reshape(half, width)
    qkv_w_sum = jnp.transpose(qkv_w_sum, (2, 0, 1))
    qkv_b_sum = biases[: 2 * half].reshape(2, half)
    up_b_sum = biases[2 * half : 2 * half + hidden]
    out_b_sum = biases[2 * half + hidden : 2 * half + hidden + width]
    down_b_sum = biases[2 * half + hidden + width :]
    return (
        layer_out,
        in_grad,
        cond_grad,
        table_grad,
        ada_w_sum[None],
        ada_b_sum[None],
        qkv_w_sum[None],
        qkv_b_sum[None],
        out_w_sum[None],
        out_b_sum[None],
        up_w_sum[None],
        up_b_sum[None],
        down_w_sum[None],
        down_b_sum[None],
    )


def solution(mesh):
    placed = (
        P("tensor", "dp", None),
        P("dp"),
        P("dp"),
        P("dp"),
        P(),
        P("section", None, "tensor"),
        P("section", "tensor"),
        P("section", None, None, "tensor"),
        P("section", None, "tensor"),
        P("section", "tensor", None),
        P("section", None),
        P("section", None, "tensor"),
        P("section", "tensor"),
        P("section", "tensor", None),
        P("section", None),
        P("tensor", "dp", None),
    )
    return jax.shard_map(
        shards,
        mesh=mesh,
        in_specs=placed,
        out_specs=(
            P("section", "tensor", "dp", None),
            P("section", "tensor", "dp", None),
            P("dp", None),
            P(),
            P("section", None, "tensor"),
            P("section", "tensor"),
            P("section", None, None, "tensor"),
            P("section", None, "tensor"),
            P("section", "tensor", None),
            P("section", None),
            P("section", None, "tensor"),
            P("section", "tensor"),
            P("section", "tensor", None),
            P("section", None),
        ),
        check_vma=False,
    )
```
